256 devices in a mesh: gx: 64 (over z, y_lo, x), gy: 4 (over y_hi, core).
Axes of the slice: x: 4, y: 4 (y_hi: 2, y_lo: 2; y = y_hi * 2 + y_lo), z: 8, core: 2. Of those that a mesh axis runs over, the one named last changes fastest.
Arguments:
- misfit: float32 [3, 512, 128, 128], P(None, 'gx', 'gy'), may hold values from -13 to 13
- damage: float32 [512, 128, 128], P('gx', 'gy'), may hold values from 0 to 0.9
- displacement: float32 [3, 512, 128, 128], P(None, 'gx', 'gy'), may hold values from -3 to 3
Outputs:
- adjoint: float32 [3, 512, 128, 128], P(None, 'gx', 'gy')
- sensitivity: float32 [512, 128, 128], P('gx', 'gy')
The draws below stay inside these ranges and needn't reach their ends.
All inputs are finite; a program needn't handle non-finite values.
Results may differ from the reference program's by a relative error of at most 0.00012.
Values sent between devices are 32-bit elements; how exact they have to be, the bound alone decides.
No kernel may reach another device: no remote copies, remote signals or barrier semaphores. Data moves between devices by JAX's collectives and lax.ppermute only.
A program may use at most 64 MiB of HBM per device.

```python
import math
import jax
import jax.numpy as jnp
import numpy as np
from jax import lax

CX = 8
ITERS = 3
NX = 512
NY = 128
NZ = 128


def draw_misfit(key, part):
    position = jnp.arange(NX, dtype=jnp.float32) / (NX - 1)
    along = (0.5 + position).reshape(1, NX, 1, 1)
    values = jnp.clip(jax.random.normal(key, (3, NX, NY, NZ), jnp.float32), -6.0, 6.0)
    result = values * along
    return result.astype(jnp.float32)


def shard_levels(rng, dims, cuts, smallest, high):
    factor_of = 1.0
    for axis_at, blocks in cuts:
        heights = jax.random.uniform(jax.random.fold_in(jax.random.fold_in(rng, 6), axis_at), (blocks,), jnp.float32, smallest / len(cuts), high / len(cuts))
        factor_of = factor_of * jnp.repeat(jnp.exp(heights), dims[axis_at] // blocks).reshape((-1,) + (1,) * (len(dims) - 1 - axis_at))
    return factor_of


def scatter_about(own_key, shape, spread, bound, cuts=(), held_as=jnp.bfloat16):
    entries = jax.random.normal(own_key, shape, jnp.float32) * spread
    if len(cuts) > 0:
        entries = shard_levels(own_key, shape, cuts, -0.22, 0.18) * entries
    return jnp.clip(entries, min=-bound, max=bound).astype(held_as)


def setup_inputs(seed: int = 0) -> dict:
    keys = jax.random.split(jax.random.key(seed), 4)
    misfit = draw_misfit(jax.random.fold_in(keys[3], 71), 0)
    damage = jnp.clip(0.9 * jax.random.uniform(keys[1], (NX, NY, NZ), jnp.float32) ** shard_levels(keys[1], (NX, NY, NZ), ((0, 64), (1, 4)), -0.2, 0.2), 0.0, 0.9)
    displacement = scatter_about(keys[2], (3, NX, NY, NZ), 0.5, 3.0, ((1, 64), (2, 4)), jnp.float32)
    return {"misfit": misfit, "damage": damage, "displacement": displacement}


def kronecker(first, second):
    return 1.0 if first == second else 0.0

def element_matrix():
    modulus = 3.0
    poisson_ratio = 0.3
    lame_first = modulus * poisson_ratio / ((1.0 + poisson_ratio) * (1.0 - 2.0 * poisson_ratio))
    shear_modulus = modulus / (2.0 * (1.0 + poisson_ratio))
    signs = [[2.0 * (corner_index >> 2 & 1) - 1.0, 2.0 * (corner_index >> 1 & 1) - 1.0, 2.0 * (corner_index & 1) - 1.0] for corner_index in range(8)]
    elastic = [[[[lame_first * kronecker(i, j) * kronecker(k, l) + shear_modulus * (kronecker(i, k) * kronecker(j, l) + kronecker(i, l) * kronecker(j, k)) for l in range(3)] for k in range(3)] for j in range(3)] for i in range(3)]
    stiffness = np.zeros((8, 3, 8, 3))
    root_three = math.sqrt(3.0)
    for gauss_index in range(8):
        gauss_point = [signs[gauss_index][dimension] / root_three for dimension in range(3)]
        gradients = [[0.0, 0.0, 0.0] for corner_index in range(8)]
        for corner_index in range(8):
            for dimension in range(3):
                factor = 0.25 * signs[corner_index][dimension]
                for others in range(3):
                    if others != dimension:
                        factor = factor * (1.0 + signs[corner_index][others] * gauss_point[others])
                gradients[corner_index][dimension] = factor
        for first_corner in range(8):
            for i in range(3):
                for second_corner in range(8):
                    for j in range(3):
                        accumulated = 0.0
                        for k in range(3):
                            for l in range(3):
                                accumulated = accumulated + gradients[first_corner][k] * elastic[i][k][j][l] * gradients[second_corner][l]
                        stiffness[first_corner, i, second_corner, j] = stiffness[first_corner, i, second_corner, j] + 0.125 * accumulated
    return stiffness.reshape(24, 24)

def corner_offsets():
    return [(corner_index >> 2 & 1, corner_index >> 1 & 1, corner_index & 1) for corner_index in range(8)]

def corner_stack(padded, count_x, count_y, count_z):
    return jnp.stack([padded[:, shift_x:shift_x + count_x, shift_y:shift_y + count_y, shift_z:shift_z + count_z] for shift_x, shift_y, shift_z in corner_offsets()], 0)

def element_forces(padded, degradation):
    count_x, count_y, count_z = degradation.shape
    stacked = corner_stack(padded, count_x, count_y, count_z).reshape(24, -1)
    table = jnp.asarray(element_matrix(), jnp.float32)
    forces = jnp.dot(table, stacked, precision=lax.Precision.HIGHEST, preferred_element_type=jnp.float32)
    return forces.reshape(8, 3, count_x, count_y, count_z) * degradation

def assemble(forces):
    total = None
    for corner_index, (shift_x, shift_y, shift_z) in enumerate(corner_offsets()):
        placed = jnp.pad(forces[corner_index], ((0, 0), (shift_x, 1 - shift_x), (shift_y, 1 - shift_y), (shift_z, 1 - shift_z)))
        total = placed if total is None else total + placed
    return total

def operate(field, degradation):
    blocks = NX // CX
    padded = jnp.pad(field, ((0, 0), (0, 1), (0, 1), (0, 1)))

    def one_block(index):
        start = index * CX
        zero = index * 0
        piece = lax.dynamic_slice(padded, (zero, start, zero, zero), (3, CX + 1, NY + 1, NZ + 1))
        local = lax.dynamic_slice(degradation, (start, zero, zero), (CX, NY, NZ))
        return assemble(element_forces(piece, local))[:, :, :NY, :NZ]
    pieces = lax.map(one_block, jnp.arange(blocks, dtype=jnp.int32))
    spill = jnp.concatenate([jnp.zeros_like(pieces[:1, :, -1:]), pieces[:-1, :, -1:]], 0)
    joined = jnp.concatenate([pieces[:, :, :1] + spill, pieces[:, :, 1:-1]], 2)
    return jnp.moveaxis(joined, 0, 1).reshape(3, NX, NY, NZ)

def sensitivity_of(adjoint, displacement, damage):
    blocks = NX // CX
    pair = jnp.pad(jnp.concatenate([adjoint, displacement], 0), ((0, 0), (0, 1), (0, 1), (0, 1)))
    table = jnp.asarray(element_matrix(), jnp.float32)

    def one_block(index):
        start = index * CX
        zero = index * 0
        piece = lax.dynamic_slice(pair, (zero, start, zero, zero), (6, CX + 1, NY + 1, NZ + 1))
        adjoint_corners = corner_stack(piece[:3], CX, NY, NZ).reshape(24, -1)
        moved_corners = corner_stack(piece[3:], CX, NY, NZ).reshape(24, -1)
        product = jnp.dot(table, moved_corners, precision=lax.Precision.HIGHEST, preferred_element_type=jnp.float32)
        return lax.optimization_barrier(jnp.sum(adjoint_corners * product, 0)).reshape(CX, NY, NZ)
    pieces = lax.map(one_block, jnp.arange(blocks, dtype=jnp.int32))
    return 2.0 * (1.0 - damage) * pieces.reshape(NX, NY, NZ)

def reference(misfit, damage, displacement):
    degradation = (1.0 - damage) * (1.0 - damage) + 0.001
    adjoint = jnp.zeros_like(misfit)
    residual = misfit
    direction = misfit
    norm_now = jnp.sum(residual * residual)
    for step in range(ITERS):
        image = operate(direction, degradation)
        alpha = norm_now / jnp.sum(direction * image)
        adjoint = adjoint + alpha * direction
        residual = residual - alpha * image
        if step + 1 < ITERS:
            norm_next = jnp.sum(residual * residual)
            direction = residual + norm_next / norm_now * direction
            norm_now = norm_next
    return (adjoint, sensitivity_of(adjoint, displacement, damage))
```

```python
import jax
import jax.numpy as jnp
from jax import lax
from jax.experimental import pallas as pl
from jax.experimental.pallas import tpu as pltpu
from jax.sharding import PartitionSpec as P

CX, CY, CZ = 8, 32, 128
ROWS = 40
AXES = ("gx", "gy")
LAM = 3.0 * 0.3 / (1.3 * 0.4)
MU = 3.0 / 2.6
F32 = jnp.float32


def exchange(x, axis, first):
    n = lax.axis_size(axis)
    pairs = []
    for i in range(first, n - 1, 2):
        pairs += [(i, i + 1), (i + 1, i)]
    return lax.ppermute(x, axis, pairs)


def iota(shape, dim):
    return lax.broadcasted_iota(jnp.int32, shape, dim)


def degradation_of(damage):
    return (1.0 - damage) * (1.0 - damage) + 0.001


def pack_y(b_lo, b_hi, h_lo, h_hi, u_lo, out_a, out_b):
    row = iota((CX, 8, CZ), 1)
    g_lo, g_hi = degradation_of(h_lo[...]), degradation_of(h_hi[...])
    up = lambda x, k: pltpu.roll(x, k % 8, 1)
    low_1 = jnp.where(row < 3, b_lo[0], jnp.where(row < 6, up(b_lo[1], 3), up(g_lo, 6)))
    low_2 = jnp.where(
        row < 3,
        b_lo[2],
        jnp.where(
            row == 3, up(u_lo[0], 3), jnp.where(row == 4, up(u_lo[1], 4), up(u_lo[2], 5))
        ),
    )
    high = jnp.where(
        row < 2,
        up(b_hi[0], 2),
        jnp.where(row < 4, up(b_hi[1], 4), jnp.where(row < 6, up(b_hi[2], 6), g_hi)),
    )
    odd = lax.rem(lax.axis_index("gy"), 2) == 1

    @pl.when(odd)
    def _():
        out_a[0], out_a[1] = low_1, low_2
        out_b[0], out_b[1] = high, high

    @pl.when(jnp.logical_not(odd))
    def _():
        out_a[0], out_a[1] = high, high
        out_b[0], out_b[1] = low_1, low_2


def pack_x(y_a, y_b, b_ref, h_ref, u_ref, out_a, out_b, halo):
    odd_y = lax.rem(lax.axis_index("gy"), 2) == 1
    row = iota((CX, 8, CZ), 1)
    up = lambda x, k: pltpu.roll(x, k % 8, 1)
    above_1 = jnp.where(odd_y, y_b[0], y_a[0])
    above_2 = jnp.where(odd_y, y_b[1], y_a[1])
    below = jnp.where(odd_y, y_a[0], y_b[0])

    def tile(head, count, tail):
        return jnp.where(row < count, head, jnp.where(row >= 6, tail, 0.0))

    halo[0] = tile(above_1, 3, up(below, 6))
    halo[1] = tile(up(above_1, -3), 3, up(below, 4))
    halo[2] = tile(above_2, 3, up(below, 2))
    halo[3] = tile(up(above_1, -6), 2, below)
    for c in range(3):
        halo[4 + c] = jnp.where(row < 1, up(above_2, -3 - c), 0.0)
    odd_x = lax.rem(lax.axis_index("gx"), 2) == 1

    def low(out):
        for c in range(3):
            for x in range(3):
                out[3 * c + x, :CY], out[3 * c + x, CY:] = b_ref[c, x], halo[c, x]
            out[11 + c, :CY], out[11 + c, CY:] = u_ref[c, 0], halo[4 + c, 0]
        for x in range(2):
            out[9 + x, :CY], out[9 + x, CY:] = degradation_of(h_ref[x]), halo[3, x]

    def high(out):
        for c in range(3):
            for x in range(2):
                out[3 * c + x, :CY], out[3 * c + x, CY:] = b_ref[c, 6 + x], halo[c, 6 + x]
            out[3 * c + 2] = jnp.zeros((ROWS, CZ), F32)
            out[11 + c] = jnp.zeros((ROWS, CZ), F32)
        for x in range(2):
            out[9 + x, :CY], out[9 + x, CY:] = degradation_of(h_ref[6 + x]), halo[3, 6 + x]

    @pl.when(odd_x)
    def _():
        low(out_a)
        high(out_b)

    @pl.when(jnp.logical_not(odd_x))
    def _():
        high(out_a)
        low(out_b)


def yz_modes(u):
    lane = iota((ROWS, CZ), 1)
    u_next = jnp.where(lane == CZ - 1, 0.0, pltpu.roll(u, CZ - 1, 1))
    out = [None] * 4
    for z, a in enumerate((u + u_next, u_next - u)):
        a_next = pltpu.roll(a, ROWS - 1, 0)
        out[z], out[2 + z] = a + a_next, a_next - a
    return out


def yz_gather(r):
    lane = iota((ROWS, CZ), 1)
    rows = []
    for z in range(2):
        s, d = r[z], r[2 + z]
        rows.append((s - d) + pltpu.roll(s + d, 1, 0))
    s, d = rows
    return (s - d) + jnp.where(lane == 0, 0.0, pltpu.roll(s + d, 1, 1))


SS, SD, DS, DD = 0, 1, 2, 3


def strains(here, there):
    s = [[here[4 * c + k] + there[4 * c + k] if k else None for k in range(4)] for c in range(3)]
    d = [[there[4 * c + k] - here[4 * c + k] for k in range(4)] for c in range(3)]
    u, v, w = range(3)
    return [
        d[u][SS], s[v][DS], s[w][SD],
        s[u][DS] + d[v][SS], s[u][SD] + d[w][SS], s[v][SD] + s[w][DS],
        s[u][DD], d[v][SD], d[w][DS],
        d[u][SD], s[v][DD], d[u][DS], s[w][DD], d[v][DS], d[w][SD],
        d[u][DD], d[v][DD], d[w][DD],
    ]


def stresses(e, g):
    scaled = (lambda k: g * k) if g is not None else (lambda k: k)
    l16, m8, m16, m48 = scaled(LAM / 16), scaled(MU / 8), scaled(MU / 16), scaled(MU / 48)
    l48, q = scaled(LAM / 48), scaled((LAM + 4 * MU) / 144)
    trace = l16 * (e[0] + e[1] + e[2])
    out = [trace + m8 * e[k] for k in range(3)]
    out += [m16 * e[k] for k in range(3, 6)]
    three = e[6] + e[7] + e[8]
    out += [m48 * (e[k] + three) for k in range(6, 9)]
    for k in (9, 11, 13):
        both = l48 * (e[k] + e[k + 1])
        out += [both + m16 * e[k], both + m16 * e[k + 1]]
    return out + [q * e[k] for k in range(15, 18)]


def x_forces(f):
    s = [[None, f[4], f[3], f[6]], [None, f[5], f[1], f[10]], [None, f[2], f[5], f[12]]]
    d = [[f[0], f[9], f[11], f[15]], [f[3], f[7], f[13], f[16]], [f[4], f[14], f[8], f[17]]]
    return [x for c in s for x in c], [x for c in d for x in c]


def inner(a, b):
    total = a[0] * b[0]
    for x, y in zip(a[1:], b[1:]):
        total = total + x * y
    return total


def main_kernel(
    b_ref, h_ref, u_ref, halo, x_a, x_b, p1_out, p2_out, t_out, row_out,
    field, g_ref, p1, p2, modes, gathered, moved, weights, sums,
):
    odd_x = lax.rem(lax.axis_index("gx"), 2) == 1
    not_last_x = jnp.where(lax.axis_index("gx") == lax.axis_size("gx") - 1, 0.0, 1.0).astype(F32)
    not_last_y = jnp.where(lax.axis_index("gy") == lax.axis_size("gy") - 1, 0.0, 1.0).astype(F32)
    row = iota((ROWS, CZ), 0)
    keep = jnp.where(jnp.logical_and(row >= CY, row < CY + 3), not_last_y, 1.0)

    def place(above, below):
        for c in range(3):
            for x in range(2):
                field[c, x] = below[3 * c + x]
            for x in range(3):
                field[c, 10 + x] = above[3 * c + x]
            moved[c, CX] = above[11 + c]
        for x in range(2):
            g_ref[x] = below[9 + x]
            g_ref[10 + x] = above[9 + x]

    @pl.when(odd_x)
    def _():
        place(x_b, x_a)

    @pl.when(jnp.logical_not(odd_x))
    def _():
        place(x_a, x_b)

    for c in range(3):
        field[c, 2:10, :CY] = b_ref[c]
        field[c, 2:10, CY:] = halo[c]
        moved[c, :CX, :CY] = u_ref[c]
        moved[c, :CX, CY:] = halo[4 + c]
    g_ref[2:10, :CY] = degradation_of(h_ref[...])
    g_ref[2:10, CY:] = halo[3]
    sums[...] = jnp.zeros_like(sums)

    def to_modes(source, layers):
        @pl.loop(0, layers)
        def _(n):
            for c in range(3):
                for k, a in enumerate(yz_modes(source[c, n])):
                    modes[4 * c + k, n] = a

    def load(n, rows):
        return [modes[k, n, rows, :] for k in range(12)]

    to_modes(moved, CX + 1)

    @pl.loop(0, CY // 8)
    def _(j):
        rows = pl.ds(pl.multiple_of(8 * j, 8), 8)
        here = load(0, rows)
        for e in range(CX):
            there = load(e + 1, rows)
            for k, f in enumerate(stresses(strains(here, there), None)):
                weights[k, e, rows, :] = f
            here = there

    def stress_gather(layers, g_first, own_first, power):
        def chunk(rows, own):
            here = load(0, rows)
            before = None
            for e in range(layers):
                there = load(e + 1, rows)
                strain = strains(here, there)
                x = e - own_first
                if own and 0 <= x < CX:
                    stiff = [weights[k, x, rows, :] for k in range(18)]
                    t_out[power, x, rows, :] = inner(strain, stiff)
                s, d = x_forces(stresses(strain, g_ref[g_first + e, rows, :]))
                if before is not None:
                    for k in range(12):
                        lower = s[k] - d[k] if s[k] is not None else -d[k]
                        gathered[k, e - 1, rows, :] = before[k] + lower
                before = [s[k] + d[k] if s[k] is not None else d[k] for k in range(12)]
                here = there

        @pl.loop(0, CY // 8)
        def _(j):
            chunk(pl.ds(pl.multiple_of(8 * j, 8), 8), True)

        chunk(pl.ds(CY, 8), False)

    def collapse(x):
        return x[0:8] + x[8:16] + x[16:24] + x[24:32]

    def nodes(layers, target, past_end):
        @pl.loop(0, layers)
        def _(n):
            factor = keep * jnp.where(n >= past_end, not_last_x, 1.0)
            for c in range(3):
                target[c, n] = factor * yz_gather([gathered[4 * c + k, n] for k in range(4)])

    to_modes(field, 13)
    stress_gather(12, 0, 2, 0)
    nodes(11, p1, 9)
    to_modes(p1, 11)
    stress_gather(10, 1, 1, 1)
    nodes(9, p2, 8)

    @pl.loop(0, CX)
    def _(x):
        for c in range(3):
            v0, v1, v2 = b_ref[c, x], p1[c, x + 1, :CY], p2[c, x, :CY]
            p1_out[c, x] = v1
            p2_out[c, x] = v2
            for k, (a, b) in enumerate(((v0, v0), (v0, v1), (v1, v1), (v1, v2), (v2, v2))):
                sums[k] += collapse(a * b)

    to_modes(p2, 9)

    @pl.loop(0, CY // 8)
    def _(j):
        rows = pl.ds(pl.multiple_of(8 * j, 8), 8)
        here = load(0, rows)
        total = jnp.zeros((8, CZ), F32)
        for e in range(CX):
            there = load(e + 1, rows)
            strain = strains(here, there)
            t_out[2, e, rows, :] = inner(strain, [weights[k, e, rows, :] for k in range(18)])
            total = total + inner(strain, stresses(strain, g_ref[2 + e, rows, :]))
            here = there
        sums[5] += total

    lane = iota((1, CZ), 1)
    line = jnp.zeros((1, CZ), F32)
    for k in range(6):
        line = jnp.where(lane == k, jnp.sum(jnp.sum(sums[k], 0, keepdims=True), 1, keepdims=True), line)
    row_out[...] = jnp.broadcast_to(line, row_out.shape)


def combine(parts, b_ref, p1, p2, t_ref, h_ref, adjoint, sensitivity):
    line = jnp.sum(parts[...], 0, keepdims=True)
    lane = iota((1, CZ), 1)
    m = [jnp.sum(jnp.where(lane == k, line, 0.0), 1, keepdims=True) for k in range(6)]
    l10, l20 = m[2] / m[1], m[3] / m[1]
    d1, h21 = m[3] - l10 * m[2], m[4] - l20 * m[2]
    l21 = h21 / d1
    d2 = m[5] - l20 * m[3] - l21 * h21
    y1 = m[1] - l10 * m[0]
    y2 = m[2] - l20 * m[0] - l21 * y1
    c2 = y2 / d2
    c1 = y1 / d1 - l21 * c2
    c0 = m[0] / m[1] - l10 * c1 - l20 * c2
    c0, c1, c2 = [jnp.broadcast_to(c, (CY, CZ)) for c in (c0, c1, c2)]
    for x in range(CX):
        for c in range(3):
            adjoint[c, x] = c0 * b_ref[c, x] + c1 * p1[c, x] + c2 * p2[c, x]
        product = c0 * t_ref[0, x] + c1 * t_ref[1, x] + c2 * t_ref[2, x]
        sensitivity[x] = 2.0 * (1.0 - h_ref[x]) * product


VMEM = pl.BlockSpec(memory_space=pltpu.VMEM)


def shape(*dims):
    return jax.ShapeDtypeStruct(dims, F32)


def body(misfit, damage, displacement):
    edge = (3, CX, 8, CZ)
    first = lambda i: (0, 0, 0, 0)
    last = lambda i: (0, 0, 3, 0)
    y_a, y_b = pl.pallas_call(
        pack_y,
        grid=(1,),
        in_specs=[
            pl.BlockSpec(edge, first),
            pl.BlockSpec(edge, last),
            pl.BlockSpec(edge[1:], lambda i: (0, 0, 0)),
            pl.BlockSpec(edge[1:], lambda i: (0, 3, 0)),
            pl.BlockSpec(edge, first),
        ],
        out_specs=[pl.BlockSpec((2, CX, 8, CZ), first)] * 2,
        out_shape=[shape(2, CX, 8, CZ)] * 2,
        name="pack_y",
    )(misfit, misfit, damage, damage, displacement)
    y_a = exchange(y_a, "gy", 0)
    y_b = exchange(y_b, "gy", 1)
    x_a, x_b, halo = pl.pallas_call(
        pack_x,
        in_specs=[VMEM] * 5,
        out_specs=[VMEM] * 3,
        out_shape=[shape(14, ROWS, CZ)] * 2 + [shape(7, CX, 8, CZ)],
        name="pack_x",
    )(y_a, y_b, misfit, damage, displacement)
    x_a = exchange(x_a, "gx", 0)
    x_b = exchange(x_b, "gx", 1)
    devices = lax.axis_size("gx") * lax.axis_size("gy")
    p1, p2, t, line = pl.pallas_call(
        main_kernel,
        in_specs=[VMEM] * 6,
        out_specs=[VMEM] * 4,
        out_shape=[shape(3, CX, CY, CZ)] * 3 + [shape(devices, CZ)],
        scratch_shapes=[
            pltpu.VMEM((3, 13, ROWS, CZ), F32),
            pltpu.VMEM((12, ROWS, CZ), F32),
            pltpu.VMEM((3, 11, ROWS, CZ), F32),
            pltpu.VMEM((3, 9, ROWS, CZ), F32),
            pltpu.VMEM((12, 13, ROWS, CZ), F32),
            pltpu.VMEM((12, 11, ROWS, CZ), F32),
            pltpu.VMEM((3, 9, ROWS, CZ), F32),
            pltpu.VMEM((18, CX, CY, CZ), F32),
            pltpu.VMEM((6, 8, CZ), F32),
        ],
        name="main",
    )(misfit, damage, displacement, halo, x_a, x_b)
    parts = lax.all_to_all(line, AXES, 0, 0, tiled=True)
    return pl.pallas_call(
        combine,
        in_specs=[VMEM] * 6,
        out_specs=[VMEM] * 2,
        out_shape=[shape(3, CX, CY, CZ), shape(CX, CY, CZ)],
        name="combine",
    )(parts, misfit, p1, p2, t, damage)


def solution(mesh):
    field, scalar = P(None, "gx", "gy", None), P("gx", "gy", None)
    return jax.shard_map(
        body, mesh=mesh, in_specs=(field, scalar, field), out_specs=(field, scalar), check_vma=False
    )
```

```python
import jax
import jax.numpy as jnp
from jax import lax
from jax.experimental import pallas as pl
from jax.experimental.pallas import tpu as pltpu
from jax.sharding import PartitionSpec as P

CX, CY, CZ = 8, 32, 128
ROWS = 40
AXES = ("gx", "gy")
LAM = 3.0 * 0.3 / (1.3 * 0.4)
MU = 3.0 / 2.6
F32 = jnp.float32


def exchange(x, axis, first):
    n = lax.axis_size(axis)
    pairs = []
    for i in range(first, n - 1, 2):
        pairs += [(i, i + 1), (i + 1, i)]
    return lax.ppermute(x, axis, pairs)


def iota(shape, dim):
    return lax.broadcasted_iota(jnp.int32, shape, dim)


def degradation_of(damage):
    return (1.0 - damage) * (1.0 - damage) + 0.001


def pack_y(b_lo, b_hi, h_lo, h_hi, u_lo, out_a, out_b):
    row = iota((CX, 8, CZ), 1)
    g_lo, g_hi = degradation_of(h_lo[...]), degradation_of(h_hi[...])
    up = lambda x, k: pltpu.roll(x, k % 8, 1)
    low_1 = jnp.where(row < 3, b_lo[0], jnp.where(row < 6, up(b_lo[1], 3), up(g_lo, 6)))
    low_2 = jnp.where(
        row < 3,
        b_lo[2],
        jnp.where(
            row == 3, up(u_lo[0], 3), jnp.where(row == 4, up(u_lo[1], 4), up(u_lo[2], 5))
        ),
    )
    high = jnp.where(
        row < 2,
        up(b_hi[0], 2),
        jnp.where(row < 4, up(b_hi[1], 4), jnp.where(row < 6, up(b_hi[2], 6), g_hi)),
    )
    odd = lax.rem(lax.axis_index("gy"), 2) == 1

    @pl.when(odd)
    def _():
        out_a[0], out_a[1] = low_1, low_2
        out_b[0], out_b[1] = high, high

    @pl.when(jnp.logical_not(odd))
    def _():
        out_a[0], out_a[1] = high, high
        out_b[0], out_b[1] = low_1, low_2


def pack_x(y_a, y_b, b_ref, h_ref, u_ref, out_a, out_b, halo):
    odd_y = lax.rem(lax.axis_index("gy"), 2) == 1
    row = iota((CX, 8, CZ), 1)
    up = lambda x, k: pltpu.roll(x, k % 8, 1)
    above_1 = jnp.where(odd_y, y_b[0], y_a[0])
    above_2 = jnp.where(odd_y, y_b[1], y_a[1])
    below = jnp.where(odd_y, y_a[0], y_b[0])

    def tile(head, count, tail):
        return jnp.where(row < count, head, jnp.where(row >= 6, tail, 0.0))

    halo[0] = tile(above_1, 3, up(below, 6))
    halo[1] = tile(up(above_1, -3), 3, up(below, 4))
    halo[2] = tile(above_2, 3, up(below, 2))
    halo[3] = tile(up(above_1, -6), 2, below)
    for c in range(3):
        halo[4 + c] = jnp.where(row < 1, up(above_2, -3 - c), 0.0)
    odd_x = lax.rem(lax.axis_index("gx"), 2) == 1

    def low(out):
        for c in range(3):
            for x in range(3):
                out[3 * c + x, :CY], out[3 * c + x, CY:] = b_ref[c, x], halo[c, x]
            out[11 + c, :CY], out[11 + c, CY:] = u_ref[c, 0], halo[4 + c, 0]
        for x in range(2):
            out[9 + x, :CY], out[9 + x, CY:] = degradation_of(h_ref[x]), halo[3, x]

    def high(out):
        for c in range(3):
            for x in range(2):
                out[3 * c + x, :CY], out[3 * c + x, CY:] = b_ref[c, 6 + x], halo[c, 6 + x]
            out[3 * c + 2] = jnp.zeros((ROWS, CZ), F32)
            out[11 + c] = jnp.zeros((ROWS, CZ), F32)
        for x in range(2):
            out[9 + x, :CY], out[9 + x, CY:] = degradation_of(h_ref[6 + x]), halo[3, 6 + x]

    @pl.when(odd_x)
    def _():
        low(out_a)
        high(out_b)

    @pl.when(jnp.logical_not(odd_x))
    def _():
        high(out_a)
        low(out_b)


def yz_modes(u):
    lane = iota((ROWS, CZ), 1)
    u_next = jnp.where(lane == CZ - 1, 0.0, pltpu.roll(u, CZ - 1, 1))
    out = [None] * 4
    for z, a in enumerate((u + u_next, u_next - u)):
        a_next = pltpu.roll(a, ROWS - 1, 0)
        out[z], out[2 + z] = a + a_next, a_next - a
    return out


def yz_gather(r):
    lane = iota((ROWS, CZ), 1)
    rows = []
    for z in range(2):
        s, d = r[z], r[2 + z]
        rows.append((s - d) + pltpu.roll(s + d, 1, 0))
    s, d = rows
    return (s - d) + jnp.where(lane == 0, 0.0, pltpu.roll(s + d, 1, 1))


SS, SD, DS, DD = 0, 1, 2, 3


def strains(here, there):
    s = [[here[4 * c + k] + there[4 * c + k] if k else None for k in range(4)] for c in range(3)]
    d = [[there[4 * c + k] - here[4 * c + k] for k in range(4)] for c in range(3)]
    u, v, w = range(3)
    return [
        d[u][SS], s[v][DS], s[w][SD],
        s[u][DS] + d[v][SS], s[u][SD] + d[w][SS], s[v][SD] + s[w][DS],
        s[u][DD], d[v][SD], d[w][DS],
        d[u][SD], s[v][DD], d[u][DS], s[w][DD], d[v][DS], d[w][SD],
        d[u][DD], d[v][DD], d[w][DD],
    ]


def stresses(e, g):
    scaled = (lambda k: g * k) if g is not None else (lambda k: k)
    l16, m8, m16, m48 = scaled(LAM / 16), scaled(MU / 8), scaled(MU / 16), scaled(MU / 48)
    l48, q = scaled(LAM / 48), scaled((LAM + 4 * MU) / 144)
    trace = l16 * (e[0] + e[1] + e[2])
    out = [trace + m8 * e[k] for k in range(3)]
    out += [m16 * e[k] for k in range(3, 6)]
    three = e[6] + e[7] + e[8]
    out += [m48 * (e[k] + three) for k in range(6, 9)]
    for k in (9, 11, 13):
        both = l48 * (e[k] + e[k + 1])
        out += [both + m16 * e[k], both + m16 * e[k + 1]]
    return out + [q * e[k] for k in range(15, 18)]


def x_forces(f):
    s = [[None, f[4], f[3], f[6]], [None, f[5], f[1], f[10]], [None, f[2], f[5], f[12]]]
    d = [[f[0], f[9], f[11], f[15]], [f[3], f[7], f[13], f[16]], [f[4], f[14], f[8], f[17]]]
    return [x for c in s for x in c], [x for c in d for x in c]


def inner(a, b):
    total = a[0] * b[0]
    for x, y in zip(a[1:], b[1:]):
        total = total + x * y
    return total


def main_kernel(
    b_ref, h_ref, u_ref, halo, x_a, x_b, p1_out, p2_out, t_out, row_out,
    field, g_ref, p1, p2, modes, gathered, moved, weights, sums,
):
    odd_x = lax.rem(lax.axis_index("gx"), 2) == 1
    not_last_x = jnp.where(lax.axis_index("gx") == lax.axis_size("gx") - 1, 0.0, 1.0).astype(F32)
    not_last_y = jnp.where(lax.axis_index("gy") == lax.axis_size("gy") - 1, 0.0, 1.0).astype(F32)
    row = iota((ROWS, CZ), 0)
    keep = jnp.where(jnp.logical_and(row >= CY, row < CY + 3), not_last_y, 1.0)

    def place(above, below):
        for c in range(3):
            for x in range(2):
                field[c, x] = below[3 * c + x]
            for x in range(3):
                field[c, 10 + x] = above[3 * c + x]
            moved[c, CX] = above[11 + c]
        for x in range(2):
            g_ref[x] = below[9 + x]
            g_ref[10 + x] = above[9 + x]

    @pl.when(odd_x)
    def _():
        place(x_b, x_a)

    @pl.when(jnp.logical_not(odd_x))
    def _():
        place(x_a, x_b)

    for c in range(3):
        field[c, 2:10, :CY] = b_ref[c]
        field[c, 2:10, CY:] = halo[c]
        moved[c, :CX, :CY] = u_ref[c]
        moved[c, :CX, CY:] = halo[4 + c]
    g_ref[2:10, :CY] = degradation_of(h_ref[...])
    g_ref[2:10, CY:] = halo[3]
    sums[...] = jnp.zeros_like(sums)

    def to_modes(source, layers):
        @pl.loop(0, layers)
        def _(n):
            for c in range(3):
                for k, a in enumerate(yz_modes(source[c, n])):
                    modes[4 * c + k, n] = a

    def load(n, rows):
        return [modes[k, n, rows, :] for k in range(12)]

    to_modes(moved, CX + 1)

    @pl.loop(0, CY // 8)
    def _(j):
        rows = pl.ds(pl.multiple_of(8 * j, 8), 8)
        here = load(0, rows)
        for e in range(CX):
            there = load(e + 1, rows)
            for k, f in enumerate(stresses(strains(here, there), None)):
                weights[k, e, rows, :] = f
            here = there

    def stress_gather(layers, g_first, own_first, power):
        def chunk(rows, own):
            here = load(0, rows)
            before = None
            for e in range(layers):
                there = load(e + 1, rows)
                strain = strains(here, there)
                x = e - own_first
                if own and 0 <= x < CX:
                    stiff = [weights[k, x, rows, :] for k in range(18)]
                    t_out[power, x, rows, :] = inner(strain, stiff)
                s, d = x_forces(stresses(strain, g_ref[g_first + e, rows, :]))
                if before is not None:
                    for k in range(12):
                        lower = s[k] - d[k] if s[k] is not None else -d[k]
                        gathered[k, e - 1, rows, :] = before[k] + lower
                before = [s[k] + d[k] if s[k] is not None else d[k] for k in range(12)]
                here = there

        @pl.loop(0, CY // 8)
        def _(j):
            chunk(pl.ds(pl.multiple_of(8 * j, 8), 8), True)

        chunk(pl.ds(CY, 8), False)

    def collapse(x):
        return x[0:8] + x[8:16] + x[16:24] + x[24:32]

    def nodes(layers, target, past_end):
        @pl.loop(0, layers)
        def _(n):
            factor = keep * jnp.where(n >= past_end, not_last_x, 1.0)
            for c in range(3):
                target[c, n] = factor * yz_gather([gathered[4 * c + k, n] for k in range(4)])

    to_modes(field, 13)
    stress_gather(12, 0, 2, 0)
    nodes(11, p1, 9)
    to_modes(p1, 11)
    stress_gather(10, 1, 1, 1)
    nodes(9, p2, 8)

    @pl.loop(0, CX)
    def _(x):
        for c in range(3):
            v0, v1, v2 = b_ref[c, x], p1[c, x + 1, :CY], p2[c, x, :CY]
            p1_out[c, x] = v1
            p2_out[c, x] = v2
            for k, (a, b) in enumerate(((v0, v0), (v0, v1), (v1, v1), (v1, v2), (v2, v2))):
                sums[k] += collapse(a * b)

    to_modes(p2, 9)

    @pl.loop(0, CY // 8)
    def _(j):
        rows = pl.ds(pl.multiple_of(8 * j, 8), 8)
        here = load(0, rows)
        total = jnp.zeros((8, CZ), F32)
        for e in range(CX):
            there = load(e + 1, rows)
            strain = strains(here, there)
            t_out[2, e, rows, :] = inner(strain, [weights[k, e, rows, :] for k in range(18)])
            total = total + inner(strain, stresses(strain, g_ref[2 + e, rows, :]))
            here = there
        sums[5] += total

    lane = iota((1, CZ), 1)
    line = jnp.zeros((1, CZ), F32)
    for k in range(6):
        line = jnp.where(lane == k, jnp.sum(jnp.sum(sums[k], 0, keepdims=True), 1, keepdims=True), line)
    row_out[...] = jnp.broadcast_to(line, row_out.shape)


def combine(parts, b_ref, p1, p2, t_ref, h_ref, adjoint, sensitivity):
    line = jnp.sum(parts[...], 0, keepdims=True)
    lane = iota((1, CZ), 1)
    m = [jnp.sum(jnp.where(lane == k, line, 0.0), 1, keepdims=True) for k in range(6)]
    l10, l20 = m[2] / m[1], m[3] / m[1]
    d1, h21 = m[3] - l10 * m[2], m[4] - l20 * m[2]
    l21 = h21 / d1
    d2 = m[5] - l20 * m[3] - l21 * h21
    y1 = m[1] - l10 * m[0]
    y2 = m[2] - l20 * m[0] - l21 * y1
    c2 = y2 / d2
    c1 = y1 / d1 - l21 * c2
    c0 = m[0] / m[1] - l10 * c1 - l20 * c2
    c0, c1, c2 = [jnp.broadcast_to(c, (CY, CZ)) for c in (c0, c1, c2)]
    for x in range(CX):
        for c in range(3):
            adjoint[c, x] = c0 * b_ref[c, x] + c1 * p1[c, x] + c2 * p2[c, x]
        product = c0 * t_ref[0, x] + c1 * t_ref[1, x] + c2 * t_ref[2, x]
        sensitivity[x] = 2.0 * (1.0 - h_ref[x]) * product


VMEM = pl.BlockSpec(memory_space=pltpu.VMEM)


def shape(*dims):
    return jax.ShapeDtypeStruct(dims, F32)


def body(misfit, damage, displacement):
    edge = (3, CX, 8, CZ)
    first = lambda i: (0, 0, 0, 0)
    last = lambda i: (0, 0, 3, 0)
    y_a, y_b = pl.pallas_call(
        pack_y,
        grid=(1,),
        in_specs=[
            pl.BlockSpec(edge, first),
            pl.BlockSpec(edge, last),
            pl.BlockSpec(edge[1:], lambda i: (0, 0, 0)),
            pl.BlockSpec(edge[1:], lambda i: (0, 3, 0)),
            pl.BlockSpec(edge, first),
        ],
        out_specs=[pl.BlockSpec((2, CX, 8, CZ), first)] * 2,
        out_shape=[shape(2, CX, 8, CZ)] * 2,
        name="pack_y",
        compiler_params=pltpu.CompilerParams(vmem_limit_bytes=4 << 20),
    )(misfit, misfit, damage, damage, displacement)
    y_a = exchange(y_a, "gy", 0)
    y_b = exchange(y_b, "gy", 1)
    x_a, x_b, halo = pl.pallas_call(
        pack_x,
        in_specs=[VMEM] * 5,
        out_specs=[VMEM] * 3,
        out_shape=[shape(14, ROWS, CZ)] * 2 + [shape(7, CX, 8, CZ)],
        name="pack_x",
        compiler_params=pltpu.CompilerParams(vmem_limit_bytes=8 << 20),
    )(y_a, y_b, misfit, damage, displacement)
    x_a = exchange(x_a, "gx", 0)
    x_b = exchange(x_b, "gx", 1)
    devices = lax.axis_size("gx") * lax.axis_size("gy")
    p1, p2, t, line = pl.pallas_call(
        main_kernel,
        in_specs=[VMEM] * 6,
        out_specs=[VMEM] * 4,
        out_shape=[shape(3, CX, CY, CZ)] * 3 + [shape(devices, CZ)],
        scratch_shapes=[
            pltpu.VMEM((3, 13, ROWS, CZ), F32),
            pltpu.VMEM((12, ROWS, CZ), F32),
            pltpu.VMEM((3, 11, ROWS, CZ), F32),
            pltpu.VMEM((3, 9, ROWS, CZ), F32),
            pltpu.VMEM((12, 13, ROWS, CZ), F32),
            pltpu.VMEM((12, 11, ROWS, CZ), F32),
            pltpu.VMEM((3, 9, ROWS, CZ), F32),
            pltpu.VMEM((18, CX, CY, CZ), F32),
            pltpu.VMEM((6, 8, CZ), F32),
        ],
        name="main",
        compiler_params=pltpu.CompilerParams(vmem_limit_bytes=28 << 20),
    )(misfit, damage, displacement, halo, x_a, x_b)
    parts = lax.all_to_all(line, AXES, 0, 0, tiled=True)
    return pl.pallas_call(
        combine,
        in_specs=[VMEM] * 6,
        out_specs=[VMEM] * 2,
        out_shape=[shape(3, CX, CY, CZ), shape(CX, CY, CZ)],
        name="combine",
        compiler_params=pltpu.CompilerParams(vmem_limit_bytes=12 << 20),
    )(parts, misfit, p1, p2, t, damage)


def solution(mesh):
    field, scalar = P(None, "gx", "gy", None), P("gx", "gy", None)
    return jax.shard_map(
        body, mesh=mesh, in_specs=(field, scalar, field), out_specs=(field, scalar), check_vma=False
    )
```

```python
import jax
import jax.numpy as jnp
from jax import lax
from jax.experimental import pallas as pl
from jax.experimental.pallas import tpu as pltpu
from jax.sharding import PartitionSpec as P

CX, CY, CZ = 8, 32, 128
ROWS = 40
AXES = ("gx", "gy")
LAM = 3.0 * 0.3 / (1.3 * 0.4)
MU = 3.0 / 2.6
F32 = jnp.float32


def exchange(x, axis, first):
    n = lax.axis_size(axis)
    pairs = []
    for i in range(first, n - 1, 2):
        pairs += [(i, i + 1), (i + 1, i)]
    return lax.ppermute(x, axis, pairs)


def iota(shape, dim):
    return lax.broadcasted_iota(jnp.int32, shape, dim)


def degradation_of(damage):
    return (1.0 - damage) * (1.0 - damage) + 0.001


def pack_y(b, h, u, out_a, out_b, b_lo, b_hi, h_lo, h_hi, u_lo, done):
    copies = []
    for k, (source, target) in enumerate(
        (
            (b.at[:, :, pl.ds(0, 8)], b_lo),
            (b.at[:, :, pl.ds(CY - 8, 8)], b_hi),
            (h.at[:, pl.ds(0, 8)], h_lo),
            (h.at[:, pl.ds(CY - 8, 8)], h_hi),
            (u.at[:, :, pl.ds(0, 8)], u_lo),
        )
    ):
        copies.append(pltpu.make_async_copy(source, target, done.at[k]))
        copies[-1].start()
    for copy in copies:
        copy.wait()
    row = iota((CX, 8, CZ), 1)
    g_lo, g_hi = degradation_of(h_lo[...]), degradation_of(h_hi[...])
    up = lambda x, k: pltpu.roll(x, k % 8, 1)
    low_1 = jnp.where(row < 3, b_lo[0], jnp.where(row < 6, up(b_lo[1], 3), up(g_lo, 6)))
    low_2 = jnp.where(
        row < 3,
        b_lo[2],
        jnp.where(
            row == 3, up(u_lo[0], 3), jnp.where(row == 4, up(u_lo[1], 4), up(u_lo[2], 5))
        ),
    )
    high = jnp.where(
        row < 2,
        up(b_hi[0], 2),
        jnp.where(row < 4, up(b_hi[1], 4), jnp.where(row < 6, up(b_hi[2], 6), g_hi)),
    )
    odd = lax.rem(lax.axis_index("gy"), 2) == 1

    @pl.when(odd)
    def _():
        out_a[0], out_a[1] = low_1, low_2
        out_b[0], out_b[1] = high, high

    @pl.when(jnp.logical_not(odd))
    def _():
        out_a[0], out_a[1] = high, high
        out_b[0], out_b[1] = low_1, low_2


def stage(b, h, u, b_out, h_out, u_out):
    b_out[...] = b[...]
    h_out[...] = h[...]
    u_out[...] = u[...]


def pack_x(y_a, y_b, b_ref, h_ref, u_ref, out_a, out_b, halo):
    odd_y = lax.rem(lax.axis_index("gy"), 2) == 1
    row = iota((CX, 8, CZ), 1)
    up = lambda x, k: pltpu.roll(x, k % 8, 1)
    above_1 = jnp.where(odd_y, y_b[0], y_a[0])
    above_2 = jnp.where(odd_y, y_b[1], y_a[1])
    below = jnp.where(odd_y, y_a[0], y_b[0])

    def tile(head, count, tail):
        return jnp.where(row < count, head, jnp.where(row >= 6, tail, 0.0))

    halo[0] = tile(above_1, 3, up(below, 6))
    halo[1] = tile(up(above_1, -3), 3, up(below, 4))
    halo[2] = tile(above_2, 3, up(below, 2))
    halo[3] = tile(up(above_1, -6), 2, below)
    for c in range(3):
        halo[4 + c] = jnp.where(row < 1, up(above_2, -3 - c), 0.0)
    odd_x = lax.rem(lax.axis_index("gx"), 2) == 1

    def low(out):
        for c in range(3):
            for x in range(3):
                out[3 * c + x, :CY], out[3 * c + x, CY:] = b_ref[c, x], halo[c, x]
            out[11 + c, :CY], out[11 + c, CY:] = u_ref[c, 0], halo[4 + c, 0]
        for x in range(2):
            out[9 + x, :CY], out[9 + x, CY:] = degradation_of(h_ref[x]), halo[3, x]

    def high(out):
        for c in range(3):
            for x in range(2):
                out[3 * c + x, :CY], out[3 * c + x, CY:] = b_ref[c, 6 + x], halo[c, 6 + x]
            out[3 * c + 2] = jnp.zeros((ROWS, CZ), F32)
            out[11 + c] = jnp.zeros((ROWS, CZ), F32)
        for x in range(2):
            out[9 + x, :CY], out[9 + x, CY:] = degradation_of(h_ref[6 + x]), halo[3, 6 + x]

    @pl.when(odd_x)
    def _():
        low(out_a)
        high(out_b)

    @pl.when(jnp.logical_not(odd_x))
    def _():
        high(out_a)
        low(out_b)


def yz_modes(u):
    lane = iota((ROWS, CZ), 1)
    u_next = jnp.where(lane == CZ - 1, 0.0, pltpu.roll(u, CZ - 1, 1))
    out = [None] * 4
    for z, a in enumerate((u + u_next, u_next - u)):
        a_next = pltpu.roll(a, ROWS - 1, 0)
        out[z], out[2 + z] = a + a_next, a_next - a
    return out


def yz_gather(r):
    lane = iota((ROWS, CZ), 1)
    rows = []
    for z in range(2):
        s, d = r[z], r[2 + z]
        rows.append((s - d) + pltpu.roll(s + d, 1, 0))
    s, d = rows
    return (s - d) + jnp.where(lane == 0, 0.0, pltpu.roll(s + d, 1, 1))


SS, SD, DS, DD = 0, 1, 2, 3


def strains(here, there):
    s = [[here[4 * c + k] + there[4 * c + k] if k else None for k in range(4)] for c in range(3)]
    d = [[there[4 * c + k] - here[4 * c + k] for k in range(4)] for c in range(3)]
    u, v, w = range(3)
    return [
        d[u][SS], s[v][DS], s[w][SD],
        s[u][DS] + d[v][SS], s[u][SD] + d[w][SS], s[v][SD] + s[w][DS],
        s[u][DD], d[v][SD], d[w][DS],
        d[u][SD], s[v][DD], d[u][DS], s[w][DD], d[v][DS], d[w][SD],
        d[u][DD], d[v][DD], d[w][DD],
    ]


def stresses(e, g):
    scaled = (lambda k: g * k) if g is not None else (lambda k: k)
    l16, m8, m16, m48 = scaled(LAM / 16), scaled(MU / 8), scaled(MU / 16), scaled(MU / 48)
    l48, q = scaled(LAM / 48), scaled((LAM + 4 * MU) / 144)
    trace = l16 * (e[0] + e[1] + e[2])
    out = [trace + m8 * e[k] for k in range(3)]
    out += [m16 * e[k] for k in range(3, 6)]
    three = e[6] + e[7] + e[8]
    out += [m48 * (e[k] + three) for k in range(6, 9)]
    for k in (9, 11, 13):
        both = l48 * (e[k] + e[k + 1])
        out += [both + m16 * e[k], both + m16 * e[k + 1]]
    return out + [q * e[k] for k in range(15, 18)]


def x_forces(f):
    s = [[None, f[4], f[3], f[6]], [None, f[5], f[1], f[10]], [None, f[2], f[5], f[12]]]
    d = [[f[0], f[9], f[11], f[15]], [f[3], f[7], f[13], f[16]], [f[4], f[14], f[8], f[17]]]
    return [x for c in s for x in c], [x for c in d for x in c]


def inner(a, b):
    total = a[0] * b[0]
    for x, y in zip(a[1:], b[1:]):
        total = total + x * y
    return total


def load(place, rows):
    ref, slot = place
    return [ref[k, slot, rows, :] for k in range(12)]


def to_modes(node, place):
    ref, slot = place
    for c in range(3):
        for k, a in enumerate(yz_modes(node(c))):
            ref[4 * c + k, slot] = a


def each_chunk(step, halo_too):
    @pl.loop(0, CY // 8)
    def _(j):
        step(pl.ds(pl.multiple_of(8 * j, 8), 8), True)

    if halo_too:
        step(pl.ds(CY, 8), False)


def sweep(elements, modes, g, add, put, visit=None):
    def step(rows, own):
        here = load(modes[elements[0]], rows)
        before = None

        def store(n, lower):
            if n not in put:
                return
            total = before
            if lower is not None:
                total = lower if total is None else [p + q for p, q in zip(total, lower)]
            if n in add:
                total = [p + q for p, q in zip(total, load(add[n], rows))]
            ref, slot = put[n]
            for k in range(12):
                ref[k, slot, rows, :] = total[k]

        for e in elements:
            there = load(modes[e + 1], rows)
            strain = strains(here, there)
            if own and visit is not None:
                visit(e, strain, rows)
            s, d = x_forces(stresses(strain, g(e, rows)))
            if e in put:
                store(e, [p - q if p is not None else -q for p, q in zip(s, d)])
            before = [p + q if p is not None else q for p, q in zip(s, d)]
            here = there
        store(elements[-1] + 1, None)

    each_chunk(step, True)


def finish(gathered, target, edge, factor=None):
    ref, slot = gathered
    out, at = target
    for c in range(3):
        v = yz_gather([ref[4 * c + k, slot] for k in range(4)])
        if factor is not None:
            v = v * factor
        out[c, at, :CY] = v[:CY]
        out[c, at, CY:] = v[CY:] * edge


def collapse(x):
    return x[0:8] + x[8:16] + x[16:24] + x[24:32]


def row_edge():
    row = iota((8, CZ), 0)
    last = lax.axis_index("gy") == lax.axis_size("gy") - 1
    return jnp.where(row < 3, jnp.where(last, 0.0, 1.0).astype(F32), 1.0)


KEPT = ("b", 0), ("b", 7), ("p1", 1), ("p1", 6), ("p2", 2), ("p2", 5), ("u", 7)
OPEN = ("p1", 0), ("p1", 7), ("p2", 1), ("p2", 6)
KEPT_WEIGHTS = (0, 1, 5, 6)


def inner_kernel(
    b_ref, h_ref, u_ref, halo, p1, p2, t, kept, opened, weights_out, sums,
    modes, gathered, weights, g_ref,
):
    edge = row_edge()
    g_ref[:, :CY] = degradation_of(h_ref[...])
    g_ref[:, CY:] = halo[3]
    g = lambda e, rows: g_ref[e, rows, :]
    keep = {name: (kept, k) for k, name in enumerate(KEPT)}
    open_at = {name: (opened, k) for k, name in enumerate(OPEN)}
    at = lambda name, n: keep.get((name, n), (modes, n))

    def own(ref, first, n):
        return lambda c: jnp.concatenate([ref[c, n], halo[first + c, n]], 0)

    u_modes = {n: at("u", n) for n in range(CX)}
    for n in range(CX):
        to_modes(own(u_ref, 4, n), u_modes[n])

    def stiffen(rows, _):
        here = load(u_modes[0], rows)
        for e in range(7):
            there = load(u_modes[e + 1], rows)
            for k, f in enumerate(stresses(strains(here, there), None)):
                if e in KEPT_WEIGHTS:
                    weights_out[k, KEPT_WEIGHTS.index(e), rows, :] = f
                else:
                    weights[k, e, rows, :] = f
            here = there

    each_chunk(stiffen, False)

    def weight(e, rows):
        if e in KEPT_WEIGHTS:
            return [weights_out[k, KEPT_WEIGHTS.index(e), rows, :] for k in range(18)]
        return [weights[k, e, rows, :] for k in range(18)]

    def visit(power):
        def f(e, strain, rows):
            t[power, e, rows, :] = inner(strain, weight(e, rows))

        return f

    b_modes = {n: at("b", n) for n in range(CX)}
    for n in range(CX):
        to_modes(own(b_ref, 0, n), b_modes[n])
    put = {n: (gathered, n) for n in range(1, 7)}
    put.update({0: open_at["p1", 0], 7: open_at["p1", 7]})
    sweep(range(0, 7), b_modes, g, {}, put, visit(0))
    for n in range(1, 7):
        finish(put[n], (p1, n - 1), edge)

    p1_modes = {n: at("p1", n) for n in range(1, 7)}
    for n in range(1, 7):
        to_modes(lambda c, n=n: p1[c, n - 1], p1_modes[n])
    put = {n: (gathered, n) for n in range(2, 6)}
    put.update({1: open_at["p2", 1], 6: open_at["p2", 6]})
    sweep(range(1, 6), p1_modes, g, {}, put, visit(1))
    for n in range(2, 6):
        finish(put[n], (p2, n - 2), edge)

    p2_modes = {n: at("p2", n) for n in range(2, 6)}
    for n in range(2, 6):
        to_modes(lambda c, n=n: p2[c, n - 2], p2_modes[n])
    sums[...] = jnp.zeros_like(sums)

    def energy(rows, _):
        here = load(p2_modes[2], rows)
        total = jnp.zeros((8, CZ), F32)
        for e in range(2, 5):
            there = load(p2_modes[e + 1], rows)
            strain = strains(here, there)
            t[2, e, rows, :] = inner(strain, weight(e, rows))
            total = total + inner(strain, stresses(strain, g(e, rows)))
            here = there
        sums[5] += total

    each_chunk(energy, False)
    total = [jnp.zeros((8, CZ), F32)] * 5
    for n in range(CX):
        for c in range(3):
            v = [b_ref[c, n]]
            if 1 <= n < 7:
                v.append(p1[c, n - 1, :CY])
            if 2 <= n < 6:
                v.append(p2[c, n - 2, :CY])
            for k, (i, j) in enumerate(((0, 0), (0, 1), (1, 1), (1, 2), (2, 2))):
                if j < len(v):
                    total[k] = total[k] + collapse(v[i] * v[j])
    for k in range(5):
        sums[k] = total[k]


def outer_kernel(
    b_ref, h_ref, halo, x_a, x_b, p1, p2, kept, opened, weights_in, sums_in,
    q1, q2, t, row_out, above, below, g_ref, modes, gathered, weights, sums,
):
    edge = row_edge()
    odd_x = lax.rem(lax.axis_index("gx"), 2) == 1
    last_x = lax.axis_index("gx") == lax.axis_size("gx") - 1
    past_x = jnp.where(last_x, 0.0, 1.0).astype(F32)

    @pl.when(odd_x)
    def _():
        above[...] = x_b[...]
        below[...] = x_a[...]

    @pl.when(jnp.logical_not(odd_x))
    def _():
        above[...] = x_a[...]
        below[...] = x_b[...]

    for k, e in enumerate((0, 1, 5, 6, 7)):
        g_ref[k, :CY] = degradation_of(h_ref[e])
        g_ref[k, CY:] = halo[3, e]

    def g(e, rows):
        if e < 0:
            return below[11 + e, rows, :]
        if e >= CX:
            return above[1 + e, rows, :]
        return g_ref[(0, 1, 5, 6, 7).index(e), rows, :]

    keep = {name: (kept, k) for k, name in enumerate(KEPT)}
    open_at = {name: (opened, k) for k, name in enumerate(OPEN)}
    new = [0]

    def fresh(nodes):
        out = {n: (modes, new[0] + k) for k, n in enumerate(nodes)}
        new[0] += len(nodes)
        return out

    u_modes = fresh([8])
    to_modes(lambda c: above[11 + c], u_modes[8])
    u_modes[7] = keep["u", 7]

    def stiffen(rows, _):
        f = stresses(strains(load(u_modes[7], rows), load(u_modes[8], rows)), None)
        for k in range(18):
            weights[k, rows, :] = f[k]

    each_chunk(stiffen, False)

    def weight(e, rows):
        if e == 7:
            return [weights[k, rows, :] for k in range(18)]
        return [weights_in[k, KEPT_WEIGHTS.index(e), rows, :] for k in range(18)]

    def visit(power):
        def f(e, strain, rows):
            if (power, e) in OUTER_T:
                t[OUTER_T.index((power, e)), rows, :] = inner(strain, weight(e, rows))

        return f

    b_modes = fresh([-2, -1, 8, 9, 10])
    for n in (-2, -1):
        to_modes(lambda c, n=n: below[3 * c + n + 2], b_modes[n])
    for n in (8, 9, 10):
        to_modes(lambda c, n=n: above[3 * c + n - 8], b_modes[n])
    b_modes.update({0: keep["b", 0], 7: keep["b", 7]})
    nodes = (-1, 0, 7, 8, 9)
    put = {n: (gathered, k) for k, n in enumerate(nodes)}
    sweep((-2, -1), b_modes, g, {0: open_at["p1", 0]}, put, visit(0))
    sweep((7, 8, 9), b_modes, g, {7: open_at["p1", 7]}, put, visit(0))
    for k, n in enumerate(nodes):
        finish(put[n], (q1, k), edge, past_x if n >= CX else None)

    p1_modes = fresh(nodes)
    for k, n in enumerate(nodes):
        to_modes(lambda c, k=k: q1[c, k], p1_modes[n])
    p1_modes.update({1: keep["p1", 1], 6: keep["p1", 6]})
    nodes = (0, 1, 6, 7, 8)
    put = {n: (gathered, k) for k, n in enumerate(nodes)}
    sweep((-1, 0), p1_modes, g, {1: open_at["p2", 1]}, put, visit(1))
    sweep((6, 7, 8), p1_modes, g, {6: open_at["p2", 6]}, put, visit(1))
    for k, n in enumerate(nodes):
        finish(put[n], (q2, k), edge, past_x if n >= CX else None)

    p2_modes = fresh(nodes)
    for k, n in enumerate(nodes):
        to_modes(lambda c, k=k: q2[c, k], p2_modes[n])
    p2_modes.update({2: keep["p2", 2], 5: keep["p2", 5]})
    sums[...] = sums_in[...]

    def energy(rows, _):
        total = jnp.zeros((8, CZ), F32)
        for elements in ((0, 1), (5, 6, 7)):
            here = load(p2_modes[elements[0]], rows)
            for e in elements:
                there = load(p2_modes[e + 1], rows)
                strain = strains(here, there)
                visit(2)(e, strain, rows)
                total = total + inner(strain, stresses(strain, g(e, rows)))
                here = there
        sums[5] += total

    each_chunk(energy, False)
    total = [sums[k] for k in range(5)]
    for n in (0, 1, 6, 7):
        for c in range(3):
            v1 = q1[c, (-1, 0, 7).index(n), :CY] if n in (0, 7) else p1[c, n - 1, :CY]
            v = (b_ref[c, n], v1, q2[c, (0, 1, 6, 7).index(n), :CY])
            for k, (i, j) in enumerate(((0, 0), (0, 1), (1, 1), (1, 2), (2, 2))):
                if k >= (1 if n in (0, 7) else 3):
                    total[k] = total[k] + collapse(v[i] * v[j])
    total.append(sums[5])
    lane = iota((1, CZ), 1)
    line = jnp.zeros((1, CZ), F32)
    for k in range(6):
        value = jnp.sum(jnp.sum(total[k], 0, keepdims=True), 1, keepdims=True)
        line = jnp.where(lane == k, value, line)
    row_out[...] = jnp.broadcast_to(line, row_out.shape)


OUTER_T = [(0, 7), (1, 0), (1, 6), (1, 7), (2, 0), (2, 1), (2, 5), (2, 6), (2, 7)]


def combine(parts, b_ref, h_ref, p1, p2, q1, q2, t_in, t_out, adjoint, sensitivity):
    line = jnp.sum(parts[...], 0, keepdims=True)
    lane = iota((1, CZ), 1)
    m = [jnp.sum(jnp.where(lane == k, line, 0.0), 1, keepdims=True) for k in range(6)]
    l10, l20 = m[2] / m[1], m[3] / m[1]
    d1, h21 = m[3] - l10 * m[2], m[4] - l20 * m[2]
    l21 = h21 / d1
    d2 = m[5] - l20 * m[3] - l21 * h21
    y1 = m[1] - l10 * m[0]
    y2 = m[2] - l20 * m[0] - l21 * y1
    c2 = y2 / d2
    c1 = y1 / d1 - l21 * c2
    c0 = m[0] / m[1] - l10 * c1 - l20 * c2
    weight = [jnp.broadcast_to(c, (CY, CZ)) for c in (c0, c1, c2)]
    for x in range(CX):
        for c in range(3):
            v1 = q1[c, (-1, 0, 7).index(x), :CY] if x in (0, 7) else p1[c, x - 1, :CY]
            v2 = p2[c, x - 2, :CY] if 2 <= x < 6 else q2[c, (0, 1, 6, 7).index(x), :CY]
            adjoint[c, x] = weight[0] * b_ref[c, x] + weight[1] * v1 + weight[2] * v2
        product = None
        for k in range(3):
            part = t_out[OUTER_T.index((k, x))] if (k, x) in OUTER_T else t_in[k, x]
            product = weight[k] * part if product is None else product + weight[k] * part
        sensitivity[x] = 2.0 * (1.0 - h_ref[x]) * product


VMEM = pl.BlockSpec(memory_space=pltpu.VMEM)


def shape(*dims):
    return jax.ShapeDtypeStruct(dims, F32)


def call(kernel, name, megabytes, inputs, outputs, scratch=(), in_specs=None):
    return pl.pallas_call(
        kernel,
        in_specs=in_specs or [VMEM] * len(inputs),
        out_specs=[VMEM] * len(outputs),
        out_shape=[shape(*dims) for dims in outputs],
        scratch_shapes=[s if not isinstance(s, tuple) else pltpu.VMEM(s, F32) for s in scratch],
        compiler_params=pltpu.CompilerParams(vmem_limit_bytes=megabytes and megabytes << 20),
        name=name,
    )(*inputs)


def body(misfit, damage, displacement):
    tile = (CX, 8, CZ)
    y_a, y_b = call(
        pack_y, "pack_y", None,
        (misfit, damage, displacement),
        [(2,) + tile] * 2,
        [(3,) + tile, (3,) + tile, tile, tile, (3,) + tile, pltpu.SemaphoreType.DMA((5,))],
        [pl.BlockSpec(memory_space=pltpu.HBM)] * 3,
    )
    y_b = exchange(y_b, "gy", 1)
    y_a = exchange(y_a, "gy", 0)
    misfit, damage, displacement = call(
        stage, "stage", 4,
        (misfit, damage, displacement),
        [(3, CX, CY, CZ), (CX, CY, CZ), (3, CX, CY, CZ)],
    )
    x_a, x_b, halo = call(
        pack_x, "pack_x", 6,
        (y_a, y_b, misfit, damage, displacement),
        [(14, ROWS, CZ)] * 2 + [(7,) + tile],
    )
    x_b = exchange(x_b, "gx", 1)
    x_a = exchange(x_a, "gx", 0)
    devices = lax.axis_size("gx") * lax.axis_size("gy")
    layer = (ROWS, CZ)
    p1, p2, t_in, kept, opened, weights, sums = call(
        inner_kernel, "inner", 20,
        (misfit, damage, displacement, halo),
        [
            (3, 6) + layer, (3, 4) + layer, (3, CX, CY, CZ), (12, len(KEPT)) + layer,
            (12, len(OPEN)) + layer, (18, len(KEPT_WEIGHTS), CY, CZ), (6, 8, CZ),
        ],
        [(12, CX) + layer, (12, CX) + layer, (18, CX, CY, CZ), (CX,) + layer],
    )
    q1, q2, t_out, line = call(
        outer_kernel, "outer", 20,
        (misfit, damage, halo, x_a, x_b, p1, p2, kept, opened, weights, sums),
        [(3, 5) + layer, (3, 5) + layer, (len(OUTER_T), CY, CZ), (devices, CZ)],
        [
            (14,) + layer, (14,) + layer, (5,) + layer, (12, 16) + layer, (12, 5) + layer,
            (18, CY, CZ), (6, 8, CZ),
        ],
    )
    parts = lax.all_to_all(line, AXES, 0, 0, tiled=True)
    return call(
        combine, "combine", 8,
        (parts, misfit, damage, p1, p2, q1, q2, t_in, t_out),
        [(3, CX, CY, CZ), (CX, CY, CZ)],
    )


def solution(mesh):
    field, scalar = P(None, "gx", "gy", None), P("gx", "gy", None)
    return jax.shard_map(
        body, mesh=mesh, in_specs=(field, scalar, field), out_specs=(field, scalar), check_vma=False
    )
```

```python
import jax
import jax.numpy as jnp
from jax import lax
from jax.experimental import pallas as pl
from jax.experimental.pallas import tpu as pltpu
from jax.sharding import PartitionSpec as P


CX, CY, CZ = 8, 32, 128
ROWS = 40
AXES = ("gx", "gy")
LAM = 3.0 * 0.3 / (1.3 * 0.4)
MU = 3.0 / 2.6
F32 = jnp.float32


def exchange(x, axis, first):
    n = lax.axis_size(axis)
    pairs = []
    for i in range(first, n - 1, 2):
        pairs += [(i, i + 1), (i + 1, i)]
    return lax.ppermute(x, axis, pairs)


def iota(shape, dim):
    return lax.broadcasted_iota(jnp.int32, shape, dim)


def degradation_of(damage):
    return (1.0 - damage) * (1.0 - damage) + 0.001


def pack_y(b, h, u, out_a, out_b, b_lo, b_hi, h_lo, h_hi, u_lo, done):
    copies = []
    for k, (source, target) in enumerate(
        (
            (b.at[:, :, pl.ds(0, 8)], b_lo),
            (b.at[:, :, pl.ds(CY - 8, 8)], b_hi),
            (h.at[:, pl.ds(0, 8)], h_lo),
            (h.at[:, pl.ds(CY - 8, 8)], h_hi),
            (u.at[:, :, pl.ds(0, 8)], u_lo),
        )
    ):
        copies.append(pltpu.make_async_copy(source, target, done.at[k]))
        copies[-1].start()
    for copy in copies:
        copy.wait()
    row = iota((CX, 8, CZ), 1)
    g_lo, g_hi = degradation_of(h_lo[...]), degradation_of(h_hi[...])
    up = lambda x, k: pltpu.roll(x, k % 8, 1)
    low_1 = jnp.where(row < 3, b_lo[0], jnp.where(row < 6, up(b_lo[1], 3), up(g_lo, 6)))
    low_2 = jnp.where(
        row < 3,
        b_lo[2],
        jnp.where(
            row == 3, up(u_lo[0], 3), jnp.where(row == 4, up(u_lo[1], 4), up(u_lo[2], 5))
        ),
    )
    high = jnp.where(
        row < 2,
        up(b_hi[0], 2),
        jnp.where(row < 4, up(b_hi[1], 4), jnp.where(row < 6, up(b_hi[2], 6), g_hi)),
    )
    odd = lax.rem(lax.axis_index("gy"), 2) == 1

    @pl.when(odd)
    def _():
        out_a[0], out_a[1] = low_1, low_2
        out_b[0], out_b[1] = high, high

    @pl.when(jnp.logical_not(odd))
    def _():
        out_a[0], out_a[1] = high, high
        out_b[0], out_b[1] = low_1, low_2


def stage(b, h, u, b_out, h_out, u_out):
    b_out[...] = b[...]
    h_out[...] = h[...]
    u_out[...] = u[...]


def pack_x(y_a, y_b, b_ref, h_ref, out_a, out_b, halo):
    odd_y = lax.rem(lax.axis_index("gy"), 2) == 1
    row = iota((CX, 8, CZ), 1)
    up = lambda x, k: pltpu.roll(x, k % 8, 1)
    above_1 = jnp.where(odd_y, y_b[0], y_a[0])
    above_2 = jnp.where(odd_y, y_b[1], y_a[1])
    below = jnp.where(odd_y, y_a[0], y_b[0])

    def tile(head, count, tail):
        return jnp.where(row < count, head, jnp.where(row >= 6, tail, 0.0))

    halo[0] = tile(above_1, 3, up(below, 6))
    halo[1] = tile(up(above_1, -3), 3, up(below, 4))
    halo[2] = tile(above_2, 3, up(below, 2))
    halo[3] = tile(up(above_1, -6), 2, below)
    for c in range(3):
        halo[4 + c] = jnp.where(row < 1, up(above_2, -3 - c), 0.0)
    odd_x = lax.rem(lax.axis_index("gx"), 2) == 1

    def low(out):
        for c in range(3):
            for x in range(3):
                out[3 * c + x, :CY], out[3 * c + x, CY:] = b_ref[c, x], halo[c, x]
        for x in range(2):
            out[9 + x, :CY], out[9 + x, CY:] = degradation_of(h_ref[x]), halo[3, x]

    def high(out):
        for c in range(3):
            for x in range(2):
                out[3 * c + x, :CY], out[3 * c + x, CY:] = b_ref[c, 6 + x], halo[c, 6 + x]
            out[3 * c + 2] = jnp.zeros((ROWS, CZ), F32)
        for x in range(2):
            out[9 + x, :CY], out[9 + x, CY:] = degradation_of(h_ref[6 + x]), halo[3, 6 + x]

    @pl.when(odd_x)
    def _():
        low(out_a)
        high(out_b)

    @pl.when(jnp.logical_not(odd_x))
    def _():
        high(out_a)
        low(out_b)


def yz_modes(u):
    lane = iota((ROWS, CZ), 1)
    u_next = jnp.where(lane == CZ - 1, 0.0, pltpu.roll(u, CZ - 1, 1))
    out = [None] * 4
    for z, a in enumerate((u + u_next, u_next - u)):
        a_next = pltpu.roll(a, ROWS - 1, 0)
        out[z], out[2 + z] = a + a_next, a_next - a
    return out


def yz_gather(r):
    lane = iota((ROWS, CZ), 1)
    rows = []
    for z in range(2):
        s, d = r[z], r[2 + z]
        rows.append((s - d) + pltpu.roll(s + d, 1, 0))
    s, d = rows
    return (s - d) + jnp.where(lane == 0, 0.0, pltpu.roll(s + d, 1, 1))


SS, SD, DS, DD = 0, 1, 2, 3


def strains(here, there):
    s = [[here[4 * c + k] + there[4 * c + k] if k else None for k in range(4)] for c in range(3)]
    d = [[there[4 * c + k] - here[4 * c + k] for k in range(4)] for c in range(3)]
    u, v, w = range(3)
    return [
        d[u][SS], s[v][DS], s[w][SD],
        s[u][DS] + d[v][SS], s[u][SD] + d[w][SS], s[v][SD] + s[w][DS],
        s[u][DD], d[v][SD], d[w][DS],
        d[u][SD], s[v][DD], d[u][DS], s[w][DD], d[v][DS], d[w][SD],
        d[u][DD], d[v][DD], d[w][DD],
    ]


def stresses(e, g):
    scaled = (lambda k: g * k) if g is not None else (lambda k: k)
    l16, m8, m16, m48 = scaled(LAM / 16), scaled(MU / 8), scaled(MU / 16), scaled(MU / 48)
    l48, q = scaled(LAM / 48), scaled((LAM + 4 * MU) / 144)
    trace = l16 * (e[0] + e[1] + e[2])
    out = [trace + m8 * e[k] for k in range(3)]
    out += [m16 * e[k] for k in range(3, 6)]
    three = e[6] + e[7] + e[8]
    out += [m48 * (e[k] + three) for k in range(6, 9)]
    for k in (9, 11, 13):
        both = l48 * (e[k] + e[k + 1])
        out += [both + m16 * e[k], both + m16 * e[k + 1]]
    return out + [q * e[k] for k in range(15, 18)]


def x_forces(f):
    s = [[None, f[4], f[3], f[6]], [None, f[5], f[1], f[10]], [None, f[2], f[5], f[12]]]
    d = [[f[0], f[9], f[11], f[15]], [f[3], f[7], f[13], f[16]], [f[4], f[14], f[8], f[17]]]
    return [x for c in s for x in c], [x for c in d for x in c]


def inner(a, b):
    total = a[0] * b[0]
    for x, y in zip(a[1:], b[1:]):
        total = total + x * y
    return total


def load(place, rows):
    ref, slot = place
    return [ref[k, slot, rows, :] for k in range(12)]


def to_modes(node, place):
    ref, slot = place
    for c in range(3):
        for k, a in enumerate(yz_modes(node(c))):
            ref[4 * c + k, slot] = a


def each_chunk(step, halo_too):
    @pl.loop(0, CY // 8)
    def _(j):
        step(pl.ds(pl.multiple_of(8 * j, 8), 8), True)

    if halo_too:
        step(pl.ds(CY, 8), False)


def sweep(elements, modes, g, add, put, visit=None):
    def step(rows, own):
        here = load(modes[elements[0]], rows)
        before = None

        def store(n, lower):
            if n not in put:
                return
            total = before
            if lower is not None:
                total = lower if total is None else [p + q for p, q in zip(total, lower)]
            if n in add:
                total = [p + q for p, q in zip(total, load(add[n], rows))]
            ref, slot = put[n]
            for k in range(12):
                ref[k, slot, rows, :] = total[k]

        for e in elements:
            there = load(modes[e + 1], rows)
            strain = strains(here, there)
            if own and visit is not None:
                visit(e, strain, rows)
            s, d = x_forces(stresses(strain, g(e, rows)))
            if e in put:
                store(e, [p - q if p is not None else -q for p, q in zip(s, d)])
            before = [p + q if p is not None else q for p, q in zip(s, d)]
            here = there
        store(elements[-1] + 1, None)

    each_chunk(step, True)


def finish(gathered, target, edge, factor=None):
    ref, slot = gathered
    out, at = target
    for c in range(3):
        v = yz_gather([ref[4 * c + k, slot] for k in range(4)])
        if factor is not None:
            v = v * factor
        out[c, at, :CY] = v[:CY]
        out[c, at, CY:] = v[CY:] * edge


def collapse(x):
    return x[0:8] + x[8:16] + x[16:24] + x[24:32]


def row_edge():
    row = iota((8, CZ), 0)
    last = lax.axis_index("gy") == lax.axis_size("gy") - 1
    return jnp.where(row < 3, jnp.where(last, 0.0, 1.0).astype(F32), 1.0)


KEPT = ("b", 0), ("b", 7), ("p1", 1), ("p1", 6), ("p2", 2), ("p2", 5), ("u", 7)
OPEN = ("p1", 0), ("p1", 7), ("p2", 1), ("p2", 6)
KEPT_WEIGHTS = (0, 1, 5, 6)


def inner_kernel(
    b_ref, h_ref, u_ref, halo, p1, p2, t, kept, opened, weights_out, sums, u_first,
    modes, gathered, weights, g_ref,
):
    edge = row_edge()
    u_first[:, :CY] = u_ref[:, 0]
    u_first[:, CY:] = halo[4:7, 0]
    g_ref[:, :CY] = degradation_of(h_ref[...])
    g_ref[:, CY:] = halo[3]
    g = lambda e, rows: g_ref[e, rows, :]
    keep = {name: (kept, k) for k, name in enumerate(KEPT)}
    open_at = {name: (opened, k) for k, name in enumerate(OPEN)}
    at = lambda name, n: keep.get((name, n), (modes, n))

    def own(ref, first, n):
        return lambda c: jnp.concatenate([ref[c, n], halo[first + c, n]], 0)

    u_modes = {n: at("u", n) for n in range(CX)}
    for n in range(CX):
        to_modes(own(u_ref, 4, n), u_modes[n])

    def stiffen(rows, _):
        here = load(u_modes[0], rows)
        for e in range(7):
            there = load(u_modes[e + 1], rows)
            for k, f in enumerate(stresses(strains(here, there), None)):
                if e in KEPT_WEIGHTS:
                    weights_out[k, KEPT_WEIGHTS.index(e), rows, :] = f
                else:
                    weights[k, e, rows, :] = f
            here = there

    each_chunk(stiffen, False)

    def weight(e, rows):
        if e in KEPT_WEIGHTS:
            return [weights_out[k, KEPT_WEIGHTS.index(e), rows, :] for k in range(18)]
        return [weights[k, e, rows, :] for k in range(18)]

    def visit(power):
        def f(e, strain, rows):
            t[power, e, rows, :] = inner(strain, weight(e, rows))

        return f

    b_modes = {n: at("b", n) for n in range(CX)}
    for n in range(CX):
        to_modes(own(b_ref, 0, n), b_modes[n])
    put = {n: (gathered, n) for n in range(1, 7)}
    put.update({0: open_at["p1", 0], 7: open_at["p1", 7]})
    sweep(range(0, 7), b_modes, g, {}, put, visit(0))
    for n in range(1, 7):
        finish(put[n], (p1, n - 1), edge)

    p1_modes = {n: at("p1", n) for n in range(1, 7)}
    for n in range(1, 7):
        to_modes(lambda c, n=n: p1[c, n - 1], p1_modes[n])
    put = {n: (gathered, n) for n in range(2, 6)}
    put.update({1: open_at["p2", 1], 6: open_at["p2", 6]})
    sweep(range(1, 6), p1_modes, g, {}, put, visit(1))
    for n in range(2, 6):
        finish(put[n], (p2, n - 2), edge)

    p2_modes = {n: at("p2", n) for n in range(2, 6)}
    for n in range(2, 6):
        to_modes(lambda c, n=n: p2[c, n - 2], p2_modes[n])
    sums[...] = jnp.zeros_like(sums)

    def energy(rows, _):
        here = load(p2_modes[2], rows)
        total = jnp.zeros((8, CZ), F32)
        for e in range(2, 5):
            there = load(p2_modes[e + 1], rows)
            strain = strains(here, there)
            t[2, e, rows, :] = inner(strain, weight(e, rows))
            total = total + inner(strain, stresses(strain, g(e, rows)))
            here = there
        sums[5] += total

    each_chunk(energy, False)
    total = [jnp.zeros((8, CZ), F32)] * 5
    for n in range(CX):
        for c in range(3):
            v = [b_ref[c, n]]
            if 1 <= n < 7:
                v.append(p1[c, n - 1, :CY])
            if 2 <= n < 6:
                v.append(p2[c, n - 2, :CY])
            for k, (i, j) in enumerate(((0, 0), (0, 1), (1, 1), (1, 2), (2, 2))):
                if j < len(v):
                    total[k] = total[k] + collapse(v[i] * v[j])
    for k in range(5):
        sums[k] = total[k]


def outer_kernel(
    b_ref, h_ref, halo, x_a, x_b, p1, p2, kept, opened, weights_in, sums_in,
    q1, q2, t, row_out, strain_7, above, below, g_ref, modes, gathered, sums,
):
    edge = row_edge()
    odd_x = lax.rem(lax.axis_index("gx"), 2) == 1
    last_x = lax.axis_index("gx") == lax.axis_size("gx") - 1
    past_x = jnp.where(last_x, 0.0, 1.0).astype(F32)

    @pl.when(odd_x)
    def _():
        above[...] = x_b[...]
        below[...] = x_a[...]

    @pl.when(jnp.logical_not(odd_x))
    def _():
        above[...] = x_a[...]
        below[...] = x_b[...]

    for k, e in enumerate((0, 1, 5, 6, 7)):
        g_ref[k, :CY] = degradation_of(h_ref[e])
        g_ref[k, CY:] = halo[3, e]

    def g(e, rows):
        if e < 0:
            return below[11 + e, rows, :]
        if e >= CX:
            return above[1 + e, rows, :]
        return g_ref[(0, 1, 5, 6, 7).index(e), rows, :]

    keep = {name: (kept, k) for k, name in enumerate(KEPT)}
    open_at = {name: (opened, k) for k, name in enumerate(OPEN)}
    new = [0]

    def fresh(nodes):
        out = {n: (modes, new[0] + k) for k, n in enumerate(nodes)}
        new[0] += len(nodes)
        return out

    def weight(e, rows):
        return [weights_in[k, KEPT_WEIGHTS.index(e), rows, :] for k in range(18)]

    def visit(power):
        def f(e, strain, rows):
            if e == 7:
                for k in range(18):
                    strain_7[power, k, rows, :] = strain[k]
            elif (power, e) in OUTER_T:
                t[OUTER_T.index((power, e)), rows, :] = inner(strain, weight(e, rows))

        return f

    b_modes = fresh([-2, -1, 8, 9, 10])
    for n in (-2, -1):
        to_modes(lambda c, n=n: below[3 * c + n + 2], b_modes[n])
    for n in (8, 9, 10):
        to_modes(lambda c, n=n: above[3 * c + n - 8], b_modes[n])
    b_modes.update({0: keep["b", 0], 7: keep["b", 7]})
    nodes = (-1, 0, 7, 8, 9)
    put = {n: (gathered, k) for k, n in enumerate(nodes)}
    sweep((-2, -1), b_modes, g, {0: open_at["p1", 0]}, put, visit(0))
    sweep((7, 8, 9), b_modes, g, {7: open_at["p1", 7]}, put, visit(0))
    for k, n in enumerate(nodes):
        finish(put[n], (q1, k), edge, past_x if n >= CX else None)

    p1_modes = fresh(nodes)
    for k, n in enumerate(nodes):
        to_modes(lambda c, k=k: q1[c, k], p1_modes[n])
    p1_modes.update({1: keep["p1", 1], 6: keep["p1", 6]})
    nodes = (0, 1, 6, 7, 8)
    put = {n: (gathered, k) for k, n in enumerate(nodes)}
    sweep((-1, 0), p1_modes, g, {1: open_at["p2", 1]}, put, visit(1))
    sweep((6, 7, 8), p1_modes, g, {6: open_at["p2", 6]}, put, visit(1))
    for k, n in enumerate(nodes):
        finish(put[n], (q2, k), edge, past_x if n >= CX else None)

    p2_modes = fresh(nodes)
    for k, n in enumerate(nodes):
        to_modes(lambda c, k=k: q2[c, k], p2_modes[n])
    p2_modes.update({2: keep["p2", 2], 5: keep["p2", 5]})
    sums[...] = sums_in[...]

    def energy(rows, _):
        total = jnp.zeros((8, CZ), F32)
        for elements in ((0, 1), (5, 6, 7)):
            here = load(p2_modes[elements[0]], rows)
            for e in elements:
                there = load(p2_modes[e + 1], rows)
                strain = strains(here, there)
                visit(2)(e, strain, rows)
                total = total + inner(strain, stresses(strain, g(e, rows)))
                here = there
        sums[5] += total

    each_chunk(energy, False)
    total = [sums[k] for k in range(5)]
    for n in (0, 1, 6, 7):
        for c in range(3):
            v1 = q1[c, (-1, 0, 7).index(n), :CY] if n in (0, 7) else p1[c, n - 1, :CY]
            v = (b_ref[c, n], v1, q2[c, (0, 1, 6, 7).index(n), :CY])
            for k, (i, j) in enumerate(((0, 0), (0, 1), (1, 1), (1, 2), (2, 2))):
                if k >= (1 if n in (0, 7) else 3):
                    total[k] = total[k] + collapse(v[i] * v[j])
    total.append(sums[5])
    lane = iota((1, CZ), 1)
    line = jnp.zeros((1, CZ), F32)
    for k in range(6):
        value = jnp.sum(jnp.sum(total[k], 0, keepdims=True), 1, keepdims=True)
        line = jnp.where(lane == k, value, line)
    row_out[...] = jnp.broadcast_to(line, row_out.shape)


OUTER_T = [(1, 0), (1, 6), (2, 0), (2, 1), (2, 5), (2, 6)]


def combine(
    parts, b_ref, h_ref, p1, p2, q1, q2, t_in, t_out, strain_7, kept, u_next, adjoint, sensitivity,
    modes,
):
    u_here, u_there = (kept, KEPT.index(("u", 7))), (modes, 0)
    to_modes(lambda c: u_next[c], u_there)
    line = jnp.sum(parts[...], 0, keepdims=True)
    lane = iota((1, CZ), 1)
    m = [jnp.sum(jnp.where(lane == k, line, 0.0), 1, keepdims=True) for k in range(6)]
    l10, l20 = m[2] / m[1], m[3] / m[1]
    d1, h21 = m[3] - l10 * m[2], m[4] - l20 * m[2]
    l21 = h21 / d1
    d2 = m[5] - l20 * m[3] - l21 * h21
    y1 = m[1] - l10 * m[0]
    y2 = m[2] - l20 * m[0] - l21 * y1
    c2 = y2 / d2
    c1 = y1 / d1 - l21 * c2
    c0 = m[0] / m[1] - l10 * c1 - l20 * c2
    weight = [jnp.broadcast_to(c, (CY, CZ)) for c in (c0, c1, c2)]
    for x in range(CX):
        for c in range(3):
            v1 = q1[c, (-1, 0, 7).index(x), :CY] if x in (0, 7) else p1[c, x - 1, :CY]
            v2 = p2[c, x - 2, :CY] if 2 <= x < 6 else q2[c, (0, 1, 6, 7).index(x), :CY]
            adjoint[c, x] = weight[0] * b_ref[c, x] + weight[1] * v1 + weight[2] * v2
        if x == 7:
            continue
        product = None
        for k in range(3):
            part = t_out[OUTER_T.index((k, x))] if (k, x) in OUTER_T else t_in[k, x]
            product = weight[k] * part if product is None else product + weight[k] * part
        sensitivity[x] = 2.0 * (1.0 - h_ref[x]) * product
    for j in range(0, CY, 8):
        rows = pl.ds(j, 8)
        stiff = stresses(strains(load(u_here, rows), load(u_there, rows)), None)
        product = None
        for k in range(3):
            part = weight[k][:8] * inner([strain_7[k, i, rows, :] for i in range(18)], stiff)
            product = part if product is None else product + part
        sensitivity[7, rows, :] = 2.0 * (1.0 - h_ref[7, rows, :]) * product


VMEM = pl.BlockSpec(memory_space=pltpu.VMEM)


def shape(*dims):
    return jax.ShapeDtypeStruct(dims, F32)


def call(kernel, megabytes, inputs, outputs, scratch=(), in_specs=None):
    return pl.pallas_call(
        kernel,
        in_specs=in_specs or [VMEM] * len(inputs),
        out_specs=[VMEM] * len(outputs),
        out_shape=[shape(*dims) for dims in outputs],
        scratch_shapes=[s if not isinstance(s, tuple) else pltpu.VMEM(s, F32) for s in scratch],
        compiler_params=pltpu.CompilerParams(vmem_limit_bytes=megabytes and megabytes << 20),
    )(*inputs)


def body(misfit, damage, displacement):
    tile = (CX, 8, CZ)
    y_a, y_b = call(
        pack_y, None,
        (misfit, damage, displacement),
        [(2,) + tile] * 2,
        [(3,) + tile, (3,) + tile, tile, tile, (3,) + tile, pltpu.SemaphoreType.DMA((5,))],
        [pl.BlockSpec(memory_space=pltpu.HBM)] * 3,
    )
    y_b = exchange(y_b, "gy", 1)
    y_a = exchange(y_a, "gy", 0)
    misfit, damage, displacement = call(
        stage, 4,
        (misfit, damage, displacement),
        [(3, CX, CY, CZ), (CX, CY, CZ), (3, CX, CY, CZ)],
    )
    x_a, x_b, halo = call(
        pack_x, 6,
        (y_a, y_b, misfit, damage),
        [(11, ROWS, CZ)] * 2 + [(7,) + tile],
    )
    x_b = exchange(x_b, "gx", 1)
    x_a = exchange(x_a, "gx", 0)
    devices = lax.axis_size("gx") * lax.axis_size("gy")
    layer = (ROWS, CZ)
    p1, p2, t_in, kept, opened, weights, sums, u_first = call(
        inner_kernel, 20,
        (misfit, damage, displacement, halo),
        [
            (3, 6) + layer, (3, 4) + layer, (3, CX, CY, CZ), (12, len(KEPT)) + layer,
            (12, len(OPEN)) + layer, (18, len(KEPT_WEIGHTS), CY, CZ), (6, 8, CZ), (3,) + layer,
        ],
        [(12, CX) + layer, (12, CX) + layer, (18, CX, CY, CZ), (CX,) + layer],
    )
    n = lax.axis_size("gx")
    u_next = lax.ppermute(u_first, "gx", [(i, i - 1) for i in range(1, n)])
    q1, q2, t_out, line, strain_7 = call(
        outer_kernel, 20,
        (misfit, damage, halo, x_a, x_b, p1, p2, kept, opened, weights, sums),
        [(3, 5) + layer, (3, 5) + layer, (len(OUTER_T), CY, CZ), (devices, CZ), (3, 18, CY, CZ)],
        [
            (11,) + layer, (11,) + layer, (5,) + layer, (12, 15) + layer, (12, 5) + layer,
            (6, 8, CZ),
        ],
    )
    line, u_next = lax.optimization_barrier((line, u_next))
    parts = lax.all_to_all(line, AXES, 0, 0, tiled=True)
    return call(
        combine, 8,
        (parts, misfit, damage, p1, p2, q1, q2, t_in, t_out, strain_7, kept, u_next),
        [(3, CX, CY, CZ), (CX, CY, CZ)],
        [(12, 1, ROWS, CZ)],
    )


def solution(mesh):
    field, scalar = P(None, "gx", "gy", None), P("gx", "gy", None)
    return jax.shard_map(
        body, mesh=mesh, in_specs=(field, scalar, field), out_specs=(field, scalar), check_vma=False
    )
```

```python
import jax
import jax.numpy as jnp
from jax import lax
from jax.experimental import pallas as pl
from jax.experimental.pallas import tpu as pltpu
from jax.sharding import PartitionSpec as P


CX, CY, CZ = 8, 32, 128
ROWS = 40
AXES = ("gx", "gy")
LAM = 3.0 * 0.3 / (1.3 * 0.4)
MU = 3.0 / 2.6
F32 = jnp.float32


def exchange(x, axis, first):
    n = lax.axis_size(axis)
    pairs = []
    for i in range(first, n - 1, 2):
        pairs += [(i, i + 1), (i + 1, i)]
    return lax.ppermute(x, axis, pairs)


def iota(shape, dim):
    return lax.broadcasted_iota(jnp.int32, shape, dim)


def degradation_of(damage):
    return (1.0 - damage) * (1.0 - damage) + 0.001


def pack_y(b, h, u, out_a, out_b, b_all, h_all, u_all, done):
    copies = []
    for k, (source, target) in enumerate(((h, h_all), (b, b_all), (u, u_all))):
        copies.append(pltpu.make_async_copy(source, target, done.at[k]))
        copies[-1].start()
    for copy in copies:
        copy.wait()
    b_lo, b_hi = b_all[:, :, :8], b_all[:, :, CY - 8 :]
    h_lo, h_hi = h_all[:, :8], h_all[:, CY - 8 :]
    u_lo = u_all[:, :, :8]
    row = iota((CX, 8, CZ), 1)
    g_lo, g_hi = degradation_of(h_lo), degradation_of(h_hi)
    up = lambda x, k: pltpu.roll(x, k % 8, 1)
    low_1 = jnp.where(row < 3, b_lo[0], jnp.where(row < 6, up(b_lo[1], 3), up(g_lo, 6)))
    low_2 = jnp.where(
        row < 3,
        b_lo[2],
        jnp.where(
            row == 3, up(u_lo[0], 3), jnp.where(row == 4, up(u_lo[1], 4), up(u_lo[2], 5))
        ),
    )
    high = jnp.where(
        row < 2,
        up(b_hi[0], 2),
        jnp.where(row < 4, up(b_hi[1], 4), jnp.where(row < 6, up(b_hi[2], 6), g_hi)),
    )
    odd = lax.rem(lax.axis_index("gy"), 2) == 1

    @pl.when(odd)
    def _():
        out_a[0], out_a[1] = low_1, low_2
        out_b[0], out_b[1] = high, high

    @pl.when(jnp.logical_not(odd))
    def _():
        out_a[0], out_a[1] = high, high
        out_b[0], out_b[1] = low_1, low_2


def pack_x(y_a, y_b, b_ref, h_ref, u_ref, out_a, out_b, halo, u_first):
    odd_y = lax.rem(lax.axis_index("gy"), 2) == 1
    row = iota((CX, 8, CZ), 1)
    up = lambda x, k: pltpu.roll(x, k % 8, 1)
    above_1 = jnp.where(odd_y, y_b[0], y_a[0])
    above_2 = jnp.where(odd_y, y_b[1], y_a[1])
    below = jnp.where(odd_y, y_a[0], y_b[0])

    def tile(head, count, tail):
        return jnp.where(row < count, head, jnp.where(row >= 6, tail, 0.0))

    halo[0] = tile(above_1, 3, up(below, 6))
    halo[1] = tile(up(above_1, -3), 3, up(below, 4))
    halo[2] = tile(above_2, 3, up(below, 2))
    halo[3] = tile(up(above_1, -6), 2, below)
    for c in range(3):
        halo[4 + c] = jnp.where(row < 1, up(above_2, -3 - c), 0.0)
    u_first[:, :CY] = u_ref[:, 0]
    u_first[:, CY:] = halo[4:7, 0]
    odd_x = lax.rem(lax.axis_index("gx"), 2) == 1

    def low(out):
        for c in range(3):
            for x in range(3):
                out[3 * c + x, :CY], out[3 * c + x, CY:] = b_ref[c, x], halo[c, x]
        for x in range(2):
            out[9 + x, :CY], out[9 + x, CY:] = degradation_of(h_ref[x]), halo[3, x]

    def high(out):
        for c in range(3):
            for x in range(2):
                out[3 * c + x, :CY], out[3 * c + x, CY:] = b_ref[c, 6 + x], halo[c, 6 + x]
            out[3 * c + 2] = jnp.zeros((ROWS, CZ), F32)
        for x in range(2):
            out[9 + x, :CY], out[9 + x, CY:] = degradation_of(h_ref[6 + x]), halo[3, 6 + x]

    @pl.when(odd_x)
    def _():
        low(out_a)
        high(out_b)

    @pl.when(jnp.logical_not(odd_x))
    def _():
        high(out_a)
        low(out_b)


def yz_modes(u):
    lane = iota((ROWS, CZ), 1)
    u_next = jnp.where(lane == CZ - 1, 0.0, pltpu.roll(u, CZ - 1, 1))
    out = [None] * 4
    for z, a in enumerate((u + u_next, u_next - u)):
        a_next = pltpu.roll(a, ROWS - 1, 0)
        out[z], out[2 + z] = a + a_next, a_next - a
    return out


def yz_gather(r):
    lane = iota((ROWS, CZ), 1)
    rows = []
    for z in range(2):
        s, d = r[z], r[2 + z]
        rows.append((s - d) + pltpu.roll(s + d, 1, 0))
    s, d = rows
    return (s - d) + jnp.where(lane == 0, 0.0, pltpu.roll(s + d, 1, 1))


SS, SD, DS, DD = 0, 1, 2, 3


def strains(here, there):
    s = [[here[4 * c + k] + there[4 * c + k] if k else None for k in range(4)] for c in range(3)]
    d = [[there[4 * c + k] - here[4 * c + k] for k in range(4)] for c in range(3)]
    u, v, w = range(3)
    return [
        d[u][SS], s[v][DS], s[w][SD],
        s[u][DS] + d[v][SS], s[u][SD] + d[w][SS], s[v][SD] + s[w][DS],
        s[u][DD], d[v][SD], d[w][DS],
        d[u][SD], s[v][DD], d[u][DS], s[w][DD], d[v][DS], d[w][SD],
        d[u][DD], d[v][DD], d[w][DD],
    ]


def stresses(e, g):
    scaled = (lambda k: g * k) if g is not None else (lambda k: k)
    l16, m8, m16, m48 = scaled(LAM / 16), scaled(MU / 8), scaled(MU / 16), scaled(MU / 48)
    l48, q = scaled(LAM / 48), scaled((LAM + 4 * MU) / 144)
    trace = l16 * (e[0] + e[1] + e[2])
    out = [trace + m8 * e[k] for k in range(3)]
    out += [m16 * e[k] for k in range(3, 6)]
    three = e[6] + e[7] + e[8]
    out += [m48 * (e[k] + three) for k in range(6, 9)]
    for k in (9, 11, 13):
        both = l48 * (e[k] + e[k + 1])
        out += [both + m16 * e[k], both + m16 * e[k + 1]]
    return out + [q * e[k] for k in range(15, 18)]


def x_forces(f):
    s = [[None, f[4], f[3], f[6]], [None, f[5], f[1], f[10]], [None, f[2], f[5], f[12]]]
    d = [[f[0], f[9], f[11], f[15]], [f[3], f[7], f[13], f[16]], [f[4], f[14], f[8], f[17]]]
    return [x for c in s for x in c], [x for c in d for x in c]


def inner(a, b):
    total = a[0] * b[0]
    for x, y in zip(a[1:], b[1:]):
        total = total + x * y
    return total


def load(place, rows):
    ref, slot = place
    return [ref[k, slot, rows, :] for k in range(12)]


def to_modes(node, place):
    ref, slot = place
    for c in range(3):
        for k, a in enumerate(yz_modes(node(c))):
            ref[4 * c + k, slot] = a


def each_chunk(step, halo_too):
    @pl.loop(0, CY // 8)
    def _(j):
        step(pl.ds(pl.multiple_of(8 * j, 8), 8), True)

    if halo_too:
        step(pl.ds(CY, 8), False)


def sweep(elements, modes, g, add, put, visit=None):
    def step(rows, own):
        here = load(modes[elements[0]], rows)
        before = None

        def store(n, lower):
            if n not in put:
                return
            total = before
            if lower is not None:
                total = lower if total is None else [p + q for p, q in zip(total, lower)]
            if n in add:
                total = [p + q for p, q in zip(total, load(add[n], rows))]
            ref, slot = put[n]
            for k in range(12):
                ref[k, slot, rows, :] = total[k]

        for e in elements:
            there = load(modes[e + 1], rows)
            strain = strains(here, there)
            if own and visit is not None:
                visit(e, strain, rows)
            s, d = x_forces(stresses(strain, g(e, rows)))
            if e in put:
                store(e, [p - q if p is not None else -q for p, q in zip(s, d)])
            before = [p + q if p is not None else q for p, q in zip(s, d)]
            here = there
        store(elements[-1] + 1, None)

    each_chunk(step, True)


def finish(gathered, target, edge, factor=None):
    ref, slot = gathered
    out, at = target
    for c in range(3):
        v = yz_gather([ref[4 * c + k, slot] for k in range(4)])
        if factor is not None:
            v = v * factor
        out[c, at, :CY] = v[:CY]
        out[c, at, CY:] = v[CY:] * edge


def collapse(x):
    return x[0:8] + x[8:16] + x[16:24] + x[24:32]


def row_edge():
    row = iota((8, CZ), 0)
    last = lax.axis_index("gy") == lax.axis_size("gy") - 1
    return jnp.where(row < 3, jnp.where(last, 0.0, 1.0).astype(F32), 1.0)


KEPT = ("b", 0), ("b", 7), ("p1", 1), ("p1", 6), ("p2", 2), ("p2", 5), ("u", 7)
OPEN = ("p1", 0), ("p1", 7), ("p2", 1), ("p2", 6)
KEPT_WEIGHTS = (0, 1, 5, 6)


def inner_kernel(
    b_ref, h_ref, u_ref, halo, p1, p2, t, kept, opened, weights_out, sums,
    modes, gathered, weights, g_ref,
):
    edge = row_edge()
    g_ref[:, :CY] = degradation_of(h_ref[...])
    g_ref[:, CY:] = halo[3]
    g = lambda e, rows: g_ref[e, rows, :]
    keep = {name: (kept, k) for k, name in enumerate(KEPT)}
    open_at = {name: (opened, k) for k, name in enumerate(OPEN)}
    at = lambda name, n: keep.get((name, n), (modes, n))

    def own(ref, first, n):
        return lambda c: jnp.concatenate([ref[c, n], halo[first + c, n]], 0)

    u_modes = {n: at("u", n) for n in range(CX)}
    for n in range(CX):
        to_modes(own(u_ref, 4, n), u_modes[n])

    def stiffen(rows, _):
        here = load(u_modes[0], rows)
        for e in range(7):
            there = load(u_modes[e + 1], rows)
            for k, f in enumerate(stresses(strains(here, there), None)):
                if e in KEPT_WEIGHTS:
                    weights_out[k, KEPT_WEIGHTS.index(e), rows, :] = f
                else:
                    weights[k, e, rows, :] = f
            here = there

    each_chunk(stiffen, False)

    def weight(e, rows):
        if e in KEPT_WEIGHTS:
            return [weights_out[k, KEPT_WEIGHTS.index(e), rows, :] for k in range(18)]
        return [weights[k, e, rows, :] for k in range(18)]

    def visit(power):
        def f(e, strain, rows):
            t[power, e, rows, :] = inner(strain, weight(e, rows))

        return f

    b_modes = {n: at("b", n) for n in range(CX)}
    for n in range(CX):
        to_modes(own(b_ref, 0, n), b_modes[n])
    put = {n: (gathered, n) for n in range(1, 7)}
    put.update({0: open_at["p1", 0], 7: open_at["p1", 7]})
    sweep(range(0, 7), b_modes, g, {}, put, visit(0))
    for n in range(1, 7):
        finish(put[n], (p1, n - 1), edge)

    p1_modes = {n: at("p1", n) for n in range(1, 7)}
    for n in range(1, 7):
        to_modes(lambda c, n=n: p1[c, n - 1], p1_modes[n])
    put = {n: (gathered, n) for n in range(2, 6)}
    put.update({1: open_at["p2", 1], 6: open_at["p2", 6]})
    sweep(range(1, 6), p1_modes, g, {}, put, visit(1))
    for n in range(2, 6):
        finish(put[n], (p2, n - 2), edge)

    p2_modes = {n: at("p2", n) for n in range(2, 6)}
    for n in range(2, 6):
        to_modes(lambda c, n=n: p2[c, n - 2], p2_modes[n])
    sums[...] = jnp.zeros_like(sums)

    def energy(rows, _):
        here = load(p2_modes[2], rows)
        total = jnp.zeros((8, CZ), F32)
        for e in range(2, 5):
            there = load(p2_modes[e + 1], rows)
            strain = strains(here, there)
            t[2, e, rows, :] = inner(strain, weight(e, rows))
            total = total + inner(strain, stresses(strain, g(e, rows)))
            here = there
        sums[5] += total

    each_chunk(energy, False)
    total = [jnp.zeros((8, CZ), F32)] * 5
    for n in range(CX):
        for c in range(3):
            v = [b_ref[c, n]]
            if 1 <= n < 7:
                v.append(p1[c, n - 1, :CY])
            if 2 <= n < 6:
                v.append(p2[c, n - 2, :CY])
            for k, (i, j) in enumerate(((0, 0), (0, 1), (1, 1), (1, 2), (2, 2))):
                if j < len(v):
                    total[k] = total[k] + collapse(v[i] * v[j])
    for k in range(5):
        sums[k] = total[k]


def outer_kernel(
    b_ref, h_ref, halo, x_a, x_b, p1, p2, kept, opened, weights_in, sums_in,
    q1, q2, t, row_out, strain_7, above, below, g_ref, modes, gathered, sums,
):
    edge = row_edge()
    odd_x = lax.rem(lax.axis_index("gx"), 2) == 1
    last_x = lax.axis_index("gx") == lax.axis_size("gx") - 1
    past_x = jnp.where(last_x, 0.0, 1.0).astype(F32)

    @pl.when(odd_x)
    def _():
        above[...] = x_b[...]
        below[...] = x_a[...]

    @pl.when(jnp.logical_not(odd_x))
    def _():
        above[...] = x_a[...]
        below[...] = x_b[...]

    for k, e in enumerate((0, 1, 5, 6, 7)):
        g_ref[k, :CY] = degradation_of(h_ref[e])
        g_ref[k, CY:] = halo[3, e]

    def g(e, rows):
        if e < 0:
            return below[11 + e, rows, :]
        if e >= CX:
            return above[1 + e, rows, :]
        return g_ref[(0, 1, 5, 6, 7).index(e), rows, :]

    keep = {name: (kept, k) for k, name in enumerate(KEPT)}
    open_at = {name: (opened, k) for k, name in enumerate(OPEN)}
    new = [0]

    def fresh(nodes):
        out = {n: (modes, new[0] + k) for k, n in enumerate(nodes)}
        new[0] += len(nodes)
        return out

    def weight(e, rows):
        return [weights_in[k, KEPT_WEIGHTS.index(e), rows, :] for k in range(18)]

    def visit(power):
        def f(e, strain, rows):
            if e == 7:
                for k in range(18):
                    strain_7[power, k, rows, :] = strain[k]
            elif (power, e) in OUTER_T:
                t[OUTER_T.index((power, e)), rows, :] = inner(strain, weight(e, rows))

        return f

    b_modes = fresh([-2, -1, 8, 9, 10])
    for n in (-2, -1):
        to_modes(lambda c, n=n: below[3 * c + n + 2], b_modes[n])
    for n in (8, 9, 10):
        to_modes(lambda c, n=n: above[3 * c + n - 8], b_modes[n])
    b_modes.update({0: keep["b", 0], 7: keep["b", 7]})
    nodes = (-1, 0, 7, 8, 9)
    put = {n: (gathered, k) for k, n in enumerate(nodes)}
    sweep((-2, -1), b_modes, g, {0: open_at["p1", 0]}, put, visit(0))
    sweep((7, 8, 9), b_modes, g, {7: open_at["p1", 7]}, put, visit(0))
    for k, n in enumerate(nodes):
        finish(put[n], (q1, k), edge, past_x if n >= CX else None)

    p1_modes = fresh(nodes)
    for k, n in enumerate(nodes):
        to_modes(lambda c, k=k: q1[c, k], p1_modes[n])
    p1_modes.update({1: keep["p1", 1], 6: keep["p1", 6]})
    nodes = (0, 1, 6, 7, 8)
    put = {n: (gathered, k) for k, n in enumerate(nodes)}
    sweep((-1, 0), p1_modes, g, {1: open_at["p2", 1]}, put, visit(1))
    sweep((6, 7, 8), p1_modes, g, {6: open_at["p2", 6]}, put, visit(1))
    for k, n in enumerate(nodes):
        finish(put[n], (q2, k), edge, past_x if n >= CX else None)

    p2_modes = fresh(nodes)
    for k, n in enumerate(nodes):
        to_modes(lambda c, k=k: q2[c, k], p2_modes[n])
    p2_modes.update({2: keep["p2", 2], 5: keep["p2", 5]})
    sums[...] = sums_in[...]

    def energy(rows, _):
        total = jnp.zeros((8, CZ), F32)
        for elements in ((0, 1), (5, 6, 7)):
            here = load(p2_modes[elements[0]], rows)
            for e in elements:
                there = load(p2_modes[e + 1], rows)
                strain = strains(here, there)
                visit(2)(e, strain, rows)
                total = total + inner(strain, stresses(strain, g(e, rows)))
                here = there
        sums[5] += total

    each_chunk(energy, False)
    total = [sums[k] for k in range(5)]
    for n in (0, 1, 6, 7):
        for c in range(3):
            v1 = q1[c, (-1, 0, 7).index(n), :CY] if n in (0, 7) else p1[c, n - 1, :CY]
            v = (b_ref[c, n], v1, q2[c, (0, 1, 6, 7).index(n), :CY])
            for k, (i, j) in enumerate(((0, 0), (0, 1), (1, 1), (1, 2), (2, 2))):
                if k >= (1 if n in (0, 7) else 3):
                    total[k] = total[k] + collapse(v[i] * v[j])
    total.append(sums[5])
    lane = iota((1, CZ), 1)
    line = jnp.zeros((1, CZ), F32)
    for k in range(6):
        value = jnp.sum(jnp.sum(total[k], 0, keepdims=True), 1, keepdims=True)
        line = jnp.where(lane == k, value, line)
    row_out[...] = jnp.broadcast_to(line, row_out.shape)


OUTER_T = [(1, 0), (1, 6), (2, 0), (2, 1), (2, 5), (2, 6)]


def combine(
    parts, b_ref, h_ref, p1, p2, q1, q2, t_in, t_out, strain_7, kept, u_next, adjoint, sensitivity,
    modes,
):
    u_here, u_there = (kept, KEPT.index(("u", 7))), (modes, 0)
    to_modes(lambda c: u_next[c], u_there)
    line = jnp.sum(parts[...], 0, keepdims=True)
    lane = iota((1, CZ), 1)
    m = [jnp.sum(jnp.where(lane == k, line, 0.0), 1, keepdims=True) for k in range(6)]
    l10, l20 = m[2] / m[1], m[3] / m[1]
    d1, h21 = m[3] - l10 * m[2], m[4] - l20 * m[2]
    l21 = h21 / d1
    d2 = m[5] - l20 * m[3] - l21 * h21
    y1 = m[1] - l10 * m[0]
    y2 = m[2] - l20 * m[0] - l21 * y1
    c2 = y2 / d2
    c1 = y1 / d1 - l21 * c2
    c0 = m[0] / m[1] - l10 * c1 - l20 * c2
    weight = [jnp.broadcast_to(c, (CY, CZ)) for c in (c0, c1, c2)]
    for x in range(CX):
        for c in range(3):
            v1 = q1[c, (-1, 0, 7).index(x), :CY] if x in (0, 7) else p1[c, x - 1, :CY]
            v2 = p2[c, x - 2, :CY] if 2 <= x < 6 else q2[c, (0, 1, 6, 7).index(x), :CY]
            adjoint[c, x] = weight[0] * b_ref[c, x] + weight[1] * v1 + weight[2] * v2
        if x == 7:
            continue
        product = None
        for k in range(3):
            part = t_out[OUTER_T.index((k, x))] if (k, x) in OUTER_T else t_in[k, x]
            product = weight[k] * part if product is None else product + weight[k] * part
        sensitivity[x] = 2.0 * (1.0 - h_ref[x]) * product
    for j in range(0, CY, 8):
        rows = pl.ds(j, 8)
        stiff = stresses(strains(load(u_here, rows), load(u_there, rows)), None)
        product = None
        for k in range(3):
            part = weight[k][:8] * inner([strain_7[k, i, rows, :] for i in range(18)], stiff)
            product = part if product is None else product + part
        sensitivity[7, rows, :] = 2.0 * (1.0 - h_ref[7, rows, :]) * product


VMEM = pl.BlockSpec(memory_space=pltpu.VMEM)


def shape(*dims):
    return jax.ShapeDtypeStruct(dims, F32)


def call(kernel, megabytes, inputs, outputs, scratch=(), in_specs=None):
    return pl.pallas_call(
        kernel,
        in_specs=in_specs or [VMEM] * len(inputs),
        out_specs=[VMEM] * len(outputs),
        out_shape=[shape(*dims) for dims in outputs],
        scratch_shapes=[s if not isinstance(s, tuple) else pltpu.VMEM(s, F32) for s in scratch],
        compiler_params=pltpu.CompilerParams(vmem_limit_bytes=megabytes and int(megabytes * 2**20)),
    )(*inputs)


def body(misfit, damage, displacement):
    tile = (CX, 8, CZ)
    y_a, y_b, misfit, damage, displacement = call(
        pack_y, 4,
        [pltpu.with_memory_space_constraint(x, pltpu.HBM) for x in (misfit, damage, displacement)],
        [(2,) + tile, (2,) + tile, (3, CX, CY, CZ), (CX, CY, CZ), (3, CX, CY, CZ)],
        [pltpu.SemaphoreType.DMA((3,))],
        [pl.BlockSpec(memory_space=pltpu.HBM)] * 3,
    )
    y_b = exchange(y_b, "gy", 1)
    y_a = exchange(y_a, "gy", 0)
    x_a, x_b, halo, u_first = call(
        pack_x, 6,
        (y_a, y_b, misfit, damage, displacement),
        [(11, ROWS, CZ)] * 2 + [(7,) + tile, (3, ROWS, CZ)],
    )
    x_b = exchange(x_b, "gx", 1)
    x_a = exchange(x_a, "gx", 0)
    devices = lax.axis_size("gx") * lax.axis_size("gy")
    layer = (ROWS, CZ)
    n = lax.axis_size("gx")
    u_next = lax.ppermute(u_first, "gx", [(i, i - 1) for i in range(1, n)])
    p1, p2, t_in, kept, opened, weights, sums = call(
        inner_kernel, 20,
        (misfit, damage, displacement, halo),
        [
            (3, 6) + layer, (3, 4) + layer, (3, CX, CY, CZ), (12, len(KEPT)) + layer,
            (12, len(OPEN)) + layer, (18, len(KEPT_WEIGHTS), CY, CZ), (6, 8, CZ),
        ],
        [(12, CX) + layer, (12, CX) + layer, (18, CX, CY, CZ), (CX,) + layer],
    )
    q1, q2, t_out, line, strain_7 = call(
        outer_kernel, 20,
        (misfit, damage, halo, x_a, x_b, p1, p2, kept, opened, weights, sums),
        [(3, 5) + layer, (3, 5) + layer, (len(OUTER_T), CY, CZ), (devices, CZ), (3, 18, CY, CZ)],
        [
            (11,) + layer, (11,) + layer, (5,) + layer, (12, 15) + layer, (12, 5) + layer,
            (6, 8, CZ),
        ],
    )
    line, u_next = lax.optimization_barrier((line, u_next))
    parts = lax.all_to_all(line, AXES, 0, 0, tiled=True)
    return call(
        combine, 8,
        (parts, misfit, damage, p1, p2, q1, q2, t_in, t_out, strain_7, kept, u_next),
        [(3, CX, CY, CZ), (CX, CY, CZ)],
        [(12, 1, ROWS, CZ)],
    )


def solution(mesh):
    field, scalar = P(None, "gx", "gy", None), P("gx", "gy", None)
    return jax.shard_map(
        body, mesh=mesh, in_specs=(field, scalar, field), out_specs=(field, scalar), check_vma=False
    )
```

```python
import jax
import jax.numpy as jnp
from jax import lax
from jax.experimental import pallas as pl
from jax.experimental.pallas import tpu as pltpu
from jax.sharding import PartitionSpec as P


CX, CY, CZ = 8, 32, 128
ROWS = 40
AXES = ("gx", "gy")
LAM = 3.0 * 0.3 / (1.3 * 0.4)
MU = 3.0 / 2.6
F32 = jnp.float32


def exchange(x, axis, first):
    n = lax.axis_size(axis)
    pairs = []
    for i in range(first, n - 1, 2):
        pairs += [(i, i + 1), (i + 1, i)]
    return lax.ppermute(x, axis, pairs)


def iota(shape, dim):
    return lax.broadcasted_iota(jnp.int32, shape, dim)


def degradation_of(damage):
    return (1.0 - damage) * (1.0 - damage) + 0.001


def pack_y(b, h, u, out_a, out_b, b_all, h_all, u_all, u_first, done):
    copies = []
    for k, (source, target) in enumerate(((h, h_all), (b, b_all), (u, u_all))):
        copies.append(pltpu.make_async_copy(source, target, done.at[k]))
        copies[-1].start()
    for copy in copies:
        copy.wait()
    u_first[...] = u_all[:, 0]
    b_lo, b_hi = b_all[:, :, :8], b_all[:, :, CY - 8 :]
    h_lo, h_hi = h_all[:, :8], h_all[:, CY - 8 :]
    u_lo = u_all[:, :, :8]
    row = iota((CX, 8, CZ), 1)
    g_lo, g_hi = degradation_of(h_lo), degradation_of(h_hi)
    up = lambda x, k: pltpu.roll(x, k % 8, 1)
    low_1 = jnp.where(row < 3, b_lo[0], jnp.where(row < 6, up(b_lo[1], 3), up(g_lo, 6)))
    low_2 = jnp.where(
        row < 3,
        b_lo[2],
        jnp.where(
            row == 3, up(u_lo[0], 3), jnp.where(row == 4, up(u_lo[1], 4), up(u_lo[2], 5))
        ),
    )
    high = jnp.where(
        row < 2,
        up(b_hi[0], 2),
        jnp.where(row < 4, up(b_hi[1], 4), jnp.where(row < 6, up(b_hi[2], 6), g_hi)),
    )
    odd = lax.rem(lax.axis_index("gy"), 2) == 1

    @pl.when(odd)
    def _():
        out_a[0], out_a[1] = low_1, low_2
        out_b[0], out_b[1] = high, high

    @pl.when(jnp.logical_not(odd))
    def _():
        out_a[0], out_a[1] = high, high
        out_b[0], out_b[1] = low_1, low_2


def pack_x(y_a, y_b, b_ref, h_ref, out_a, out_b, halo):
    odd_y = lax.rem(lax.axis_index("gy"), 2) == 1
    row = iota((CX, 8, CZ), 1)
    up = lambda x, k: pltpu.roll(x, k % 8, 1)
    above_1 = jnp.where(odd_y, y_b[0], y_a[0])
    above_2 = jnp.where(odd_y, y_b[1], y_a[1])
    below = jnp.where(odd_y, y_a[0], y_b[0])

    def tile(head, count, tail):
        return jnp.where(row < count, head, jnp.where(row >= 6, tail, 0.0))

    halo[0] = tile(above_1, 3, up(below, 6))
    halo[1] = tile(up(above_1, -3), 3, up(below, 4))
    halo[2] = tile(above_2, 3, up(below, 2))
    halo[3] = tile(up(above_1, -6), 2, below)
    for c in range(3):
        halo[4 + c] = jnp.where(row < 1, up(above_2, -3 - c), 0.0)
    odd_x = lax.rem(lax.axis_index("gx"), 2) == 1

    def low(out):
        for c in range(3):
            for x in range(3):
                edge = halo[c, x]
                if x == 0:
                    edge = jnp.where(row[0] == 3, pltpu.roll(halo[4 + c, 0], 3, 0), edge)
                out[3 * c + x, :CY], out[3 * c + x, CY:] = b_ref[c, x], edge
        for x in range(2):
            out[9 + x, :CY], out[9 + x, CY:] = degradation_of(h_ref[x]), halo[3, x]

    def high(out):
        for c in range(3):
            for x in range(2):
                out[3 * c + x, :CY], out[3 * c + x, CY:] = b_ref[c, 6 + x], halo[c, 6 + x]
            out[3 * c + 2] = jnp.zeros((ROWS, CZ), F32)
        for x in range(2):
            out[9 + x, :CY], out[9 + x, CY:] = degradation_of(h_ref[6 + x]), halo[3, 6 + x]

    @pl.when(odd_x)
    def _():
        low(out_a)
        high(out_b)

    @pl.when(jnp.logical_not(odd_x))
    def _():
        high(out_a)
        low(out_b)


def yz_modes(u):
    lane = iota((ROWS, CZ), 1)
    u_next = jnp.where(lane == CZ - 1, 0.0, pltpu.roll(u, CZ - 1, 1))
    out = [None] * 4
    for z, a in enumerate((u + u_next, u_next - u)):
        a_next = pltpu.roll(a, ROWS - 1, 0)
        out[z], out[2 + z] = a + a_next, a_next - a
    return out


def yz_gather(r):
    lane = iota((ROWS, CZ), 1)
    rows = []
    for z in range(2):
        s, d = r[z], r[2 + z]
        rows.append((s - d) + pltpu.roll(s + d, 1, 0))
    s, d = rows
    return (s - d) + jnp.where(lane == 0, 0.0, pltpu.roll(s + d, 1, 1))


SS, SD, DS, DD = 0, 1, 2, 3


def strains(here, there):
    s = [[here[4 * c + k] + there[4 * c + k] if k else None for k in range(4)] for c in range(3)]
    d = [[there[4 * c + k] - here[4 * c + k] for k in range(4)] for c in range(3)]
    u, v, w = range(3)
    return [
        d[u][SS], s[v][DS], s[w][SD],
        s[u][DS] + d[v][SS], s[u][SD] + d[w][SS], s[v][SD] + s[w][DS],
        s[u][DD], d[v][SD], d[w][DS],
        d[u][SD], s[v][DD], d[u][DS], s[w][DD], d[v][DS], d[w][SD],
        d[u][DD], d[v][DD], d[w][DD],
    ]


def stresses(e, g):
    scaled = (lambda k: g * k) if g is not None else (lambda k: k)
    l16, m8, m16, m48 = scaled(LAM / 16), scaled(MU / 8), scaled(MU / 16), scaled(MU / 48)
    l48, q = scaled(LAM / 48), scaled((LAM + 4 * MU) / 144)
    trace = l16 * (e[0] + e[1] + e[2])
    out = [trace + m8 * e[k] for k in range(3)]
    out += [m16 * e[k] for k in range(3, 6)]
    three = e[6] + e[7] + e[8]
    out += [m48 * (e[k] + three) for k in range(6, 9)]
    for k in (9, 11, 13):
        both = l48 * (e[k] + e[k + 1])
        out += [both + m16 * e[k], both + m16 * e[k + 1]]
    return out + [q * e[k] for k in range(15, 18)]


def x_forces(f):
    s = [[None, f[4], f[3], f[6]], [None, f[5], f[1], f[10]], [None, f[2], f[5], f[12]]]
    d = [[f[0], f[9], f[11], f[15]], [f[3], f[7], f[13], f[16]], [f[4], f[14], f[8], f[17]]]
    return [x for c in s for x in c], [x for c in d for x in c]


def inner(a, b):
    total = a[0] * b[0]
    for x, y in zip(a[1:], b[1:]):
        total = total + x * y
    return total


def load(place, rows):
    ref, slot = place
    return [ref[k, slot, rows, :] for k in range(12)]


def to_modes(node, place):
    ref, slot = place
    for c in range(3):
        for k, a in enumerate(yz_modes(node(c))):
            ref[4 * c + k, slot] = a


def each_chunk(step, halo_too):
    @pl.loop(0, CY // 8)
    def _(j):
        step(pl.ds(pl.multiple_of(8 * j, 8), 8), True)

    if halo_too:
        step(pl.ds(CY, 8), False)


def sweep(elements, modes, g, add, put, visit=None):
    def step(rows, own):
        here = load(modes[elements[0]], rows)
        before = None

        def store(n, lower):
            if n not in put:
                return
            total = before
            if lower is not None:
                total = lower if total is None else [p + q for p, q in zip(total, lower)]
            if n in add:
                total = [p + q for p, q in zip(total, load(add[n], rows))]
            ref, slot = put[n]
            for k in range(12):
                ref[k, slot, rows, :] = total[k]

        for e in elements:
            there = load(modes[e + 1], rows)
            strain = strains(here, there)
            if own and visit is not None:
                visit(e, strain, rows)
            s, d = x_forces(stresses(strain, g(e, rows)))
            if e in put:
                store(e, [p - q if p is not None else -q for p, q in zip(s, d)])
            before = [p + q if p is not None else q for p, q in zip(s, d)]
            here = there
        store(elements[-1] + 1, None)

    each_chunk(step, True)


def finish(gathered, target, edge, factor=None):
    ref, slot = gathered
    out, at = target
    for c in range(3):
        v = yz_gather([ref[4 * c + k, slot] for k in range(4)])
        if factor is not None:
            v = v * factor
        out[c, at, :CY] = v[:CY]
        out[c, at, CY:] = v[CY:] * edge


def collapse(x):
    return x[0:8] + x[8:16] + x[16:24] + x[24:32]


def row_edge():
    row = iota((8, CZ), 0)
    last = lax.axis_index("gy") == lax.axis_size("gy") - 1
    return jnp.where(row < 3, jnp.where(last, 0.0, 1.0).astype(F32), 1.0)


KEPT = ("b", 0), ("b", 7), ("p1", 1), ("p1", 6), ("p2", 2), ("p2", 5), ("u", 7)
OPEN = ("p1", 0), ("p1", 7), ("p2", 1), ("p2", 6)
KEPT_WEIGHTS = (0, 1, 5, 6)


def inner_kernel(
    b_ref, h_ref, u_ref, halo, p1, p2, t, kept, opened, weights_out, sums,
    modes, gathered, weights, g_ref,
):
    edge = row_edge()
    g_ref[:, :CY] = degradation_of(h_ref[...])
    g_ref[:, CY:] = halo[3]
    g = lambda e, rows: g_ref[e, rows, :]
    keep = {name: (kept, k) for k, name in enumerate(KEPT)}
    open_at = {name: (opened, k) for k, name in enumerate(OPEN)}
    at = lambda name, n: keep.get((name, n), (modes, n))

    def own(ref, first, n):
        return lambda c: jnp.concatenate([ref[c, n], halo[first + c, n]], 0)

    u_modes = {n: at("u", n) for n in range(CX)}
    for n in range(CX):
        to_modes(own(u_ref, 4, n), u_modes[n])

    def stiffen(rows, _):
        here = load(u_modes[0], rows)
        for e in range(7):
            there = load(u_modes[e + 1], rows)
            for k, f in enumerate(stresses(strains(here, there), None)):
                if e in KEPT_WEIGHTS:
                    weights_out[k, KEPT_WEIGHTS.index(e), rows, :] = f
                else:
                    weights[k, e, rows, :] = f
            here = there

    each_chunk(stiffen, False)

    def weight(e, rows):
        if e in KEPT_WEIGHTS:
            return [weights_out[k, KEPT_WEIGHTS.index(e), rows, :] for k in range(18)]
        return [weights[k, e, rows, :] for k in range(18)]

    def visit(power):
        def f(e, strain, rows):
            t[power, e, rows, :] = inner(strain, weight(e, rows))

        return f

    b_modes = {n: at("b", n) for n in range(CX)}
    for n in range(CX):
        to_modes(own(b_ref, 0, n), b_modes[n])
    put = {n: (gathered, n) for n in range(1, 7)}
    put.update({0: open_at["p1", 0], 7: open_at["p1", 7]})
    sweep(range(0, 7), b_modes, g, {}, put, visit(0))
    for n in range(1, 7):
        finish(put[n], (p1, n - 1), edge)

    p1_modes = {n: at("p1", n) for n in range(1, 7)}
    for n in range(1, 7):
        to_modes(lambda c, n=n: p1[c, n - 1], p1_modes[n])
    put = {n: (gathered, n) for n in range(2, 6)}
    put.update({1: open_at["p2", 1], 6: open_at["p2", 6]})
    sweep(range(1, 6), p1_modes, g, {}, put, visit(1))
    for n in range(2, 6):
        finish(put[n], (p2, n - 2), edge)

    p2_modes = {n: at("p2", n) for n in range(2, 6)}
    for n in range(2, 6):
        to_modes(lambda c, n=n: p2[c, n - 2], p2_modes[n])
    sums[...] = jnp.zeros_like(sums)

    def energy(rows, _):
        here = load(p2_modes[2], rows)
        total = jnp.zeros((8, CZ), F32)
        for e in range(2, 5):
            there = load(p2_modes[e + 1], rows)
            strain = strains(here, there)
            t[2, e, rows, :] = inner(strain, weight(e, rows))
            total = total + inner(strain, stresses(strain, g(e, rows)))
            here = there
        sums[5] += total

    each_chunk(energy, False)
    total = [jnp.zeros((8, CZ), F32)] * 5
    for n in range(CX):
        for c in range(3):
            v = [b_ref[c, n]]
            if 1 <= n < 7:
                v.append(p1[c, n - 1, :CY])
            if 2 <= n < 6:
                v.append(p2[c, n - 2, :CY])
            for k, (i, j) in enumerate(((0, 0), (0, 1), (1, 1), (1, 2), (2, 2))):
                if j < len(v):
                    total[k] = total[k] + collapse(v[i] * v[j])
    for k in range(5):
        sums[k] = total[k]


def outer_kernel(
    b_ref, h_ref, halo, x_a, x_b, p1, p2, kept, opened, weights_in, sums_in,
    q1, q2, t, row_out, strain_7, u_edge, above, below, g_ref, modes, gathered, sums,
):
    edge = row_edge()
    odd_x = lax.rem(lax.axis_index("gx"), 2) == 1
    last_x = lax.axis_index("gx") == lax.axis_size("gx") - 1
    past_x = jnp.where(last_x, 0.0, 1.0).astype(F32)

    @pl.when(odd_x)
    def _():
        above[...] = x_b[...]
        below[...] = x_a[...]

    @pl.when(jnp.logical_not(odd_x))
    def _():
        above[...] = x_a[...]
        below[...] = x_b[...]

    for c in range(3):
        u_edge[c] = pltpu.roll(above[3 * c, CY:], 5, 0)
    for k, e in enumerate((0, 1, 5, 6, 7)):
        g_ref[k, :CY] = degradation_of(h_ref[e])
        g_ref[k, CY:] = halo[3, e]

    def g(e, rows):
        if e < 0:
            return below[11 + e, rows, :]
        if e >= CX:
            return above[1 + e, rows, :]
        return g_ref[(0, 1, 5, 6, 7).index(e), rows, :]

    keep = {name: (kept, k) for k, name in enumerate(KEPT)}
    open_at = {name: (opened, k) for k, name in enumerate(OPEN)}
    new = [0]

    def fresh(nodes):
        out = {n: (modes, new[0] + k) for k, n in enumerate(nodes)}
        new[0] += len(nodes)
        return out

    def weight(e, rows):
        return [weights_in[k, KEPT_WEIGHTS.index(e), rows, :] for k in range(18)]

    def visit(power):
        def f(e, strain, rows):
            if e == 7:
                for k in range(18):
                    strain_7[power, k, rows, :] = strain[k]
            elif (power, e) in OUTER_T:
                t[OUTER_T.index((power, e)), rows, :] = inner(strain, weight(e, rows))

        return f

    b_modes = fresh([-2, -1, 8, 9, 10])
    for n in (-2, -1):
        to_modes(lambda c, n=n: below[3 * c + n + 2], b_modes[n])
    for n in (8, 9, 10):
        to_modes(lambda c, n=n: above[3 * c + n - 8], b_modes[n])
    b_modes.update({0: keep["b", 0], 7: keep["b", 7]})
    nodes = (-1, 0, 7, 8, 9)
    put = {n: (gathered, k) for k, n in enumerate(nodes)}
    sweep((-2, -1), b_modes, g, {0: open_at["p1", 0]}, put, visit(0))
    sweep((7, 8, 9), b_modes, g, {7: open_at["p1", 7]}, put, visit(0))
    for k, n in enumerate(nodes):
        finish(put[n], (q1, k), edge, past_x if n >= CX else None)

    p1_modes = fresh(nodes)
    for k, n in enumerate(nodes):
        to_modes(lambda c, k=k: q1[c, k], p1_modes[n])
    p1_modes.update({1: keep["p1", 1], 6: keep["p1", 6]})
    nodes = (0, 1, 6, 7, 8)
    put = {n: (gathered, k) for k, n in enumerate(nodes)}
    sweep((-1, 0), p1_modes, g, {1: open_at["p2", 1]}, put, visit(1))
    sweep((6, 7, 8), p1_modes, g, {6: open_at["p2", 6]}, put, visit(1))
    for k, n in enumerate(nodes):
        finish(put[n], (q2, k), edge, past_x if n >= CX else None)

    p2_modes = fresh(nodes)
    for k, n in enumerate(nodes):
        to_modes(lambda c, k=k: q2[c, k], p2_modes[n])
    p2_modes.update({2: keep["p2", 2], 5: keep["p2", 5]})
    sums[...] = sums_in[...]

    def energy(rows, _):
        total = jnp.zeros((8, CZ), F32)
        for elements in ((0, 1), (5, 6, 7)):
            here = load(p2_modes[elements[0]], rows)
            for e in elements:
                there = load(p2_modes[e + 1], rows)
                strain = strains(here, there)
                visit(2)(e, strain, rows)
                total = total + inner(strain, stresses(strain, g(e, rows)))
                here = there
        sums[5] += total

    each_chunk(energy, False)
    total = [sums[k] for k in range(5)]
    for n in (0, 1, 6, 7):
        for c in range(3):
            v1 = q1[c, (-1, 0, 7).index(n), :CY] if n in (0, 7) else p1[c, n - 1, :CY]
            v = (b_ref[c, n], v1, q2[c, (0, 1, 6, 7).index(n), :CY])
            for k, (i, j) in enumerate(((0, 0), (0, 1), (1, 1), (1, 2), (2, 2))):
                if k >= (1 if n in (0, 7) else 3):
                    total[k] = total[k] + collapse(v[i] * v[j])
    total.append(sums[5])
    lane = iota((1, CZ), 1)
    line = jnp.zeros((1, CZ), F32)
    for k in range(6):
        value = jnp.sum(jnp.sum(total[k], 0, keepdims=True), 1, keepdims=True)
        line = jnp.where(lane == k, value, line)
    row_out[...] = jnp.broadcast_to(line, row_out.shape)


OUTER_T = [(1, 0), (1, 6), (2, 0), (2, 1), (2, 5), (2, 6)]


def combine(
    parts, b_ref, h_ref, p1, p2, q1, q2, t_in, t_out, strain_7, kept, u_next, u_edge, adjoint, sensitivity,
    modes,
):
    u_here, u_there = (kept, KEPT.index(("u", 7))), (modes, 0)
    to_modes(lambda c: jnp.concatenate([u_next[c], u_edge[c]], 0), u_there)
    line = jnp.sum(parts[...], 0, keepdims=True)
    lane = iota((1, CZ), 1)
    m = [jnp.sum(jnp.where(lane == k, line, 0.0), 1, keepdims=True) for k in range(6)]
    l10, l20 = m[2] / m[1], m[3] / m[1]
    d1, h21 = m[3] - l10 * m[2], m[4] - l20 * m[2]
    l21 = h21 / d1
    d2 = m[5] - l20 * m[3] - l21 * h21
    y1 = m[1] - l10 * m[0]
    y2 = m[2] - l20 * m[0] - l21 * y1
    c2 = y2 / d2
    c1 = y1 / d1 - l21 * c2
    c0 = m[0] / m[1] - l10 * c1 - l20 * c2
    weight = [jnp.broadcast_to(c, (CY, CZ)) for c in (c0, c1, c2)]
    for x in range(CX):
        for c in range(3):
            v1 = q1[c, (-1, 0, 7).index(x), :CY] if x in (0, 7) else p1[c, x - 1, :CY]
            v2 = p2[c, x - 2, :CY] if 2 <= x < 6 else q2[c, (0, 1, 6, 7).index(x), :CY]
            adjoint[c, x] = weight[0] * b_ref[c, x] + weight[1] * v1 + weight[2] * v2
        if x == 7:
            continue
        product = None
        for k in range(3):
            part = t_out[OUTER_T.index((k, x))] if (k, x) in OUTER_T else t_in[k, x]
            product = weight[k] * part if product is None else product + weight[k] * part
        sensitivity[x] = 2.0 * (1.0 - h_ref[x]) * product
    for j in range(0, CY, 8):
        rows = pl.ds(j, 8)
        stiff = stresses(strains(load(u_here, rows), load(u_there, rows)), None)
        product = None
        for k in range(3):
            part = weight[k][:8] * inner([strain_7[k, i, rows, :] for i in range(18)], stiff)
            product = part if product is None else product + part
        sensitivity[7, rows, :] = 2.0 * (1.0 - h_ref[7, rows, :]) * product


VMEM = pl.BlockSpec(memory_space=pltpu.VMEM)


def shape(*dims):
    return jax.ShapeDtypeStruct(dims, F32)


def call(kernel, megabytes, inputs, outputs, scratch=(), in_specs=None):
    return pl.pallas_call(
        kernel,
        in_specs=in_specs or [VMEM] * len(inputs),
        out_specs=[VMEM] * len(outputs),
        out_shape=[shape(*dims) for dims in outputs],
        scratch_shapes=[s if not isinstance(s, tuple) else pltpu.VMEM(s, F32) for s in scratch],
        compiler_params=pltpu.CompilerParams(vmem_limit_bytes=megabytes and int(megabytes * 2**20)),
    )(*inputs)


def body(misfit, damage, displacement):
    tile = (CX, 8, CZ)
    y_a, y_b, misfit, damage, displacement, u_first = call(
        pack_y, 4,
        [pltpu.with_memory_space_constraint(x, pltpu.HBM) for x in (misfit, damage, displacement)],
        [
            (2,) + tile, (2,) + tile, (3, CX, CY, CZ), (CX, CY, CZ), (3, CX, CY, CZ), (3, CY, CZ),
        ],
        [pltpu.SemaphoreType.DMA((3,))],
        [pl.BlockSpec(memory_space=pltpu.HBM)] * 3,
    )
    y_b = exchange(y_b, "gy", 1)
    y_a = exchange(y_a, "gy", 0)
    n = lax.axis_size("gx")
    u_next = lax.ppermute(u_first, "gx", [(i, i - 1) for i in range(1, n)])
    x_a, x_b, halo = call(
        pack_x, 6,
        (y_a, y_b, misfit, damage),
        [(11, ROWS, CZ)] * 2 + [(7,) + tile],
    )
    x_b = exchange(x_b, "gx", 1)
    x_a = exchange(x_a, "gx", 0)
    devices = lax.axis_size("gx") * lax.axis_size("gy")
    layer = (ROWS, CZ)
    p1, p2, t_in, kept, opened, weights, sums = call(
        inner_kernel, 20,
        (misfit, damage, displacement, halo),
        [
            (3, 6) + layer, (3, 4) + layer, (3, CX, CY, CZ), (12, len(KEPT)) + layer,
            (12, len(OPEN)) + layer, (18, len(KEPT_WEIGHTS), CY, CZ), (6, 8, CZ),
        ],
        [(12, CX) + layer, (12, CX) + layer, (18, CX, CY, CZ), (CX,) + layer],
    )
    q1, q2, t_out, line, strain_7, u_edge = call(
        outer_kernel, 20,
        (misfit, damage, halo, x_a, x_b, p1, p2, kept, opened, weights, sums),
        [(3, 5) + layer, (3, 5) + layer, (len(OUTER_T), CY, CZ), (devices, CZ), (3, 18, CY, CZ), (3, 8, CZ)],
        [
            (11,) + layer, (11,) + layer, (5,) + layer, (12, 15) + layer, (12, 5) + layer,
            (6, 8, CZ),
        ],
    )
    line, u_next = lax.optimization_barrier((line, u_next))
    parts = lax.all_to_all(line, AXES, 0, 0, tiled=True)
    return call(
        combine, 8,
        (parts, misfit, damage, p1, p2, q1, q2, t_in, t_out, strain_7, kept, u_next, u_edge),
        [(3, CX, CY, CZ), (CX, CY, CZ)],
        [(12, 1, ROWS, CZ)],
    )


def solution(mesh):
    field, scalar = P(None, "gx", "gy", None), P("gx", "gy", None)
    return jax.shard_map(
        body, mesh=mesh, in_specs=(field, scalar, field), out_specs=(field, scalar), check_vma=False
    )
```

```python
import jax
import jax.numpy as jnp
from jax import lax
from jax.experimental import pallas as pl
from jax.experimental.pallas import tpu as pltpu
from jax.sharding import PartitionSpec as P


CX, CY, CZ = 8, 32, 128
ROWS = 40
AXES = ("gx", "gy")
LAM = 3.0 * 0.3 / (1.3 * 0.4)
MU = 3.0 / 2.6
F32 = jnp.float32


def exchange(x, axis, first):
    n = lax.axis_size(axis)
    pairs = []
    for i in range(first, n - 1, 2):
        pairs += [(i, i + 1), (i + 1, i)]
    return lax.ppermute(x, axis, pairs)


def iota(shape, dim):
    return lax.broadcasted_iota(jnp.int32, shape, dim)


def degradation_of(damage):
    return (1.0 - damage) * (1.0 - damage) + 0.001


def pack_y(b, h, u, out_a, out_b, b_all, h_all, u_all, u_first, done):
    copies = []
    for k, (source, target) in enumerate(((h, h_all), (b, b_all), (u, u_all))):
        copies.append(pltpu.make_async_copy(source, target, done.at[k]))
        copies[-1].start()
    for copy in copies:
        copy.wait()
    u_first[...] = u_all[:, 0]
    b_lo, b_hi = b_all[:, :, :8], b_all[:, :, CY - 8 :]
    h_lo, h_hi = h_all[:, :8], h_all[:, CY - 8 :]
    u_lo = u_all[:, :, :8]
    row = iota((CX, 8, CZ), 1)
    g_lo, g_hi = degradation_of(h_lo), degradation_of(h_hi)
    up = lambda x, k: pltpu.roll(x, k % 8, 1)
    low_1 = jnp.where(row < 3, b_lo[0], jnp.where(row < 6, up(b_lo[1], 3), up(g_lo, 6)))
    low_2 = jnp.where(
        row < 3,
        b_lo[2],
        jnp.where(
            row == 3, up(u_lo[0], 3), jnp.where(row == 4, up(u_lo[1], 4), up(u_lo[2], 5))
        ),
    )
    high = jnp.where(
        row < 2,
        up(b_hi[0], 2),
        jnp.where(row < 4, up(b_hi[1], 4), jnp.where(row < 6, up(b_hi[2], 6), g_hi)),
    )
    odd = lax.rem(lax.axis_index("gy"), 2) == 1

    @pl.when(odd)
    def _():
        out_a[0], out_a[1] = low_1, low_2
        out_b[0], out_b[1] = high, high

    @pl.when(jnp.logical_not(odd))
    def _():
        out_a[0], out_a[1] = high, high
        out_b[0], out_b[1] = low_1, low_2


def pack_x(y_a, y_b, b_ref, h_ref, out_a, out_b, halo):
    odd_y = lax.rem(lax.axis_index("gy"), 2) == 1
    row = iota((CX, 8, CZ), 1)
    up = lambda x, k: pltpu.roll(x, k % 8, 1)
    above_1 = jnp.where(odd_y, y_b[0], y_a[0])
    above_2 = jnp.where(odd_y, y_b[1], y_a[1])
    below = jnp.where(odd_y, y_a[0], y_b[0])

    def tile(head, count, tail):
        return jnp.where(row < count, head, jnp.where(row >= 6, tail, 0.0))

    halo[0] = tile(above_1, 3, up(below, 6))
    halo[1] = tile(up(above_1, -3), 3, up(below, 4))
    halo[2] = tile(above_2, 3, up(below, 2))
    halo[3] = tile(up(above_1, -6), 2, below)
    for c in range(3):
        halo[4 + c] = jnp.where(row < 1, up(above_2, -3 - c), 0.0)
    odd_x = lax.rem(lax.axis_index("gx"), 2) == 1

    def low(out):
        for c in range(3):
            for x in range(3):
                edge = halo[c, x]
                if x == 0:
                    edge = jnp.where(row[0] == 3, pltpu.roll(halo[4 + c, 0], 3, 0), edge)
                out[3 * c + x, :CY], out[3 * c + x, CY:] = b_ref[c, x], edge
        for x in range(2):
            out[9 + x, :CY], out[9 + x, CY:] = degradation_of(h_ref[x]), halo[3, x]

    def high(out):
        for c in range(3):
            for x in range(2):
                out[3 * c + x, :CY], out[3 * c + x, CY:] = b_ref[c, 6 + x], halo[c, 6 + x]
            out[3 * c + 2] = jnp.zeros((ROWS, CZ), F32)
        for x in range(2):
            out[9 + x, :CY], out[9 + x, CY:] = degradation_of(h_ref[6 + x]), halo[3, 6 + x]

    @pl.when(odd_x)
    def _():
        low(out_a)
        high(out_b)

    @pl.when(jnp.logical_not(odd_x))
    def _():
        high(out_a)
        low(out_b)


def yz_modes(u):
    lane = iota((ROWS, CZ), 1)
    u_next = jnp.where(lane == CZ - 1, 0.0, pltpu.roll(u, CZ - 1, 1))
    out = [None] * 4
    for z, a in enumerate((u + u_next, u_next - u)):
        a_next = pltpu.roll(a, ROWS - 1, 0)
        out[z], out[2 + z] = a + a_next, a_next - a
    return out


def yz_gather(r):
    lane = iota((ROWS, CZ), 1)
    rows = []
    for z in range(2):
        s, d = r[z], r[2 + z]
        rows.append((s - d) + pltpu.roll(s + d, 1, 0))
    s, d = rows
    return (s - d) + jnp.where(lane == 0, 0.0, pltpu.roll(s + d, 1, 1))


SS, SD, DS, DD = 0, 1, 2, 3


def strains(here, there):
    s = [[here[4 * c + k] + there[4 * c + k] if k else None for k in range(4)] for c in range(3)]
    d = [[there[4 * c + k] - here[4 * c + k] for k in range(4)] for c in range(3)]
    u, v, w = range(3)
    return [
        d[u][SS], s[v][DS], s[w][SD],
        s[u][DS] + d[v][SS], s[u][SD] + d[w][SS], s[v][SD] + s[w][DS],
        s[u][DD], d[v][SD], d[w][DS],
        d[u][SD], s[v][DD], d[u][DS], s[w][DD], d[v][DS], d[w][SD],
        d[u][DD], d[v][DD], d[w][DD],
    ]


def stresses(e, g):
    scaled = (lambda k: g * k) if g is not None else (lambda k: k)
    l16, m8, m16, m48 = scaled(LAM / 16), scaled(MU / 8), scaled(MU / 16), scaled(MU / 48)
    l48, q = scaled(LAM / 48), scaled((LAM + 4 * MU) / 144)
    trace = l16 * (e[0] + e[1] + e[2])
    out = [trace + m8 * e[k] for k in range(3)]
    out += [m16 * e[k] for k in range(3, 6)]
    three = e[6] + e[7] + e[8]
    out += [m48 * (e[k] + three) for k in range(6, 9)]
    for k in (9, 11, 13):
        both = l48 * (e[k] + e[k + 1])
        out += [both + m16 * e[k], both + m16 * e[k + 1]]
    return out + [q * e[k] for k in range(15, 18)]


def x_forces(f):
    s = [[None, f[4], f[3], f[6]], [None, f[5], f[1], f[10]], [None, f[2], f[5], f[12]]]
    d = [[f[0], f[9], f[11], f[15]], [f[3], f[7], f[13], f[16]], [f[4], f[14], f[8], f[17]]]
    return [x for c in s for x in c], [x for c in d for x in c]


def inner(a, b):
    total = a[0] * b[0]
    for x, y in zip(a[1:], b[1:]):
        total = total + x * y
    return total


def load(place, rows):
    ref, slot = place
    return [ref[k, slot, rows, :] for k in range(12)]


def to_modes(node, place):
    ref, slot = place
    for c in range(3):
        for k, a in enumerate(yz_modes(node(c))):
            ref[4 * c + k, slot] = a


def each_chunk(step, halo_too):
    @pl.loop(0, CY // 8)
    def _(j):
        step(pl.ds(pl.multiple_of(8 * j, 8), 8))

    if halo_too:
        step(pl.ds(CY, 8))


def sweep(elements, modes, g, add, put):
    def step(rows):
        here = load(modes[elements[0]], rows)
        before = None

        def store(n, lower):
            if n not in put:
                return
            total = before
            if lower is not None:
                total = lower if total is None else [p + q for p, q in zip(total, lower)]
            if n in add:
                total = [p + q for p, q in zip(total, load(add[n], rows))]
            ref, slot = put[n]
            for k in range(12):
                ref[k, slot, rows, :] = total[k]

        for e in elements:
            there = load(modes[e + 1], rows)
            s, d = x_forces(stresses(strains(here, there), g(e, rows)))
            if e in put:
                store(e, [p - q if p is not None else -q for p, q in zip(s, d)])
            before = [p + q if p is not None else q for p, q in zip(s, d)]
            here = there
        store(elements[-1] + 1, None)

    each_chunk(step, True)


def finish(gathered, target, edge, factor=None):
    ref, slot = gathered
    out, at = target
    for c in range(3):
        v = yz_gather([ref[4 * c + k, slot] for k in range(4)])
        if factor is not None:
            v = v * factor
        out[c, at, :CY] = v[:CY]
        out[c, at, CY:] = v[CY:] * edge


def collapse(x):
    return x[0:8] + x[8:16] + x[16:24] + x[24:32]


def row_edge():
    row = iota((8, CZ), 0)
    last = lax.axis_index("gy") == lax.axis_size("gy") - 1
    return jnp.where(row < 3, jnp.where(last, 0.0, 1.0).astype(F32), 1.0)


KEPT = ("b", 0), ("b", 7), ("p1", 1), ("p1", 6), ("p2", 2), ("p2", 5)
OPEN = ("p1", 0), ("p1", 7), ("p2", 1), ("p2", 6)


def add_energy(total, elements, modes, g, rows):
    here = load(modes[elements[0]], rows)
    for e in elements:
        there = load(modes[e + 1], rows)
        strain = strains(here, there)
        total = total + inner(strain, stresses(strain, g(e, rows)))
        here = there
    return total


def inner_kernel(b_ref, h_ref, halo, p1, p2, kept, opened, sums, modes, gathered, g_ref):
    edge = row_edge()
    g_ref[:, :CY] = degradation_of(h_ref[...])
    g_ref[:, CY:] = halo[3]
    g = lambda e, rows: g_ref[e, rows, :]
    keep = {name: (kept, k) for k, name in enumerate(KEPT)}
    open_at = {name: (opened, k) for k, name in enumerate(OPEN)}
    at = lambda name, n: keep.get((name, n), (modes, n))

    b_modes = {n: at("b", n) for n in range(CX)}
    for n in range(CX):
        to_modes(lambda c, n=n: jnp.concatenate([b_ref[c, n], halo[c, n]], 0), b_modes[n])
    put = {n: (gathered, n) for n in range(1, 7)}
    put.update({0: open_at["p1", 0], 7: open_at["p1", 7]})
    sweep(range(0, 7), b_modes, g, {}, put)
    for n in range(1, 7):
        finish(put[n], (p1, n - 1), edge)

    p1_modes = {n: at("p1", n) for n in range(1, 7)}
    for n in range(1, 7):
        to_modes(lambda c, n=n: p1[c, n - 1], p1_modes[n])
    put = {n: (gathered, n) for n in range(2, 6)}
    put.update({1: open_at["p2", 1], 6: open_at["p2", 6]})
    sweep(range(1, 6), p1_modes, g, {}, put)
    for n in range(2, 6):
        finish(put[n], (p2, n - 2), edge)

    p2_modes = {n: at("p2", n) for n in range(2, 6)}
    for n in range(2, 6):
        to_modes(lambda c, n=n: p2[c, n - 2], p2_modes[n])
    sums[...] = jnp.zeros_like(sums)

    def energy(rows):
        sums[5] += add_energy(jnp.zeros((8, CZ), F32), range(2, 5), p2_modes, g, rows)

    each_chunk(energy, False)
    total = [jnp.zeros((8, CZ), F32)] * 5
    for n in range(CX):
        for c in range(3):
            v = [b_ref[c, n]]
            if 1 <= n < 7:
                v.append(p1[c, n - 1, :CY])
            if 2 <= n < 6:
                v.append(p2[c, n - 2, :CY])
            for k, (i, j) in enumerate(((0, 0), (0, 1), (1, 1), (1, 2), (2, 2))):
                if j < len(v):
                    total[k] = total[k] + collapse(v[i] * v[j])
    for k in range(5):
        sums[k] = total[k]


def outer_kernel(
    b_ref, h_ref, halo, x_a, x_b, p1, p2, kept, opened, sums_in,
    q1, q2, row_out, b_next, u_edge, above, below, g_ref, modes, gathered, sums,
):
    edge = row_edge()
    odd_x = lax.rem(lax.axis_index("gx"), 2) == 1
    last_x = lax.axis_index("gx") == lax.axis_size("gx") - 1
    past_x = jnp.where(last_x, 0.0, 1.0).astype(F32)

    @pl.when(odd_x)
    def _():
        above[...] = x_b[...]
        below[...] = x_a[...]

    @pl.when(jnp.logical_not(odd_x))
    def _():
        above[...] = x_a[...]
        below[...] = x_b[...]

    for c in range(3):
        u_edge[c] = pltpu.roll(above[3 * c, CY:], 5, 0)
        b_next[c] = above[3 * c]
    for k, e in enumerate((0, 1, 5, 6, 7)):
        g_ref[k, :CY] = degradation_of(h_ref[e])
        g_ref[k, CY:] = halo[3, e]

    def g(e, rows):
        if e < 0:
            return below[11 + e, rows, :]
        if e >= CX:
            return above[1 + e, rows, :]
        return g_ref[(0, 1, 5, 6, 7).index(e), rows, :]

    keep = {name: (kept, k) for k, name in enumerate(KEPT)}
    open_at = {name: (opened, k) for k, name in enumerate(OPEN)}
    new = [0]

    def fresh(nodes):
        out = {n: (modes, new[0] + k) for k, n in enumerate(nodes)}
        new[0] += len(nodes)
        return out

    b_modes = fresh([-2, -1, 8, 9, 10])
    for n in (-2, -1):
        to_modes(lambda c, n=n: below[3 * c + n + 2], b_modes[n])
    for n in (8, 9, 10):
        to_modes(lambda c, n=n: above[3 * c + n - 8], b_modes[n])
    b_modes.update({0: keep["b", 0], 7: keep["b", 7]})
    nodes = (-1, 0, 7, 8, 9)
    put = {n: (gathered, k) for k, n in enumerate(nodes)}
    sweep((-2, -1), b_modes, g, {0: open_at["p1", 0]}, put)
    sweep((7, 8, 9), b_modes, g, {7: open_at["p1", 7]}, put)
    for k, n in enumerate(nodes):
        finish(put[n], (q1, k), edge, past_x if n >= CX else None)

    p1_modes = fresh(nodes)
    for k, n in enumerate(nodes):
        to_modes(lambda c, k=k: q1[c, k], p1_modes[n])
    p1_modes.update({1: keep["p1", 1], 6: keep["p1", 6]})
    nodes = (0, 1, 6, 7, 8)
    put = {n: (gathered, k) for k, n in enumerate(nodes)}
    sweep((-1, 0), p1_modes, g, {1: open_at["p2", 1]}, put)
    sweep((6, 7, 8), p1_modes, g, {6: open_at["p2", 6]}, put)
    for k, n in enumerate(nodes):
        finish(put[n], (q2, k), edge, past_x if n >= CX else None)

    p2_modes = fresh(nodes)
    for k, n in enumerate(nodes):
        to_modes(lambda c, k=k: q2[c, k], p2_modes[n])
    p2_modes.update({2: keep["p2", 2], 5: keep["p2", 5]})
    sums[...] = sums_in[...]

    def energy(rows):
        total = jnp.zeros((8, CZ), F32)
        for elements in ((0, 1), (5, 6, 7)):
            total = add_energy(total, elements, p2_modes, g, rows)
        sums[5] += total

    each_chunk(energy, False)
    total = [sums[k] for k in range(5)]
    for n in (0, 1, 6, 7):
        for c in range(3):
            v1 = q1[c, (-1, 0, 7).index(n), :CY] if n in (0, 7) else p1[c, n - 1, :CY]
            v = (b_ref[c, n], v1, q2[c, (0, 1, 6, 7).index(n), :CY])
            for k, (i, j) in enumerate(((0, 0), (0, 1), (1, 1), (1, 2), (2, 2))):
                if k >= (1 if n in (0, 7) else 3):
                    total[k] = total[k] + collapse(v[i] * v[j])
    total.append(sums[5])
    lane = iota((1, CZ), 1)
    line = jnp.zeros((1, CZ), F32)
    for k in range(6):
        value = jnp.sum(jnp.sum(total[k], 0, keepdims=True), 1, keepdims=True)
        line = jnp.where(lane == k, value, line)
    row_out[...] = jnp.broadcast_to(line, row_out.shape)


def products(
    b_ref, u_ref, halo, b_next, u_next, u_edge, p1, p2, q1, q2, t, b_modes, p1_modes, p2_modes, u_modes,
):
    for n in range(CX + 1):
        if n < CX:
            to_modes(lambda c: jnp.concatenate([b_ref[c, n], halo[c, n]], 0), (b_modes, n))
            to_modes(lambda c: jnp.concatenate([u_ref[c, n], halo[4 + c, n]], 0), (u_modes, n))
        else:
            to_modes(lambda c: b_next[c], (b_modes, n))
            to_modes(lambda c: jnp.concatenate([u_next[c], u_edge[c]], 0), (u_modes, n))
        to_modes(lambda c: q1[c, Q1.index(n)] if n in Q1 else p1[c, n - 1], (p1_modes, n))
        to_modes(lambda c: q2[c, Q2.index(n)] if n in Q2 else p2[c, n - 2], (p2_modes, n))
    fields = (b_modes, p1_modes, p2_modes)

    def step(rows):
        for e in range(CX):
            stiff = stresses(strains(load((u_modes, e), rows), load((u_modes, e + 1), rows)), None)
            for k, m in enumerate(fields):
                strain = strains(load((m, e), rows), load((m, e + 1), rows))
                t[k, e, rows, :] = inner(strain, stiff)

    each_chunk(step, False)


Q1, Q2 = (-1, 0, 7, 8, 9), (0, 1, 6, 7, 8)


def combine(parts, b_ref, h_ref, p1, p2, q1, q2, t, adjoint, sensitivity):
    line = jnp.sum(parts[...], 0, keepdims=True)
    lane = iota((1, CZ), 1)
    m = [jnp.sum(jnp.where(lane == k, line, 0.0), 1, keepdims=True) for k in range(6)]
    l10, l20 = m[2] / m[1], m[3] / m[1]
    d1, h21 = m[3] - l10 * m[2], m[4] - l20 * m[2]
    l21 = h21 / d1
    d2 = m[5] - l20 * m[3] - l21 * h21
    y1 = m[1] - l10 * m[0]
    y2 = m[2] - l20 * m[0] - l21 * y1
    c2 = y2 / d2
    c1 = y1 / d1 - l21 * c2
    c0 = m[0] / m[1] - l10 * c1 - l20 * c2
    weight = [jnp.broadcast_to(c, (CY, CZ)) for c in (c0, c1, c2)]
    for x in range(CX):
        for c in range(3):
            v1 = q1[c, Q1.index(x), :CY] if x in Q1 else p1[c, x - 1, :CY]
            v2 = q2[c, Q2.index(x), :CY] if x in Q2 else p2[c, x - 2, :CY]
            adjoint[c, x] = weight[0] * b_ref[c, x] + weight[1] * v1 + weight[2] * v2
        product = weight[0] * t[0, x] + weight[1] * t[1, x] + weight[2] * t[2, x]
        sensitivity[x] = 2.0 * (1.0 - h_ref[x]) * product


VMEM = pl.BlockSpec(memory_space=pltpu.VMEM)


def shape(*dims):
    return jax.ShapeDtypeStruct(dims, F32)


def call(kernel, megabytes, inputs, outputs, scratch=(), in_specs=None):
    return pl.pallas_call(
        kernel,
        in_specs=in_specs or [VMEM] * len(inputs),
        out_specs=[VMEM] * len(outputs),
        out_shape=[shape(*dims) for dims in outputs],
        scratch_shapes=[s if not isinstance(s, tuple) else pltpu.VMEM(s, F32) for s in scratch],
        compiler_params=pltpu.CompilerParams(vmem_limit_bytes=megabytes and int(megabytes * 2**20)),
    )(*inputs)


def body(misfit, damage, displacement):
    tile = (CX, 8, CZ)
    y_a, y_b, misfit, damage, displacement, u_first = call(
        pack_y, 4,
        [pltpu.with_memory_space_constraint(x, pltpu.HBM) for x in (misfit, damage, displacement)],
        [
            (2,) + tile, (2,) + tile, (3, CX, CY, CZ), (CX, CY, CZ), (3, CX, CY, CZ), (3, CY, CZ),
        ],
        [pltpu.SemaphoreType.DMA((3,))],
        [pl.BlockSpec(memory_space=pltpu.HBM)] * 3,
    )
    y_b = exchange(y_b, "gy", 1)
    y_a = exchange(y_a, "gy", 0)
    x_a, x_b, halo = call(
        pack_x, 6,
        (y_a, y_b, misfit, damage),
        [(11, ROWS, CZ)] * 2 + [(7,) + tile],
    )
    x_b = exchange(x_b, "gx", 1)
    x_a = exchange(x_a, "gx", 0)
    devices = lax.axis_size("gx") * lax.axis_size("gy")
    layer = (ROWS, CZ)
    p1, p2, kept, opened, sums = call(
        inner_kernel, 20,
        (misfit, damage, halo),
        [
            (3, 6) + layer, (3, 4) + layer, (12, len(KEPT)) + layer, (12, len(OPEN)) + layer,
            (6, 8, CZ),
        ],
        [(12, CX) + layer, (12, CX) + layer, (CX,) + layer],
    )
    q1, q2, line, b_next, u_edge = call(
        outer_kernel, 20,
        (misfit, damage, halo, x_a, x_b, p1, p2, kept, opened, sums),
        [(3, 5) + layer, (3, 5) + layer, (devices, CZ), (3,) + layer, (3, 8, CZ)],
        [
            (11,) + layer, (11,) + layer, (5,) + layer, (12, 15) + layer, (12, 5) + layer,
            (6, 8, CZ),
        ],
    )
    parts = lax.all_to_all(line, AXES, 0, 0, tiled=True)
    n = lax.axis_size("gx")
    u_next = lax.ppermute(u_first, "gx", [(i, i - 1) for i in range(1, n)])
    (t,) = call(
        products, 20,
        (misfit, displacement, halo, b_next, u_next, u_edge, p1, p2, q1, q2),
        [(3, CX, CY, CZ)],
        [(12, CX + 1) + layer] * 4,
    )
    return call(
        combine, 8,
        (parts, misfit, damage, p1, p2, q1, q2, t),
        [(3, CX, CY, CZ), (CX, CY, CZ)],
    )


def solution(mesh):
    field, scalar = P(None, "gx", "gy", None), P("gx", "gy", None)
    return jax.shard_map(
        body, mesh=mesh, in_specs=(field, scalar, field), out_specs=(field, scalar), check_vma=False
    )
```

```python
import jax
import jax.numpy as jnp
from jax import lax
from jax.experimental import pallas as pl
from jax.experimental.pallas import tpu as pltpu
from jax.sharding import PartitionSpec as P


CX, CY, CZ = 8, 32, 128
ROWS = 40
AXES = ("gx", "gy")
LAM = 3.0 * 0.3 / (1.3 * 0.4)
MU = 3.0 / 2.6
F32 = jnp.float32


def exchange(x, axis, first):
    n = lax.axis_size(axis)
    pairs = []
    for i in range(first, n - 1, 2):
        pairs += [(i, i + 1), (i + 1, i)]
    return lax.ppermute(x, axis, pairs)


def iota(shape, dim):
    return lax.broadcasted_iota(jnp.int32, shape, dim)


def degradation_of(damage):
    return (1.0 - damage) * (1.0 - damage) + 0.001


def pack_y(b, h, u, out_a, out_b, b_all, h_all, u_all, done):
    copies = []
    for k, (source, target) in enumerate(((h, h_all), (b, b_all), (u, u_all))):
        copies.append(pltpu.make_async_copy(source, target, done.at[k]))
        copies[-1].start()
    for copy in copies:
        copy.wait()
    b_lo, b_hi = b_all[:, :, :8], b_all[:, :, CY - 8 :]
    h_lo, h_hi = h_all[:, :8], h_all[:, CY - 8 :]
    u_lo = u_all[:, :, :8]
    row = iota((CX, 8, CZ), 1)
    g_lo, g_hi = degradation_of(h_lo), degradation_of(h_hi)
    up = lambda x, k: pltpu.roll(x, k % 8, 1)
    low_1 = jnp.where(row < 3, b_lo[0], jnp.where(row < 6, up(b_lo[1], 3), up(g_lo, 6)))
    low_2 = jnp.where(
        row < 3,
        b_lo[2],
        jnp.where(
            row == 3, up(u_lo[0], 3), jnp.where(row == 4, up(u_lo[1], 4), up(u_lo[2], 5))
        ),
    )
    high = jnp.where(
        row < 2,
        up(b_hi[0], 2),
        jnp.where(row < 4, up(b_hi[1], 4), jnp.where(row < 6, up(b_hi[2], 6), g_hi)),
    )
    odd = lax.rem(lax.axis_index("gy"), 2) == 1

    @pl.when(odd)
    def _():
        out_a[0], out_a[1] = low_1, low_2
        out_b[0], out_b[1] = high, high

    @pl.when(jnp.logical_not(odd))
    def _():
        out_a[0], out_a[1] = high, high
        out_b[0], out_b[1] = low_1, low_2


def pack_x(y_a, y_b, b_ref, h_ref, u_ref, out_a, out_b, halo):
    odd_y = lax.rem(lax.axis_index("gy"), 2) == 1
    row = iota((CX, 8, CZ), 1)
    up = lambda x, k: pltpu.roll(x, k % 8, 1)
    above_1 = jnp.where(odd_y, y_b[0], y_a[0])
    above_2 = jnp.where(odd_y, y_b[1], y_a[1])
    below = jnp.where(odd_y, y_a[0], y_b[0])

    def tile(head, count, tail):
        return jnp.where(row < count, head, jnp.where(row >= 6, tail, 0.0))

    halo[0] = tile(above_1, 3, up(below, 6))
    halo[1] = tile(up(above_1, -3), 3, up(below, 4))
    halo[2] = tile(above_2, 3, up(below, 2))
    halo[3] = tile(up(above_1, -6), 2, below)
    for c in range(3):
        halo[4 + c] = jnp.where(row < 1, up(above_2, -3 - c), 0.0)
    odd_x = lax.rem(lax.axis_index("gx"), 2) == 1

    def put(out, plane, own, edge):
        out[plane * ROWS : plane * ROWS + CY] = own
        out[plane * ROWS + CY : (plane + 1) * ROWS] = edge

    def low(out):
        for c in range(3):
            for x in range(3):
                edge = halo[c, x]
                if x == 0:
                    edge = jnp.where(row[0] == 3, pltpu.roll(halo[4 + c, 0], 3, 0), edge)
                put(out, 3 * c + x, b_ref[c, x], edge)
            out[11 * ROWS + c * CY : 11 * ROWS + (c + 1) * CY] = u_ref[c, 0]
        for x in range(2):
            put(out, 9 + x, degradation_of(h_ref[x]), halo[3, x])

    def high(out):
        for c in range(3):
            for x in range(2):
                put(out, 3 * c + x, b_ref[c, 6 + x], halo[c, 6 + x])
            out[(3 * c + 2) * ROWS : (3 * c + 3) * ROWS] = jnp.zeros((ROWS, CZ), F32)
            out[11 * ROWS + c * CY : 11 * ROWS + (c + 1) * CY] = jnp.zeros((CY, CZ), F32)
        for x in range(2):
            put(out, 9 + x, degradation_of(h_ref[6 + x]), halo[3, 6 + x])

    @pl.when(odd_x)
    def _():
        low(out_a)
        high(out_b)

    @pl.when(jnp.logical_not(odd_x))
    def _():
        high(out_a)
        low(out_b)


def yz_modes(u):
    lane = iota((ROWS, CZ), 1)
    u_next = jnp.where(lane == CZ - 1, 0.0, pltpu.roll(u, CZ - 1, 1))
    out = [None] * 4
    for z, a in enumerate((u + u_next, u_next - u)):
        a_next = pltpu.roll(a, ROWS - 1, 0)
        out[z], out[2 + z] = a + a_next, a_next - a
    return out


def yz_gather(r):
    lane = iota((ROWS, CZ), 1)
    rows = []
    for z in range(2):
        s, d = r[z], r[2 + z]
        rows.append((s - d) + pltpu.roll(s + d, 1, 0))
    s, d = rows
    return (s - d) + jnp.where(lane == 0, 0.0, pltpu.roll(s + d, 1, 1))


SS, SD, DS, DD = 0, 1, 2, 3


def strains(here, there):
    s = [[here[4 * c + k] + there[4 * c + k] if k else None for k in range(4)] for c in range(3)]
    d = [[there[4 * c + k] - here[4 * c + k] for k in range(4)] for c in range(3)]
    u, v, w = range(3)
    return [
        d[u][SS], s[v][DS], s[w][SD],
        s[u][DS] + d[v][SS], s[u][SD] + d[w][SS], s[v][SD] + s[w][DS],
        s[u][DD], d[v][SD], d[w][DS],
        d[u][SD], s[v][DD], d[u][DS], s[w][DD], d[v][DS], d[w][SD],
        d[u][DD], d[v][DD], d[w][DD],
    ]


def stresses(e, g):
    scaled = (lambda k: g * k) if g is not None else (lambda k: k)
    l16, m8, m16, m48 = scaled(LAM / 16), scaled(MU / 8), scaled(MU / 16), scaled(MU / 48)
    l48, q = scaled(LAM / 48), scaled((LAM + 4 * MU) / 144)
    trace = l16 * (e[0] + e[1] + e[2])
    out = [trace + m8 * e[k] for k in range(3)]
    out += [m16 * e[k] for k in range(3, 6)]
    three = e[6] + e[7] + e[8]
    out += [m48 * (e[k] + three) for k in range(6, 9)]
    for k in (9, 11, 13):
        both = l48 * (e[k] + e[k + 1])
        out += [both + m16 * e[k], both + m16 * e[k + 1]]
    return out + [q * e[k] for k in range(15, 18)]


def x_forces(f):
    s = [[None, f[4], f[3], f[6]], [None, f[5], f[1], f[10]], [None, f[2], f[5], f[12]]]
    d = [[f[0], f[9], f[11], f[15]], [f[3], f[7], f[13], f[16]], [f[4], f[14], f[8], f[17]]]
    return [x for c in s for x in c], [x for c in d for x in c]


def inner(a, b):
    total = a[0] * b[0]
    for x, y in zip(a[1:], b[1:]):
        total = total + x * y
    return total


def load(place, rows):
    ref, slot = place
    return [ref[k, slot, rows, :] for k in range(12)]


def to_modes(node, place):
    ref, slot = place
    for c in range(3):
        for k, a in enumerate(yz_modes(node(c))):
            ref[4 * c + k, slot] = a


def each_chunk(step, halo_too):
    @pl.loop(0, CY // 8)
    def _(j):
        step(pl.ds(pl.multiple_of(8 * j, 8), 8))

    if halo_too:
        step(pl.ds(CY, 8))


def sweep(elements, modes, g, add, put):
    def step(rows):
        here = load(modes[elements[0]], rows)
        before = None

        def store(n, lower):
            if n not in put:
                return
            total = before
            if lower is not None:
                total = lower if total is None else [p + q for p, q in zip(total, lower)]
            if n in add:
                total = [p + q for p, q in zip(total, load(add[n], rows))]
            ref, slot = put[n]
            for k in range(12):
                ref[k, slot, rows, :] = total[k]

        for e in elements:
            there = load(modes[e + 1], rows)
            s, d = x_forces(stresses(strains(here, there), g(e, rows)))
            if e in put:
                store(e, [p - q if p is not None else -q for p, q in zip(s, d)])
            before = [p + q if p is not None else q for p, q in zip(s, d)]
            here = there
        store(elements[-1] + 1, None)

    each_chunk(step, True)


def finish(gathered, target, edge, factor=None):
    ref, slot = gathered
    out, at = target
    for c in range(3):
        v = yz_gather([ref[4 * c + k, slot] for k in range(4)])
        if factor is not None:
            v = v * factor
        out[c, at, :CY] = v[:CY]
        out[c, at, CY:] = v[CY:] * edge


def collapse(x):
    return x[0:8] + x[8:16] + x[16:24] + x[24:32]


def row_edge():
    row = iota((8, CZ), 0)
    last = lax.axis_index("gy") == lax.axis_size("gy") - 1
    return jnp.where(row < 3, jnp.where(last, 0.0, 1.0).astype(F32), 1.0)


KEPT = ("b", 0), ("b", 7), ("p1", 1), ("p1", 6), ("p2", 2), ("p2", 5)
OPEN = ("p1", 0), ("p1", 7), ("p2", 1), ("p2", 6)


def add_energy(total, elements, modes, g, rows):
    here = load(modes[elements[0]], rows)
    for e in elements:
        there = load(modes[e + 1], rows)
        strain = strains(here, there)
        total = total + inner(strain, stresses(strain, g(e, rows)))
        here = there
    return total


def inner_kernel(b_ref, h_ref, halo, p1, p2, kept, opened, sums, modes, gathered, g_ref):
    edge = row_edge()
    g_ref[:, :CY] = degradation_of(h_ref[...])
    g_ref[:, CY:] = halo[3]
    g = lambda e, rows: g_ref[e, rows, :]
    keep = {name: (kept, k) for k, name in enumerate(KEPT)}
    open_at = {name: (opened, k) for k, name in enumerate(OPEN)}
    at = lambda name, n: keep.get((name, n), (modes, n))

    b_modes = {n: at("b", n) for n in range(CX)}
    for n in range(CX):
        to_modes(lambda c, n=n: jnp.concatenate([b_ref[c, n], halo[c, n]], 0), b_modes[n])
    put = {n: (gathered, n) for n in range(1, 7)}
    put.update({0: open_at["p1", 0], 7: open_at["p1", 7]})
    sweep(range(0, 7), b_modes, g, {}, put)
    for n in range(1, 7):
        finish(put[n], (p1, n - 1), edge)

    p1_modes = {n: at("p1", n) for n in range(1, 7)}
    for n in range(1, 7):
        to_modes(lambda c, n=n: p1[c, n - 1], p1_modes[n])
    put = {n: (gathered, n) for n in range(2, 6)}
    put.update({1: open_at["p2", 1], 6: open_at["p2", 6]})
    sweep(range(1, 6), p1_modes, g, {}, put)
    for n in range(2, 6):
        finish(put[n], (p2, n - 2), edge)

    p2_modes = {n: at("p2", n) for n in range(2, 6)}
    for n in range(2, 6):
        to_modes(lambda c, n=n: p2[c, n - 2], p2_modes[n])
    sums[...] = jnp.zeros_like(sums)

    def energy(rows):
        sums[5] += add_energy(jnp.zeros((8, CZ), F32), range(2, 5), p2_modes, g, rows)

    each_chunk(energy, False)
    total = [jnp.zeros((8, CZ), F32)] * 5
    for n in range(CX):
        for c in range(3):
            v = [b_ref[c, n]]
            if 1 <= n < 7:
                v.append(p1[c, n - 1, :CY])
            if 2 <= n < 6:
                v.append(p2[c, n - 2, :CY])
            for k, (i, j) in enumerate(((0, 0), (0, 1), (1, 1), (1, 2), (2, 2))):
                if j < len(v):
                    total[k] = total[k] + collapse(v[i] * v[j])
    for k in range(5):
        sums[k] = total[k]


def outer_kernel(
    b_ref, h_ref, halo, x_a, x_b, p1, p2, kept, opened, sums_in,
    q1, q2, row_out, b_next, u_next, above, below, g_ref, modes, gathered, sums,
):
    edge = row_edge()
    odd_x = lax.rem(lax.axis_index("gx"), 2) == 1
    last_x = lax.axis_index("gx") == lax.axis_size("gx") - 1
    past_x = jnp.where(last_x, 0.0, 1.0).astype(F32)

    def split(x_above, x_below):
        for k in range(11):
            above[k] = x_above[k * ROWS : (k + 1) * ROWS]
            below[k] = x_below[k * ROWS : (k + 1) * ROWS]
        for c in range(3):
            u_next[c, :CY] = x_above[11 * ROWS + c * CY : 11 * ROWS + (c + 1) * CY]
            u_next[c, CY:] = pltpu.roll(x_above[3 * c * ROWS + CY : (3 * c + 1) * ROWS], 5, 0)
            b_next[c] = x_above[3 * c * ROWS : (3 * c + 1) * ROWS]

    @pl.when(odd_x)
    def _():
        split(x_b, x_a)

    @pl.when(jnp.logical_not(odd_x))
    def _():
        split(x_a, x_b)

    for k, e in enumerate((0, 1, 5, 6, 7)):
        g_ref[k, :CY] = degradation_of(h_ref[e])
        g_ref[k, CY:] = halo[3, e]

    def g(e, rows):
        if e < 0:
            return below[11 + e, rows, :]
        if e >= CX:
            return above[1 + e, rows, :]
        return g_ref[(0, 1, 5, 6, 7).index(e), rows, :]

    keep = {name: (kept, k) for k, name in enumerate(KEPT)}
    open_at = {name: (opened, k) for k, name in enumerate(OPEN)}
    new = [0]

    def fresh(nodes):
        out = {n: (modes, new[0] + k) for k, n in enumerate(nodes)}
        new[0] += len(nodes)
        return out

    b_modes = fresh([-2, -1, 8, 9, 10])
    for n in (-2, -1):
        to_modes(lambda c, n=n: below[3 * c + n + 2], b_modes[n])
    for n in (8, 9, 10):
        to_modes(lambda c, n=n: above[3 * c + n - 8], b_modes[n])
    b_modes.update({0: keep["b", 0], 7: keep["b", 7]})
    nodes = (-1, 0, 7, 8, 9)
    put = {n: (gathered, k) for k, n in enumerate(nodes)}
    sweep((-2, -1), b_modes, g, {0: open_at["p1", 0]}, put)
    sweep((7, 8, 9), b_modes, g, {7: open_at["p1", 7]}, put)
    for k, n in enumerate(nodes):
        finish(put[n], (q1, k), edge, past_x if n >= CX else None)

    p1_modes = fresh(nodes)
    for k, n in enumerate(nodes):
        to_modes(lambda c, k=k: q1[c, k], p1_modes[n])
    p1_modes.update({1: keep["p1", 1], 6: keep["p1", 6]})
    nodes = (0, 1, 6, 7, 8)
    put = {n: (gathered, k) for k, n in enumerate(nodes)}
    sweep((-1, 0), p1_modes, g, {1: open_at["p2", 1]}, put)
    sweep((6, 7, 8), p1_modes, g, {6: open_at["p2", 6]}, put)
    for k, n in enumerate(nodes):
        finish(put[n], (q2, k), edge, past_x if n >= CX else None)

    p2_modes = fresh(nodes)
    for k, n in enumerate(nodes):
        to_modes(lambda c, k=k: q2[c, k], p2_modes[n])
    p2_modes.update({2: keep["p2", 2], 5: keep["p2", 5]})
    sums[...] = sums_in[...]

    def energy(rows):
        total = jnp.zeros((8, CZ), F32)
        for elements in ((0, 1), (5, 6, 7)):
            total = add_energy(total, elements, p2_modes, g, rows)
        sums[5] += total

    each_chunk(energy, False)
    total = [sums[k] for k in range(5)]
    for n in (0, 1, 6, 7):
        for c in range(3):
            v1 = q1[c, (-1, 0, 7).index(n), :CY] if n in (0, 7) else p1[c, n - 1, :CY]
            v = (b_ref[c, n], v1, q2[c, (0, 1, 6, 7).index(n), :CY])
            for k, (i, j) in enumerate(((0, 0), (0, 1), (1, 1), (1, 2), (2, 2))):
                if k >= (1 if n in (0, 7) else 3):
                    total[k] = total[k] + collapse(v[i] * v[j])
    total.append(sums[5])
    lane = iota((1, CZ), 1)
    line = jnp.zeros((1, CZ), F32)
    for k in range(6):
        value = jnp.sum(jnp.sum(total[k], 0, keepdims=True), 1, keepdims=True)
        line = jnp.where(lane == k, value, line)
    row_out[...] = jnp.broadcast_to(line, row_out.shape)


def products(
    b_ref, u_ref, halo, b_next, u_next, p1, p2, q1, q2, t, b_modes, p1_modes, p2_modes, u_modes,
):
    for n in range(CX + 1):
        if n < CX:
            to_modes(lambda c: jnp.concatenate([b_ref[c, n], halo[c, n]], 0), (b_modes, n))
            to_modes(lambda c: jnp.concatenate([u_ref[c, n], halo[4 + c, n]], 0), (u_modes, n))
        else:
            to_modes(lambda c: b_next[c], (b_modes, n))
            to_modes(lambda c: u_next[c], (u_modes, n))
        to_modes(lambda c: q1[c, Q1.index(n)] if n in Q1 else p1[c, n - 1], (p1_modes, n))
        to_modes(lambda c: q2[c, Q2.index(n)] if n in Q2 else p2[c, n - 2], (p2_modes, n))
    fields = (b_modes, p1_modes, p2_modes)

    def step(rows):
        for e in range(CX):
            stiff = stresses(strains(load((u_modes, e), rows), load((u_modes, e + 1), rows)), None)
            for k, m in enumerate(fields):
                strain = strains(load((m, e), rows), load((m, e + 1), rows))
                t[k, e, rows, :] = inner(strain, stiff)

    each_chunk(step, False)


Q1, Q2 = (-1, 0, 7, 8, 9), (0, 1, 6, 7, 8)


def combine(parts, b_ref, h_ref, p1, p2, q1, q2, t, adjoint, sensitivity):
    line = jnp.sum(parts[...], 0, keepdims=True)
    lane = iota((1, CZ), 1)
    m = [jnp.sum(jnp.where(lane == k, line, 0.0), 1, keepdims=True) for k in range(6)]
    l10, l20 = m[2] / m[1], m[3] / m[1]
    d1, h21 = m[3] - l10 * m[2], m[4] - l20 * m[2]
    l21 = h21 / d1
    d2 = m[5] - l20 * m[3] - l21 * h21
    y1 = m[1] - l10 * m[0]
    y2 = m[2] - l20 * m[0] - l21 * y1
    c2 = y2 / d2
    c1 = y1 / d1 - l21 * c2
    c0 = m[0] / m[1] - l10 * c1 - l20 * c2
    weight = [jnp.broadcast_to(c, (CY, CZ)) for c in (c0, c1, c2)]
    for x in range(CX):
        for c in range(3):
            v1 = q1[c, Q1.index(x), :CY] if x in Q1 else p1[c, x - 1, :CY]
            v2 = q2[c, Q2.index(x), :CY] if x in Q2 else p2[c, x - 2, :CY]
            adjoint[c, x] = weight[0] * b_ref[c, x] + weight[1] * v1 + weight[2] * v2
        product = weight[0] * t[0, x] + weight[1] * t[1, x] + weight[2] * t[2, x]
        sensitivity[x] = 2.0 * (1.0 - h_ref[x]) * product


VMEM = pl.BlockSpec(memory_space=pltpu.VMEM)


def shape(*dims):
    return jax.ShapeDtypeStruct(dims, F32)


def call(kernel, megabytes, inputs, outputs, scratch=(), in_specs=None):
    return pl.pallas_call(
        kernel,
        in_specs=in_specs or [VMEM] * len(inputs),
        out_specs=[VMEM] * len(outputs),
        out_shape=[shape(*dims) for dims in outputs],
        scratch_shapes=[s if not isinstance(s, tuple) else pltpu.VMEM(s, F32) for s in scratch],
        compiler_params=pltpu.CompilerParams(vmem_limit_bytes=megabytes and int(megabytes * 2**20)),
    )(*inputs)


def body(misfit, damage, displacement):
    tile = (CX, 8, CZ)
    y_a, y_b, misfit, damage, displacement = call(
        pack_y, 4,
        [pltpu.with_memory_space_constraint(x, pltpu.HBM) for x in (misfit, damage, displacement)],
        [
            (2,) + tile, (2,) + tile, (3, CX, CY, CZ), (CX, CY, CZ), (3, CX, CY, CZ),
        ],
        [pltpu.SemaphoreType.DMA((3,))],
        [pl.BlockSpec(memory_space=pltpu.HBM)] * 3,
    )
    y_b = exchange(y_b, "gy", 1)
    y_a = exchange(y_a, "gy", 0)
    x_a, x_b, halo = call(
        pack_x, 6,
        (y_a, y_b, misfit, damage, displacement),
        [(11 * ROWS + 3 * CY, CZ)] * 2 + [(7,) + tile],
    )
    x_b = exchange(x_b, "gx", 1)
    x_a = exchange(x_a, "gx", 0)
    devices = lax.axis_size("gx") * lax.axis_size("gy")
    layer = (ROWS, CZ)
    p1, p2, kept, opened, sums = call(
        inner_kernel, 20,
        (misfit, damage, halo),
        [
            (3, 6) + layer, (3, 4) + layer, (12, len(KEPT)) + layer, (12, len(OPEN)) + layer,
            (6, 8, CZ),
        ],
        [(12, CX) + layer, (12, CX) + layer, (CX,) + layer],
    )
    q1, q2, line, b_next, u_next = call(
        outer_kernel, 20,
        (misfit, damage, halo, x_a, x_b, p1, p2, kept, opened, sums),
        [(3, 5) + layer, (3, 5) + layer, (devices, CZ), (3,) + layer, (3,) + layer],
        [
            (11,) + layer, (11,) + layer, (5,) + layer, (12, 15) + layer, (12, 5) + layer,
            (6, 8, CZ),
        ],
    )
    parts = lax.all_to_all(line, AXES, 0, 0, tiled=True)
    (t,) = call(
        products, 20,
        (misfit, displacement, halo, b_next, u_next, p1, p2, q1, q2),
        [(3, CX, CY, CZ)],
        [(12, CX + 1) + layer] * 4,
    )
    return call(
        combine, 8,
        (parts, misfit, damage, p1, p2, q1, q2, t),
        [(3, CX, CY, CZ), (CX, CY, CZ)],
    )


def solution(mesh):
    field, scalar = P(None, "gx", "gy", None), P("gx", "gy", None)
    return jax.shard_map(
        body, mesh=mesh, in_specs=(field, scalar, field), out_specs=(field, scalar), check_vma=False
    )
```

```python
import jax
import jax.numpy as jnp
from jax import lax
from jax.experimental import pallas as pl
from jax.experimental.pallas import tpu as pltpu
from jax.sharding import PartitionSpec as P


CX, CY, CZ = 8, 32, 128
ROWS = 40
AXES = ("gx", "gy")
LAM = 3.0 * 0.3 / (1.3 * 0.4)
MU = 3.0 / 2.6
F32 = jnp.float32


def exchange(x, axis, first):
    n = lax.axis_size(axis)
    pairs = []
    for i in range(first, n - 1, 2):
        pairs += [(i, i + 1), (i + 1, i)]
    return lax.ppermute(x, axis, pairs)


def iota(shape, dim):
    return lax.broadcasted_iota(jnp.int32, shape, dim)


def degradation_of(damage):
    return (1.0 - damage) * (1.0 - damage) + 0.001


def pack_y(b, h, u, out_a, out_b, x_a, x_b, b_all, h_all, u_all, done):
    copies = []
    for k, (source, target) in enumerate(((h, h_all), (b, b_all), (u, u_all))):
        copies.append(pltpu.make_async_copy(source, target, done.at[k]))
        copies[-1].start()
    for copy in copies:
        copy.wait()
    b_lo, b_hi = b_all[:, :, :8], b_all[:, :, CY - 8 :]
    h_lo, h_hi = h_all[:, :8], h_all[:, CY - 8 :]
    u_lo = u_all[:, :, :8]
    row = iota((CX, 8, CZ), 1)
    g_lo, g_hi = degradation_of(h_lo), degradation_of(h_hi)
    up = lambda x, k: pltpu.roll(x, k % 8, 1)
    low_1 = jnp.where(row < 3, b_lo[0], jnp.where(row < 6, up(b_lo[1], 3), up(g_lo, 6)))
    low_2 = jnp.where(
        row < 3,
        b_lo[2],
        jnp.where(
            row == 3, up(u_lo[0], 3), jnp.where(row == 4, up(u_lo[1], 4), up(u_lo[2], 5))
        ),
    )
    high = jnp.where(
        row < 2,
        up(b_hi[0], 2),
        jnp.where(row < 4, up(b_hi[1], 4), jnp.where(row < 6, up(b_hi[2], 6), g_hi)),
    )
    odd = lax.rem(lax.axis_index("gy"), 2) == 1

    @pl.when(odd)
    def _():
        out_a[0], out_a[1] = low_1, low_2
        out_b[0], out_b[1] = high, high

    @pl.when(jnp.logical_not(odd))
    def _():
        out_a[0], out_a[1] = high, high
        out_b[0], out_b[1] = low_1, low_2

    def low_x(out):
        for c in range(3):
            for x in range(3):
                out[3 * c + x] = b_all[c, x]
            out[11 + c] = u_all[c, 0]
        for x in range(2):
            out[9 + x] = degradation_of(h_all[x])

    def high_x(out):
        for c in range(3):
            for x in range(2):
                out[3 * c + x] = b_all[c, 6 + x]
            out[3 * c + 2] = jnp.zeros((CY, CZ), F32)
            out[11 + c] = jnp.zeros((CY, CZ), F32)
        for x in range(2):
            out[9 + x] = degradation_of(h_all[6 + x])

    odd_x = lax.rem(lax.axis_index("gx"), 2) == 1

    @pl.when(odd_x)
    def _():
        low_x(x_a)
        high_x(x_b)

    @pl.when(jnp.logical_not(odd_x))
    def _():
        high_x(x_a)
        low_x(x_b)


def pack_strips(y_a, y_b, out_a, out_b, halo):
    odd_y = lax.rem(lax.axis_index("gy"), 2) == 1
    row = iota((CX, 8, CZ), 1)
    up = lambda x, k: pltpu.roll(x, k % 8, 1)
    above_1 = jnp.where(odd_y, y_b[0], y_a[0])
    above_2 = jnp.where(odd_y, y_b[1], y_a[1])
    below = jnp.where(odd_y, y_a[0], y_b[0])

    def tile(head, count, tail):
        return jnp.where(row < count, head, jnp.where(row >= 6, tail, 0.0))

    halo[0] = tile(above_1, 3, up(below, 6))
    halo[1] = tile(up(above_1, -3), 3, up(below, 4))
    halo[2] = tile(above_2, 3, up(below, 2))
    halo[3] = tile(up(above_1, -6), 2, below)
    for c in range(3):
        halo[4 + c] = jnp.where(row < 1, up(above_2, -3 - c), 0.0)
    odd_x = lax.rem(lax.axis_index("gx"), 2) == 1

    def low(out):
        for c in range(3):
            for x in range(3):
                edge = halo[c, x]
                if x == 0:
                    edge = jnp.where(row[0] == 3, pltpu.roll(halo[4 + c, 0], 3, 0), edge)
                out[3 * c + x] = edge
        for x in range(2):
            out[9 + x] = halo[3, x]

    def high(out):
        for c in range(3):
            for x in range(2):
                out[3 * c + x] = halo[c, 6 + x]
            out[3 * c + 2] = jnp.zeros((8, CZ), F32)
        for x in range(2):
            out[9 + x] = halo[3, 6 + x]

    @pl.when(odd_x)
    def _():
        low(out_a)
        high(out_b)

    @pl.when(jnp.logical_not(odd_x))
    def _():
        high(out_a)
        low(out_b)


def yz_modes(u):
    lane = iota((ROWS, CZ), 1)
    u_next = jnp.where(lane == CZ - 1, 0.0, pltpu.roll(u, CZ - 1, 1))
    out = [None] * 4
    for z, a in enumerate((u + u_next, u_next - u)):
        a_next = pltpu.roll(a, ROWS - 1, 0)
        out[z], out[2 + z] = a + a_next, a_next - a
    return out


def yz_gather(r):
    lane = iota((ROWS, CZ), 1)
    rows = []
    for z in range(2):
        s, d = r[z], r[2 + z]
        rows.append((s - d) + pltpu.roll(s + d, 1, 0))
    s, d = rows
    return (s - d) + jnp.where(lane == 0, 0.0, pltpu.roll(s + d, 1, 1))


SS, SD, DS, DD = 0, 1, 2, 3


def strains(here, there):
    s = [[here[4 * c + k] + there[4 * c + k] if k else None for k in range(4)] for c in range(3)]
    d = [[there[4 * c + k] - here[4 * c + k] for k in range(4)] for c in range(3)]
    u, v, w = range(3)
    return [
        d[u][SS], s[v][DS], s[w][SD],
        s[u][DS] + d[v][SS], s[u][SD] + d[w][SS], s[v][SD] + s[w][DS],
        s[u][DD], d[v][SD], d[w][DS],
        d[u][SD], s[v][DD], d[u][DS], s[w][DD], d[v][DS], d[w][SD],
        d[u][DD], d[v][DD], d[w][DD],
    ]


def stresses(e, g):
    scaled = (lambda k: g * k) if g is not None else (lambda k: k)
    l16, m8, m16, m48 = scaled(LAM / 16), scaled(MU / 8), scaled(MU / 16), scaled(MU / 48)
    l48, q = scaled(LAM / 48), scaled((LAM + 4 * MU) / 144)
    trace = l16 * (e[0] + e[1] + e[2])
    out = [trace + m8 * e[k] for k in range(3)]
    out += [m16 * e[k] for k in range(3, 6)]
    three = e[6] + e[7] + e[8]
    out += [m48 * (e[k] + three) for k in range(6, 9)]
    for k in (9, 11, 13):
        both = l48 * (e[k] + e[k + 1])
        out += [both + m16 * e[k], both + m16 * e[k + 1]]
    return out + [q * e[k] for k in range(15, 18)]


def x_forces(f):
    s = [[None, f[4], f[3], f[6]], [None, f[5], f[1], f[10]], [None, f[2], f[5], f[12]]]
    d = [[f[0], f[9], f[11], f[15]], [f[3], f[7], f[13], f[16]], [f[4], f[14], f[8], f[17]]]
    return [x for c in s for x in c], [x for c in d for x in c]


def inner(a, b):
    total = a[0] * b[0]
    for x, y in zip(a[1:], b[1:]):
        total = total + x * y
    return total


def load(place, rows):
    ref, slot = place
    return [ref[k, slot, rows, :] for k in range(12)]


def to_modes(node, place):
    ref, slot = place
    for c in range(3):
        for k, a in enumerate(yz_modes(node(c))):
            ref[4 * c + k, slot] = a


def each_chunk(step, halo_too):
    @pl.loop(0, CY // 8)
    def _(j):
        step(pl.ds(pl.multiple_of(8 * j, 8), 8))

    if halo_too:
        step(pl.ds(CY, 8))


def sweep(elements, modes, g, add, put):
    def step(rows):
        here = load(modes[elements[0]], rows)
        before = None

        def store(n, lower):
            if n not in put:
                return
            total = before
            if lower is not None:
                total = lower if total is None else [p + q for p, q in zip(total, lower)]
            if n in add:
                total = [p + q for p, q in zip(total, load(add[n], rows))]
            ref, slot = put[n]
            for k in range(12):
                ref[k, slot, rows, :] = total[k]

        for e in elements:
            there = load(modes[e + 1], rows)
            s, d = x_forces(stresses(strains(here, there), g(e, rows)))
            if e in put:
                store(e, [p - q if p is not None else -q for p, q in zip(s, d)])
            before = [p + q if p is not None else q for p, q in zip(s, d)]
            here = there
        store(elements[-1] + 1, None)

    each_chunk(step, True)


def finish(gathered, target, edge, factor=None):
    ref, slot = gathered
    out, at = target
    for c in range(3):
        v = yz_gather([ref[4 * c + k, slot] for k in range(4)])
        if factor is not None:
            v = v * factor
        out[c, at, :CY] = v[:CY]
        out[c, at, CY:] = v[CY:] * edge


def collapse(x):
    return x[0:8] + x[8:16] + x[16:24] + x[24:32]


def row_edge():
    row = iota((8, CZ), 0)
    last = lax.axis_index("gy") == lax.axis_size("gy") - 1
    return jnp.where(row < 3, jnp.where(last, 0.0, 1.0).astype(F32), 1.0)


KEPT = ("b", 0), ("b", 7), ("p1", 1), ("p1", 6), ("p2", 2), ("p2", 5)
OPEN = ("p1", 0), ("p1", 7), ("p2", 1), ("p2", 6)


def add_energy(total, elements, modes, g, rows):
    here = load(modes[elements[0]], rows)
    for e in elements:
        there = load(modes[e + 1], rows)
        strain = strains(here, there)
        total = total + g(e, rows) * inner(strain, stresses(strain, None))
        here = there
    return total


def inner_kernel(b_ref, h_ref, halo, p1, p2, kept, opened, sums, modes, gathered, g_ref):
    edge = row_edge()
    g_ref[:, :CY] = degradation_of(h_ref[...])
    g_ref[:, CY:] = halo[3]
    g = lambda e, rows: g_ref[e, rows, :]
    keep = {name: (kept, k) for k, name in enumerate(KEPT)}
    open_at = {name: (opened, k) for k, name in enumerate(OPEN)}
    at = lambda name, n: keep.get((name, n), (modes, n))

    b_modes = {n: at("b", n) for n in range(CX)}
    for n in range(CX):
        to_modes(lambda c, n=n: jnp.concatenate([b_ref[c, n], halo[c, n]], 0), b_modes[n])
    put = {n: (gathered, n) for n in range(1, 7)}
    put.update({0: open_at["p1", 0], 7: open_at["p1", 7]})
    sweep(range(0, 7), b_modes, g, {}, put)
    for n in range(1, 7):
        finish(put[n], (p1, n - 1), edge)

    p1_modes = {n: at("p1", n) for n in range(1, 7)}
    for n in range(1, 7):
        to_modes(lambda c, n=n: p1[c, n - 1], p1_modes[n])
    put = {n: (gathered, n) for n in range(2, 6)}
    put.update({1: open_at["p2", 1], 6: open_at["p2", 6]})
    sweep(range(1, 6), p1_modes, g, {}, put)
    for n in range(2, 6):
        finish(put[n], (p2, n - 2), edge)

    p2_modes = {n: at("p2", n) for n in range(2, 6)}
    for n in range(2, 6):
        to_modes(lambda c, n=n: p2[c, n - 2], p2_modes[n])
    sums[...] = jnp.zeros_like(sums)

    def energy(rows):
        sums[5] += add_energy(jnp.zeros((8, CZ), F32), range(2, 5), p2_modes, g, rows)

    each_chunk(energy, False)
    total = [jnp.zeros((8, CZ), F32)] * 5
    for n in range(CX):
        for c in range(3):
            v = [b_ref[c, n]]
            if 1 <= n < 7:
                v.append(p1[c, n - 1, :CY])
            if 2 <= n < 6:
                v.append(p2[c, n - 2, :CY])
            for k, (i, j) in enumerate(((0, 0), (0, 1), (1, 1), (1, 2), (2, 2))):
                if j < len(v):
                    total[k] = total[k] + collapse(v[i] * v[j])
    for k in range(5):
        sums[k] = total[k]


def outer_kernel(
    b_ref, h_ref, halo, x_a, x_b, s_a, s_b, p1, p2, kept, opened, sums_in,
    q1, q2, row_out, b_next, u_next, above, below, g_ref, modes, gathered, sums,
):
    edge = row_edge()
    odd_x = lax.rem(lax.axis_index("gx"), 2) == 1
    last_x = lax.axis_index("gx") == lax.axis_size("gx") - 1
    past_x = jnp.where(last_x, 0.0, 1.0).astype(F32)

    def split(x_above, s_above, x_below, s_below):
        for k in range(11):
            above[k, :CY], above[k, CY:] = x_above[k], s_above[k]
            below[k, :CY], below[k, CY:] = x_below[k], s_below[k]
        for c in range(3):
            u_next[c, :CY], u_next[c, CY:] = x_above[11 + c], pltpu.roll(s_above[3 * c], 5, 0)
            b_next[c, :CY], b_next[c, CY:] = x_above[3 * c], s_above[3 * c]

    @pl.when(odd_x)
    def _():
        split(x_b, s_b, x_a, s_a)

    @pl.when(jnp.logical_not(odd_x))
    def _():
        split(x_a, s_a, x_b, s_b)

    for k, e in enumerate((0, 1, 5, 6, 7)):
        g_ref[k, :CY] = degradation_of(h_ref[e])
        g_ref[k, CY:] = halo[3, e]

    def g(e, rows):
        if e < 0:
            return below[11 + e, rows, :]
        if e >= CX:
            return above[1 + e, rows, :]
        return g_ref[(0, 1, 5, 6, 7).index(e), rows, :]

    keep = {name: (kept, k) for k, name in enumerate(KEPT)}
    open_at = {name: (opened, k) for k, name in enumerate(OPEN)}
    new = [0]

    def fresh(nodes):
        out = {n: (modes, new[0] + k) for k, n in enumerate(nodes)}
        new[0] += len(nodes)
        return out

    b_modes = fresh([-2, -1, 8, 9, 10])
    for n in (-2, -1):
        to_modes(lambda c, n=n: below[3 * c + n + 2], b_modes[n])
    for n in (8, 9, 10):
        to_modes(lambda c, n=n: above[3 * c + n - 8], b_modes[n])
    b_modes.update({0: keep["b", 0], 7: keep["b", 7]})
    nodes = (-1, 0, 7, 8, 9)
    put = {n: (gathered, k) for k, n in enumerate(nodes)}
    sweep((-2, -1), b_modes, g, {0: open_at["p1", 0]}, put)
    sweep((7, 8, 9), b_modes, g, {7: open_at["p1", 7]}, put)
    for k, n in enumerate(nodes):
        finish(put[n], (q1, k), edge, past_x if n >= CX else None)

    p1_modes = fresh(nodes)
    for k, n in enumerate(nodes):
        to_modes(lambda c, k=k: q1[c, k], p1_modes[n])
    p1_modes.update({1: keep["p1", 1], 6: keep["p1", 6]})
    nodes = (0, 1, 6, 7, 8)
    put = {n: (gathered, k) for k, n in enumerate(nodes)}
    sweep((-1, 0), p1_modes, g, {1: open_at["p2", 1]}, put)
    sweep((6, 7, 8), p1_modes, g, {6: open_at["p2", 6]}, put)
    for k, n in enumerate(nodes):
        finish(put[n], (q2, k), edge, past_x if n >= CX else None)

    p2_modes = fresh(nodes)
    for k, n in enumerate(nodes):
        to_modes(lambda c, k=k: q2[c, k], p2_modes[n])
    p2_modes.update({2: keep["p2", 2], 5: keep["p2", 5]})
    sums[...] = sums_in[...]

    def energy(rows):
        total = jnp.zeros((8, CZ), F32)
        for elements in ((0, 1), (5, 6, 7)):
            total = add_energy(total, elements, p2_modes, g, rows)
        sums[5] += total

    each_chunk(energy, False)
    total = [sums[k] for k in range(5)]
    for n in (0, 1, 6, 7):
        for c in range(3):
            v1 = q1[c, (-1, 0, 7).index(n), :CY] if n in (0, 7) else p1[c, n - 1, :CY]
            v = (b_ref[c, n], v1, q2[c, (0, 1, 6, 7).index(n), :CY])
            for k, (i, j) in enumerate(((0, 0), (0, 1), (1, 1), (1, 2), (2, 2))):
                if k >= (1 if n in (0, 7) else 3):
                    total[k] = total[k] + collapse(v[i] * v[j])
    total.append(sums[5])
    lane = iota((1, CZ), 1)
    line = jnp.zeros((1, CZ), F32)
    for k in range(6):
        value = jnp.sum(jnp.sum(total[k], 0, keepdims=True), 1, keepdims=True)
        line = jnp.where(lane == k, value, line)
    row_out[...] = jnp.broadcast_to(line, row_out.shape)


def products(
    b_ref, u_ref, halo, b_next, u_next, p1, p2, q1, q2, t, b_modes, p1_modes, p2_modes, u_modes,
):
    for n in range(CX + 1):
        if n < CX:
            to_modes(lambda c: jnp.concatenate([b_ref[c, n], halo[c, n]], 0), (b_modes, n))
            to_modes(lambda c: jnp.concatenate([u_ref[c, n], halo[4 + c, n]], 0), (u_modes, n))
        else:
            to_modes(lambda c: b_next[c], (b_modes, n))
            to_modes(lambda c: u_next[c], (u_modes, n))
        to_modes(lambda c: q1[c, Q1.index(n)] if n in Q1 else p1[c, n - 1], (p1_modes, n))
        to_modes(lambda c: q2[c, Q2.index(n)] if n in Q2 else p2[c, n - 2], (p2_modes, n))
    fields = (b_modes, p1_modes, p2_modes)

    def step(rows):
        for e in range(CX):
            stiff = stresses(strains(load((u_modes, e), rows), load((u_modes, e + 1), rows)), None)
            for k, m in enumerate(fields):
                strain = strains(load((m, e), rows), load((m, e + 1), rows))
                t[k, e, rows, :] = inner(strain, stiff)

    each_chunk(step, False)


Q1, Q2 = (-1, 0, 7, 8, 9), (0, 1, 6, 7, 8)


def combine(parts, b_ref, h_ref, p1, p2, q1, q2, t, adjoint, sensitivity):
    line = jnp.sum(parts[...], 0, keepdims=True)
    lane = iota((1, CZ), 1)
    m = [jnp.sum(jnp.where(lane == k, line, 0.0), 1, keepdims=True) for k in range(6)]
    l10, l20 = m[2] / m[1], m[3] / m[1]
    d1, h21 = m[3] - l10 * m[2], m[4] - l20 * m[2]
    l21 = h21 / d1
    d2 = m[5] - l20 * m[3] - l21 * h21
    y1 = m[1] - l10 * m[0]
    y2 = m[2] - l20 * m[0] - l21 * y1
    c2 = y2 / d2
    c1 = y1 / d1 - l21 * c2
    c0 = m[0] / m[1] - l10 * c1 - l20 * c2
    weight = [jnp.broadcast_to(c, (CY, CZ)) for c in (c0, c1, c2)]
    for x in range(CX):
        for c in range(3):
            v1 = q1[c, Q1.index(x), :CY] if x in Q1 else p1[c, x - 1, :CY]
            v2 = q2[c, Q2.index(x), :CY] if x in Q2 else p2[c, x - 2, :CY]
            adjoint[c, x] = weight[0] * b_ref[c, x] + weight[1] * v1 + weight[2] * v2
        product = weight[0] * t[0, x] + weight[1] * t[1, x] + weight[2] * t[2, x]
        sensitivity[x] = 2.0 * (1.0 - h_ref[x]) * product


VMEM = pl.BlockSpec(memory_space=pltpu.VMEM)


def shape(*dims):
    return jax.ShapeDtypeStruct(dims, F32)


def call(kernel, megabytes, inputs, outputs, scratch=(), in_specs=None):
    return pl.pallas_call(
        kernel,
        in_specs=in_specs or [VMEM] * len(inputs),
        out_specs=[VMEM] * len(outputs),
        out_shape=[shape(*dims) for dims in outputs],
        scratch_shapes=[s if not isinstance(s, tuple) else pltpu.VMEM(s, F32) for s in scratch],
        compiler_params=pltpu.CompilerParams(vmem_limit_bytes=megabytes and int(megabytes * 2**20)),
    )(*inputs)


def body(misfit, damage, displacement):
    tile = (CX, 8, CZ)
    y_a, y_b, x_a, x_b, misfit, damage, displacement = call(
        pack_y, 6,
        [pltpu.with_memory_space_constraint(x, pltpu.HBM) for x in (misfit, damage, displacement)],
        [(2,) + tile] * 2
        + [(14, CY, CZ)] * 2
        + [(3, CX, CY, CZ), (CX, CY, CZ), (3, CX, CY, CZ)],
        [pltpu.SemaphoreType.DMA((3,))],
        [pl.BlockSpec(memory_space=pltpu.HBM)] * 3,
    )
    y_b = exchange(y_b, "gy", 1)
    y_a = exchange(y_a, "gy", 0)
    x_b = exchange(x_b, "gx", 1)
    x_a = exchange(x_a, "gx", 0)
    s_a, s_b, halo = call(
        pack_strips, 4,
        (y_a, y_b),
        [(11, 8, CZ)] * 2 + [(7,) + tile],
    )
    s_b = exchange(s_b, "gx", 1)
    s_a = exchange(s_a, "gx", 0)
    devices = lax.axis_size("gx") * lax.axis_size("gy")
    layer = (ROWS, CZ)
    p1, p2, kept, opened, sums = call(
        inner_kernel, 20,
        (misfit, damage, halo),
        [
            (3, 6) + layer, (3, 4) + layer, (12, len(KEPT)) + layer, (12, len(OPEN)) + layer,
            (6, 8, CZ),
        ],
        [(12, CX) + layer, (12, CX) + layer, (CX,) + layer],
    )
    q1, q2, line, b_next, u_next = call(
        outer_kernel, 20,
        (misfit, damage, halo, x_a, x_b, s_a, s_b, p1, p2, kept, opened, sums),
        [(3, 5) + layer, (3, 5) + layer, (devices, CZ), (3,) + layer, (3,) + layer],
        [
            (11,) + layer, (11,) + layer, (5,) + layer, (12, 15) + layer, (12, 5) + layer,
            (6, 8, CZ),
        ],
    )
    parts = lax.all_to_all(line, AXES, 0, 0, tiled=True)
    (t,) = call(
        products, 20,
        (misfit, displacement, halo, b_next, u_next, p1, p2, q1, q2),
        [(3, CX, CY, CZ)],
        [(12, CX + 1) + layer] * 4,
    )
    return call(
        combine, 8,
        (parts, misfit, damage, p1, p2, q1, q2, t),
        [(3, CX, CY, CZ), (CX, CY, CZ)],
    )


def solution(mesh):
    field, scalar = P(None, "gx", "gy", None), P("gx", "gy", None)
    return jax.shard_map(
        body, mesh=mesh, in_specs=(field, scalar, field), out_specs=(field, scalar), check_vma=False
    )
```
